128 devices in a mesh: row: 16 (over z, y), col: 8 (over x, core).
Axes of the slice: x: 4, y: 4, z: 4, core: 2. Of those that a mesh axis runs over, the one named last changes fastest.
Arguments:
- trailing: bfloat16 [24576, 24576], P('row', 'col'), may hold values from -6 to 6
- rows_a: int32 [16, 12], replicated, may hold values from 0 to 11, as said below
- counts_a: int32 [16], replicated, may hold values from 1 to 12, as said below
- factor_a: bfloat16 [24576, 512], P('row'), may hold values from -0.0390625 to 0.0390625
- rows_b: int32 [16, 12], replicated, may hold values from 0 to 11, as said below
- counts_b: int32 [16], replicated, may hold values from 1 to 12, as said below
- factor_b: bfloat16 [24576, 512], P('row'), may hold values from -0.0390625 to 0.0390625
- factor_top: bfloat16 [512, 512], replicated, may hold values from -0.25 to 0.25
- base_a: float32 [512, 512], P('col'), may hold values from -3 to 3
- base_b: float32 [512, 512], P('col'), may hold values from -3 to 3
Outputs:
- column_a: bfloat16 [24576, 512], P('row')
- diag_a: float32 [512, 512], P('col')
- column_b: bfloat16 [24576, 512], P('row')
- top_b: bfloat16 [512, 512], P('col')
- diag_b: float32 [512, 512], P('col')
The draws below stay inside these ranges and needn't reach their ends.
Inputs may be any that keep to these rules, and one draw needn't show every extreme that they name: `rows_a`: the first counts_a[r] entries of row r are distinct; the rest of the row is padding. `counts_a`: some owner uses all 12 slots in every draw. `rows_b`: the first counts_b[r] entries of row r are distinct and lie among the first counts_a[r] entries of row r of rows_a; the rest is padding. counts_b[r] <= counts_a[r]; some owner uses all 12 slots in every draw.
All inputs are finite; a program needn't handle non-finite values.
Results may differ from the reference program's by a relative error of at most 0.007.
Values may be sent and summed in bfloat16 or wider, within the bound.
No kernel may reach another device: no remote copies, remote signals or barrier semaphores. Data moves between devices by JAX's collectives and lax.ppermute only.
A program may use at most 128 MiB of HBM per device.

```python
import jax
import jax.numpy as jnp
from jax import lax

BS = 128
W = 512
RBD = 12
PAD = 12
OWNERS = 16
COL_OWNERS = 8
CBD = 24
TRAIL = 24576
SROWS = 24576


def structure(key):
    seeded = jax.random.fold_in(key, 11)
    perm_keys = jax.random.split(jax.random.fold_in(seeded, 1), OWNERS)
    orders = jax.vmap(lambda single: jax.random.permutation(single, RBD))(perm_keys).astype(jnp.int32)
    rows_first = orders[:, :PAD]
    counts = jax.random.randint(jax.random.fold_in(seeded, 2), (OWNERS,), PAD // 2, PAD + 1, dtype=jnp.int32)
    busiest = jax.random.randint(jax.random.fold_in(seeded, 3), (), 0, OWNERS, dtype=jnp.int32)
    lighter = (busiest + 1) % OWNERS
    owners = jnp.arange(OWNERS, dtype=jnp.int32)
    counts_first = jnp.where((owners == busiest) | (owners == lighter), PAD, counts).astype(jnp.int32)
    second = jax.random.randint(jax.random.fold_in(seeded, 4), (OWNERS,), (counts_first + 1) // 2, counts_first + 1, dtype=jnp.int32)
    counts_second = jnp.where(owners == busiest, PAD, second)
    counts_second = jnp.where(owners == lighter, PAD - 1, counts_second).astype(jnp.int32)
    shuffle_keys = jax.random.split(jax.random.fold_in(seeded, 5), OWNERS)
    shuffles = jax.vmap(lambda single: jax.random.permutation(single, PAD))(shuffle_keys).astype(jnp.int32)
    slot_ids = jnp.arange(PAD, dtype=jnp.int32)
    scores = jnp.where(slot_ids[None, :] < counts_first[:, None], shuffles, shuffles + PAD)
    sort_order = jnp.argsort(scores, axis=1, stable=True)
    rows_second = jnp.take_along_axis(rows_first, sort_order, axis=1).astype(jnp.int32)
    return (rows_first, counts_first, rows_second, counts_second)


def draw_rows_a(key, part):
    return structure(key)[0]


def draw_counts_a(key, part):
    return structure(key)[1]


def draw_rows_b(key, part):
    return structure(key)[2]


def draw_counts_b(key, part):
    return structure(key)[3]


def steps_of(rng, dims, pieces, low, largest):
    level = 1.0
    for axis_at, parts in pieces:
        steps = jax.random.uniform(jax.random.fold_in(jax.random.fold_in(rng, 6), axis_at), (parts,), jnp.float32, low / len(pieces), largest / len(pieces))
        level = level * jnp.repeat(jnp.exp(steps), dims[axis_at] // parts).reshape((-1,) + (1,) * (len(dims) - 1 - axis_at))
    return level


def scatter_about(key, shape, deviation, most, cuts=(), kind=jnp.bfloat16):
    loudness = steps_of(key, shape, cuts, -0.22, 0.18) if cuts else 1.0
    drawn = jax.random.normal(key, shape, jnp.float32) * deviation * loudness
    return jnp.minimum(jnp.maximum(drawn, -most), most).astype(kind)


def setup_inputs(seed: int = 0) -> dict:
    keys = jax.random.split(jax.random.key(seed), 11)
    trailing = scatter_about(keys[0], (TRAIL, TRAIL), 1.0, 6.0, ((0, 16), (1, 8)))
    rows_a = draw_rows_a(jax.random.fold_in(keys[10], 71), 0)
    counts_a = draw_counts_a(jax.random.fold_in(keys[10], 71), 0)
    factor_a = scatter_about(keys[3], (SROWS, W), SROWS ** -0.5, 0.0390625, ((0, 16),))
    rows_b = draw_rows_b(jax.random.fold_in(keys[10], 71), 0)
    counts_b = draw_counts_b(jax.random.fold_in(keys[10], 71), 0)
    factor_b = scatter_about(keys[6], (SROWS, W), SROWS ** -0.5, 0.0390625, ((0, 16),))
    factor_top = scatter_about(keys[7], (W, W), W ** -0.5, 0.25)
    base_a = scatter_about(keys[8], (W, W), 0.5, 3.0, ((0, 8),), jnp.float32)
    base_b = scatter_about(keys[9], (W, W), 0.5, 3.0, ((0, 8),), jnp.float32)
    return dict(trailing=trailing, rows_a=rows_a, counts_a=counts_a, factor_a=factor_a, rows_b=rows_b, counts_b=counts_b, factor_b=factor_b, factor_top=factor_top, base_a=base_a, base_b=base_b)


def live_mask(counts):
    slot_ids = jnp.arange(PAD, dtype=jnp.int32)
    return (slot_ids[None, :] < counts[:, None]).astype(jnp.float32)


def block_tiles(trailing, rows):
    owners = jnp.arange(OWNERS, dtype=jnp.int32)
    global_ids = rows * OWNERS + owners[:, None]
    row_pos = (owners[:, None] * RBD + rows).reshape(-1).astype(jnp.int32)
    col_pos = ((global_ids % COL_OWNERS) * CBD + global_ids // COL_OWNERS).reshape(-1).astype(jnp.int32)
    blocks = trailing.reshape(TRAIL // BS, BS, TRAIL // BS, BS)
    picked = jnp.take(blocks, row_pos, axis=0)
    picked = jnp.take(picked, col_pos, axis=2)
    slot_count = OWNERS * PAD
    return picked.reshape(slot_count * BS, slot_count * BS)


def reference(trailing, rows_a, counts_a, factor_a, rows_b, counts_b, factor_b, factor_top, base_a, base_b):
    live_a = live_mask(counts_a)
    live_b = live_mask(counts_b)
    gate_a = jnp.repeat(live_a.reshape(-1), BS)[:, None]
    gate_b = jnp.repeat(live_b.reshape(-1), BS)[:, None]
    tiles_a = block_tiles(trailing, rows_a)
    masked_a = factor_a * gate_a.astype(jnp.bfloat16)
    column_a = (-jnp.dot(tiles_a, masked_a, preferred_element_type=jnp.float32) * gate_a).astype(jnp.bfloat16)
    diag_a = base_a - jnp.dot(column_a.T, factor_a, preferred_element_type=jnp.float32)
    pairing = ((rows_b[:, :, None] == rows_a[:, None, :]) & (live_a[:, None, :] > 0.5) & (live_b[:, :, None] > 0.5)).astype(jnp.float32)
    stacked = column_a.reshape(OWNERS, PAD, BS * W).astype(jnp.float32)
    carried = jnp.einsum("rkq,rqx->rkx", pairing, stacked).reshape(SROWS, W).astype(jnp.bfloat16)
    top_b = (-(jnp.dot(carried.T, factor_b, preferred_element_type=jnp.float32) + jnp.dot(diag_a, factor_top.astype(jnp.float32), precision=lax.Precision.HIGHEST))).astype(jnp.bfloat16)
    tiles_b = block_tiles(trailing, rows_b)
    masked_b = factor_b * gate_b.astype(jnp.bfloat16)
    summed_b = jnp.dot(tiles_b, masked_b, preferred_element_type=jnp.float32) + jnp.dot(carried, factor_top, preferred_element_type=jnp.float32)
    column_b = (-summed_b * gate_b).astype(jnp.bfloat16)
    diag_b = base_b - jnp.dot(column_b.T, factor_b, preferred_element_type=jnp.float32) - jnp.dot(top_b.T, factor_top, preferred_element_type=jnp.float32)
    return column_a, diag_a, column_b, top_b, diag_b
```

```python
import functools

import jax
import jax.numpy as jnp
from jax import lax
from jax.experimental import pallas as pl
from jax.experimental.pallas import tpu as pltpu
from jax.sharding import PartitionSpec as P

BS = 128
W = 512
NB = 12
HALF = NB // 2
ROWS = NB * BS
SIDE = 4
PART = 64
BOTH = ("row", "col")
VMEM_LIMIT = 56 * 1024 * 1024
BF = jnp.bfloat16
F32 = jnp.float32


def device(z, y, x, core):
    return ((z % SIDE) * SIDE + y % SIDE) * 8 + (x % SIDE) * 2 + core % 2


def all_places():
    return [
        (z, y, x, core)
        for z in range(SIDE)
        for y in range(SIDE)
        for x in range(SIDE)
        for core in range(2)
    ]


def shifted(dz=0, dy=0, dx=0, dc=0):
    return [
        (device(z, y, x, c), device(z + dz, y + dy, x + dx, c + dc))
        for z, y, x, c in all_places()
    ]


def spread_pairs(along_z):
    pairs = []
    for z, y, x, core in all_places():
        owner = z * SIDE + y
        plane, second = owner % 8, owner // 8
        far = (2 - (x - plane // 2)) % SIDE
        if along_z:
            to_z, to_y = z + core, y + far
        else:
            to_z, to_y = z + far, y + 2 * second + core
        pairs.append((device(z, y, x, core), device(to_z, to_y, plane // 2, plane % 2)))
    return pairs


def params(**more):
    return pltpu.CompilerParams(vmem_limit_bytes=VMEM_LIMIT, **more)


def cost(flops, moved):
    return pl.CostEstimate(flops=flops, bytes_accessed=moved, transcendentals=0)


def whole(shape):
    return pl.BlockSpec(shape, lambda *_: (0,) * len(shape))


def find_slot(rows, counts, owner, block):
    slot = jnp.int32(0)
    live = jnp.int32(0)
    for k in range(NB):
        hit = (rows[owner, k] == block) & (k < counts[owner])
        slot = jnp.where(hit, k, slot)
        live = jnp.where(hit, 1, live)
    return slot, live


def prep_body(place, rows_a, counts_a, rows_b, counts_b, fa, fb, top, a_lo, a_hi, b_lo, b_hi, top_t):
    owner = place[0]
    for rows, counts, factor, low, high in (
        (rows_a, counts_a, fa, a_lo, a_hi),
        (rows_b, counts_b, fb, b_lo, b_hi),
    ):
        for block in range(NB):
            slot, live = find_slot(rows, counts, owner, block)
            piece = factor[pl.ds(pl.multiple_of(slot * BS, BS), BS), :]
            piece = jnp.where(live > 0, piece, jnp.zeros_like(piece))
            target = low if block < HALF else high
            target[block % HALF] = piece.T
    top_t[...] = top[...].T


def prep(place, lists, factor_a, factor_b, factor_top):
    quarter = jax.ShapeDtypeStruct((HALF, 2 * BS, BS), BF)
    half_width = pl.BlockSpec((ROWS, W // 2), lambda i, place, *_: (0, place[1] % 2))
    return pl.pallas_call(
        prep_body,
        name="prep",
        grid_spec=pltpu.PrefetchScalarGridSpec(
            num_scalar_prefetch=5,
            grid=(1,),
            in_specs=[half_width, half_width, whole((W, W))],
            out_specs=[whole((HALF, 2 * BS, BS))] * 4 + [whole((W, W))],
        ),
        out_shape=[quarter] * 4 + [jax.ShapeDtypeStruct((W, W), BF)],
        compiler_params=params(),
        cost_estimate=cost(0, 4 * ROWS * W),
    )(place, *lists, factor_a, factor_b, factor_top)


def product_body(corrected, place, *refs):
    bufs = refs[:8]
    if corrected:
        tile, top_t, before, full, give, spread, sems = refs[8:]
    else:
        tile, full, give, spread, sems = refs[8:]
    core = place[1] % 2
    zc, yc = (place[1] // SIDE) % SIDE, place[1] % SIDE
    z, y = place[0] // SIDE, place[0] % SIDE

    @pl.when(pl.program_id(0) == 0)
    def _():
        copies = []
        for i in range(8):
            steps = i % 4
            q = ((z - zc) if i < 4 else (y - yc)) - steps + 2 * SIDE
            q = q % SIDE
            first = 0 if i < 4 else HALF
            copies.append(
                pltpu.make_async_copy(
                    bufs[i],
                    spread.at[
                        pl.ds(first, HALF),
                        q // 2,
                        pl.ds(pl.multiple_of((q % 2) * 2 * BS, 2 * BS), 2 * BS),
                        :,
                    ],
                    sems.at[i],
                )
            )
        for copy in copies:
            copy.start()
        for copy in copies:
            copy.wait()

    for part in range(2):
        at = slice(part * 2 * BS, (part + 1) * 2 * BS)
        left = jnp.concatenate(
            [spread[n, h, at, :] for n in range(NB) for h in range(2)], axis=1
        )
        value = lax.dot_general(
            left, tile[...], (((1,), (1,)), ((), ())), preferred_element_type=F32
        )
        if corrected:
            value = value - jnp.dot(
                top_t[at, :], before[...], preferred_element_type=F32
            )
        full[at, :] = value.astype(BF)
    for xs in range(SIDE):
        give[xs] = full[pl.ds(pl.multiple_of(xs * BS + (1 - core) * PART, PART), PART), :]


def product(place, bufs, trailing, correction=None):
    width = 2 * BS
    steps = ROWS // width
    in_specs = [pl.BlockSpec(memory_space=pl.ANY)] * 8 + [
        pl.BlockSpec((width, trailing.shape[1]), lambda i, *_: (i, 0))
    ]
    operands = [*bufs, trailing]
    if correction is not None:
        in_specs += [whole((W, W)), pl.BlockSpec((W, width), lambda i, *_: (0, i))]
        operands += list(correction)
    return pl.pallas_call(
        functools.partial(product_body, correction is not None),
        name="product",
        grid_spec=pltpu.PrefetchScalarGridSpec(
            num_scalar_prefetch=1,
            grid=(steps,),
            in_specs=in_specs,
            out_specs=[
                pl.BlockSpec((W, width), lambda i, *_: (0, i)),
                pl.BlockSpec((SIDE, PART, width), lambda i, *_: (0, 0, i)),
            ],
            scratch_shapes=[
                pltpu.VMEM((NB, 2, W, BS), BF),
                pltpu.SemaphoreType.DMA((8,)),
            ],
        ),
        out_shape=[
            jax.ShapeDtypeStruct((W, ROWS), BF),
            jax.ShapeDtypeStruct((SIDE, PART, ROWS), BF),
        ],
        compiler_params=params(dimension_semantics=("arbitrary",)),
        cost_estimate=cost(2 * W * ROWS * 2 * ROWS, 2 * ROWS * 2 * ROWS + 6 * W * ROWS),
    )(place, *operands)


def pair_body(place, full, taken, *outs):
    core, x = place[1] % 2, place[1] // 2
    for i in range(SIDE):
        xs = (x + i) % SIDE
        mine = full[pl.ds(pl.multiple_of(xs * BS + core * PART, PART), PART), :]
        outs[i][...] = (mine.astype(F32) + taken[xs].astype(F32)).astype(BF)


def pair_sum(place, full, taken):
    return pl.pallas_call(
        pair_body,
        name="pair_sum",
        grid_spec=pltpu.PrefetchScalarGridSpec(
            num_scalar_prefetch=1,
            grid=(1,),
            in_specs=[whole((W, ROWS)), whole((SIDE, PART, ROWS))],
            out_specs=[whole((PART, ROWS))] * SIDE,
        ),
        out_shape=[jax.ShapeDtypeStruct((PART, ROWS), BF)] * SIDE,
        compiler_params=params(),
        cost_estimate=cost(W * ROWS, 3 * W * ROWS),
    )(place, full, taken)


def cut(outcome, pieces, first):
    rows = outcome.shape[0] // SIDE
    for p in range(16):
        up, across = p // SIDE, p % SIDE
        pieces[p] = outcome[up * rows : (up + 1) * rows, across * BS : (across + 1) * BS].astype(BF)


def slots_body(with_a, place, rows_a, counts_a, rows_b, counts_b, *refs):
    if with_a:
        s0, s1, s2, s3, fa, fb, column, pieces, natural, carried = refs
    else:
        s0, s1, s2, s3, fb, column, pieces, natural = refs
    owner = place[0]
    total = (s0[...].astype(F32) + s1[...].astype(F32)) + (
        s2[...].astype(F32) + s3[...].astype(F32)
    )
    natural[...] = (-total).astype(BF)

    def place_slots(rows, counts, target):
        for k in range(NB):
            block = rows[owner, k]
            piece = natural[:, pl.ds(pl.multiple_of(block * BS, BS), BS)]
            target[:, k * BS : (k + 1) * BS] = jnp.where(
                k < counts[owner], piece, jnp.zeros_like(piece)
            )

    if with_a:
        place_slots(rows_a, counts_a, column)
        place_slots(rows_b, counts_b, carried)
        first = jnp.dot(column[...], fa[...], preferred_element_type=F32)
        second = jnp.dot(carried[...], fb[...], preferred_element_type=F32)
        cut(jnp.concatenate([first, second], axis=0), pieces, 0)
    else:
        place_slots(rows_b, counts_b, column)
        cut(jnp.dot(column[...], fb[...], preferred_element_type=F32), pieces, 0)


def slots(place, lists, slabs, factors):
    with_a = len(factors) == 2
    rows = PART * len(factors) // SIDE
    return pl.pallas_call(
        functools.partial(slots_body, with_a),
        name="slots",
        grid_spec=pltpu.PrefetchScalarGridSpec(
            num_scalar_prefetch=5,
            grid=(1,),
            in_specs=[whole((PART, ROWS))] * SIDE + [whole((ROWS, W))] * len(factors),
            out_specs=[whole((PART, ROWS)), whole((16, rows, BS))],
            scratch_shapes=[pltpu.VMEM((PART, ROWS), BF)] * len(factors),
        ),
        out_shape=[
            jax.ShapeDtypeStruct((PART, ROWS), BF),
            jax.ShapeDtypeStruct((16, rows, BS), BF),
        ],
        compiler_params=params(),
        cost_estimate=cost(
            2 * PART * ROWS * W * len(factors), 2 * ROWS * W * len(factors) + 10 * PART * ROWS
        ),
    )(place, *lists, *slabs, *factors)


def column_body(place, *refs):
    slabs, out, scratch = refs[:8], refs[8], refs[9]
    core, x = place[1] % 2, place[1] // 2
    for i in range(8):
        xs = (x - i % SIDE + SIDE) % SIDE
        which = core if i < SIDE else 1 - core
        scratch[pl.ds(pl.multiple_of(xs * BS + which * PART, PART), PART), :] = slabs[i][...]
    out[...] = scratch[...].T


def whole_column(place, slabs):
    lanes = 4 * BS
    return pl.pallas_call(
        column_body,
        name="whole_column",
        grid_spec=pltpu.PrefetchScalarGridSpec(
            num_scalar_prefetch=1,
            grid=(ROWS // lanes,),
            in_specs=[pl.BlockSpec((PART, lanes), lambda i, *_: (0, i))] * 8,
            out_specs=pl.BlockSpec((lanes, W), lambda i, *_: (i, 0)),
            scratch_shapes=[pltpu.VMEM((W, lanes), BF)],
        ),
        out_shape=jax.ShapeDtypeStruct((ROWS, W), BF),
        compiler_params=params(dimension_semantics=("arbitrary",)),
        cost_estimate=cost(0, 4 * ROWS * W),
    )(place, *slabs)


def send(value, **by):
    return lax.ppermute(value, BOTH, shifted(**by))


def gather_factor(low, high):
    low = lax.ppermute(low, BOTH, spread_pairs(True))
    high = lax.ppermute(high, BOTH, spread_pairs(False))
    lows = [low, send(low, dz=1), send(low, dz=2), send(low, dz=-1)]
    highs = [high, send(high, dy=1), send(high, dy=2), send(high, dy=-1)]
    return lows + highs


def scatter_sum(place, full, give):
    taken = send(give, dc=1)
    own, one, two, three = pair_sum(place, full, taken)
    return [own, send(one, dx=1), send(two, dx=2), send(three, dx=-1)]


def gather_column(place, column):
    mine = [column, send(column, dx=1), send(column, dx=2), send(column, dx=-1)]
    return whole_column(place, mine + [send(slab, dc=1) for slab in mine])


def row_sum(pieces):
    count, rows, lanes = pieces.shape
    parts = lax.all_to_all(pieces, "row", 0, 0)
    summed = jnp.sum(parts.astype(F32), axis=0).astype(BF)
    spread = jnp.broadcast_to(summed[None], pieces.shape)
    got = lax.all_to_all(spread, "row", 0, 0)
    got = got.reshape(SIDE, SIDE, rows, lanes).transpose(0, 2, 1, 3)
    return got.reshape(SIDE * rows, W).astype(F32)


def on_device(
    trailing, rows_a, counts_a, factor_a, rows_b, counts_b, factor_b, factor_top, base_a, base_b
):
    place = jnp.stack([lax.axis_index("row"), lax.axis_index("col")]).astype(jnp.int32)
    lists = (rows_a, counts_a, rows_b, counts_b)
    a_lo, a_hi, b_lo, b_hi, top_t = prep(place, lists, factor_a, factor_b, factor_top)
    bufs_a = gather_factor(a_lo, a_hi)
    bufs_b = gather_factor(b_lo, b_hi)
    full_a, give_a = product(place, bufs_a, trailing)
    slabs_a = scatter_sum(place, full_a, give_a)
    full_b, give_b = product(place, bufs_b, trailing, (top_t, full_a))
    slabs_b = scatter_sum(place, full_b, give_b)

    part_a, pieces_a = slots(place, lists, slabs_a, (factor_a, factor_b))
    column_a = gather_column(place, part_a)
    sums_a = row_sum(pieces_a)
    diag_a = base_a - sums_a[:PART]
    top_b = (
        -(
            sums_a[PART:]
            + jnp.dot(diag_a, factor_top.astype(F32), precision=lax.Precision.HIGHEST)
        )
    ).astype(BF)
    blocks = top_b.reshape(PART, 8, PART).transpose(1, 0, 2)
    top_cols = lax.all_to_all(blocks, "col", 0, 0).reshape(W, PART)

    part_b, pieces_b = slots(place, lists, slabs_b, (factor_b,))
    column_b = gather_column(place, part_b)
    cross = lax.dot_general(
        top_cols, factor_top, (((0,), (0,)), ((), ())), preferred_element_type=F32
    )
    diag_b = base_b - row_sum(pieces_b) - cross
    return (column_a, diag_a, column_b, top_b, diag_b)


def solution(mesh):
    in_specs = (
        P("row", "col"),
        P(),
        P(),
        P("row", None),
        P(),
        P(),
        P("row", None),
        P(),
        P("col", None),
        P("col", None),
    )
    out_specs = (P("row", None), P("col", None), P("row", None), P("col", None), P("col", None))
    return jax.shard_map(
        on_device, mesh=mesh, in_specs=in_specs, out_specs=out_specs, check_vma=False
    )
```

```python
import functools

import jax
import jax.numpy as jnp
from jax import lax
from jax.experimental import pallas as pl
from jax.experimental.pallas import tpu as pltpu
from jax.sharding import PartitionSpec as P

BS = 128
W = 512
NB = 12
ROWS = NB * BS
SIDE = 4
PART = 64
COLS = 8
PAIR = 2 * PART
BOTH = ("row", "col")
MIB = 1024 * 1024
BF = jnp.bfloat16
F32 = jnp.float32


def device(z, y, x, core):
    return ((z % SIDE) * SIDE + y % SIDE) * 8 + (x % SIDE) * 2 + core % 2


def all_places():
    return [
        (z, y, x, core)
        for z in range(SIDE)
        for y in range(SIDE)
        for x in range(SIDE)
        for core in range(2)
    ]


def shifted(dz=0, dy=0, dx=0, dc=0):
    return [
        (device(z, y, x, c), device(z + dz, y + dy, x + dx, c + dc))
        for z, y, x, c in all_places()
    ]


def spread_pairs():
    pairs = []
    for z, y, x, core in all_places():
        plane = (z * SIDE + y) % 8
        far = (2 - (x - plane // 2)) % SIDE
        to = device(z + core, y + far, plane // 2, plane % 2)
        pairs.append((device(z, y, x, core), to))
    return pairs


def params(mib=24, **more):
    return pltpu.CompilerParams(vmem_limit_bytes=mib * MIB, **more)


def cost(flops, moved):
    return pl.CostEstimate(flops=flops, bytes_accessed=moved, transcendentals=0)


def whole(shape):
    return pl.BlockSpec(shape, lambda *_: (0,) * len(shape))


def find_slot(rows, counts, owner, block):
    slot = jnp.int32(0)
    live = jnp.int32(0)
    for k in range(NB):
        hit = (rows[owner, k] == block) & (k < counts[owner])
        slot = jnp.where(hit, k, slot)
        live = jnp.where(hit, 1, live)
    return slot, live


def prep_body(place, rows_a, counts_a, rows_b, counts_b, fa, fb, top, out, top_t):
    owner = place[0]
    upper = place[1] % 2
    for first, rows, counts, factor in (
        (0, rows_a, counts_a, fa),
        (PART, rows_b, counts_b, fb),
    ):
        for block in range(NB):
            slot, live = find_slot(rows, counts, owner, block)
            piece = factor[pl.ds(pl.multiple_of(slot * BS, BS), BS), :].T
            piece = jnp.where(upper > 0, piece[PART:], piece[:PART])
            piece = jnp.where(live > 0, piece, jnp.zeros_like(piece))
            out[block, first : first + PART, :] = piece
    top_t[...] = top[...].T


def prep(place, lists, factor_a, factor_b, factor_top):
    slice_spec = pl.BlockSpec((ROWS, BS), lambda i, place, *_: (0, place[1] // 2))
    return pl.pallas_call(
        prep_body,
        name="prep",
        grid_spec=pltpu.PrefetchScalarGridSpec(
            num_scalar_prefetch=5,
            grid=(1,),
            in_specs=[slice_spec, slice_spec, whole((W, W))],
            out_specs=[whole((NB, PAIR, BS)), whole((W, W))],
        ),
        out_shape=[
            jax.ShapeDtypeStruct((NB, PAIR, BS), BF),
            jax.ShapeDtypeStruct((W, W), BF),
        ],
        compiler_params=params(),
        cost_estimate=cost(0, 4 * ROWS * BS),
    )(place, *lists, factor_a, factor_b, factor_top)


def product_body(place, gathered, tile, top_t, keep, give, spread, sums, ready, sems):
    plane = place[1]
    core = plane % 2

    @pl.when(pl.program_id(0) == 0)
    def _():
        copies = []
        for h in range(2):
            for c in range(COLS):
                far = (2 - (c // 2 - plane // 2) + SIDE) % SIDE
                z = (plane // SIDE + 2 * h + c % 2) % SIDE
                y = (plane % SIDE + far) % SIDE
                copies.append(
                    pltpu.make_async_copy(
                        gathered.at[z * SIDE + y],
                        spread.at[:, h, pl.ds(c * PAIR, PAIR), :],
                        sems.at[h * COLS + c],
                    )
                )
        for copy in copies:
            copy.start()
        for copy in copies:
            copy.wait()

    for c in range(0, COLS, 2):
        at = slice(c * PAIR, (c + 2) * PAIR)
        left = jnp.concatenate(
            [spread[n, h, at, :] for n in range(NB) for h in range(2)], axis=1
        )
        value = lax.dot_general(
            left, tile[...], (((1,), (1,)), ((), ())), preferred_element_type=F32
        )
        sums[c : c + 2] = value.reshape(2, PAIR, value.shape[1])
    first = sums[:, :PART, :].astype(BF)
    fix = jnp.dot(top_t[...], first.reshape(W, first.shape[2]), preferred_element_type=F32)
    ready[:, :PART, :] = first
    ready[:, PART:, :] = (sums[:, PART:, :] - fix.reshape(COLS, PART, fix.shape[1])).astype(BF)
    for x in range(SIDE):
        keep[x] = ready[2 * x + core]
        give[x] = ready[2 * x + 1 - core]


def product(place, gathered, trailing, top_t):
    width = 2 * BS
    deep = trailing.shape[1]
    out = jax.ShapeDtypeStruct((SIDE, PAIR, ROWS), BF)
    spec = pl.BlockSpec((SIDE, PAIR, width), lambda i, *_: (0, 0, i))
    return pl.pallas_call(
        product_body,
        name="product",
        grid_spec=pltpu.PrefetchScalarGridSpec(
            num_scalar_prefetch=1,
            grid=(ROWS // width,),
            in_specs=[
                pl.BlockSpec(memory_space=pl.ANY),
                pl.BlockSpec((width, deep), lambda i, *_: (i, 0)),
                whole((W, W)),
            ],
            out_specs=[spec, spec],
            scratch_shapes=[
                pltpu.VMEM((NB, 2, 2 * W, BS), BF),
                pltpu.VMEM((COLS, PAIR, width), F32),
                pltpu.VMEM((COLS, PAIR, width), BF),
                pltpu.SemaphoreType.DMA((2 * COLS,)),
            ],
        ),
        out_shape=[out, out],
        compiler_params=params(56, dimension_semantics=("arbitrary",)),
        cost_estimate=cost(4 * W * ROWS * deep, 2 * ROWS * deep + 4 * W * deep + 4 * W * ROWS),
    )(place, gathered, trailing, top_t)


def pair_body(place, mine, taken, *outs):
    x = place[1] // 2
    for i in range(SIDE):
        at = (x + i) % SIDE
        outs[i][...] = (mine[at].astype(F32) + taken[at].astype(F32)).astype(BF)


def pair_sum(place, mine, taken):
    lanes = 4 * BS
    spec = pl.BlockSpec((SIDE, PAIR, lanes), lambda i, *_: (0, 0, i))
    return pl.pallas_call(
        pair_body,
        name="pair_sum",
        grid_spec=pltpu.PrefetchScalarGridSpec(
            num_scalar_prefetch=1,
            grid=(ROWS // lanes,),
            in_specs=[spec, spec],
            out_specs=[pl.BlockSpec((PAIR, lanes), lambda i, *_: (0, i))] * SIDE,
        ),
        out_shape=[jax.ShapeDtypeStruct((PAIR, ROWS), BF)] * SIDE,
        compiler_params=params(dimension_semantics=("arbitrary",)),
        cost_estimate=cost(W * ROWS, 6 * W * ROWS),
    )(place, mine, taken)


def slots_body(
    place, rows_a, counts_a, rows_b, counts_b, s0, s1, s2, s3, fa, fb, columns, pieces, natural, left
):
    owner = place[0]
    total = (s0[...].astype(F32) + s1[...].astype(F32)) + (
        s2[...].astype(F32) + s3[...].astype(F32)
    )
    natural[...] = (-total).astype(BF)
    for k in range(NB):
        at = slice(k * BS, (k + 1) * BS)
        block = natural[:PART, pl.ds(pl.multiple_of(rows_a[owner, k] * BS, BS), BS)]
        columns[:PART, at] = jnp.where(k < counts_a[owner], block, jnp.zeros_like(block))
        block = natural[:, pl.ds(pl.multiple_of(rows_b[owner, k] * BS, BS), BS)]
        block = jnp.where(k < counts_b[owner], block, jnp.zeros_like(block))
        left[:, at] = block
        columns[PART:, at] = block[PART:]
    one = jnp.dot(columns[:PART, :], fa[...], preferred_element_type=F32)
    two = jnp.dot(left[...], fb[...], preferred_element_type=F32)
    outcome = jnp.concatenate([one, two], axis=0).astype(BF)
    rows = outcome.shape[0] // SIDE
    for p in range(SIDE * SIDE):
        up, across = p // SIDE, p % SIDE
        pieces[p] = outcome[up * rows : (up + 1) * rows, across * BS : (across + 1) * BS]


def slots(place, lists, slabs, factors):
    rows = 3 * PART // SIDE
    return pl.pallas_call(
        slots_body,
        name="slots",
        grid_spec=pltpu.PrefetchScalarGridSpec(
            num_scalar_prefetch=5,
            grid=(1,),
            in_specs=[whole((PAIR, ROWS))] * SIDE + [whole((ROWS, W))] * 2,
            out_specs=[whole((PAIR, ROWS)), whole((SIDE * SIDE, rows, BS))],
            scratch_shapes=[pltpu.VMEM((PAIR, ROWS), BF)] * 2,
        ),
        out_shape=[
            jax.ShapeDtypeStruct((PAIR, ROWS), BF),
            jax.ShapeDtypeStruct((SIDE * SIDE, rows, BS), BF),
        ],
        compiler_params=params(),
        cost_estimate=cost(6 * PART * ROWS * W, 4 * ROWS * W + 10 * PAIR * ROWS),
    )(place, *lists, *slabs, *factors)


def column_body(slabs, column_a, column_b):
    for first, out in ((0, column_a), (PART, column_b)):
        out[...] = slabs[:, first : first + PART, :].reshape(W, slabs.shape[2]).T


def whole_columns(slabs):
    lanes = 2 * BS
    out = jax.ShapeDtypeStruct((ROWS, W), BF)
    return pl.pallas_call(
        column_body,
        name="whole_columns",
        grid=(ROWS // lanes,),
        in_specs=[pl.BlockSpec((COLS, PAIR, lanes), lambda i: (0, 0, i))],
        out_specs=[pl.BlockSpec((lanes, W), lambda i: (i, 0))] * 2,
        out_shape=[out, out],
        compiler_params=params(dimension_semantics=("arbitrary",)),
        cost_estimate=cost(0, 8 * ROWS * W),
    )(slabs)


def fold_body(parts, out):
    total = jnp.sum(parts[...].astype(F32), axis=0).astype(BF)
    out[...] = jnp.broadcast_to(total[None], out.shape)


def row_sum(pieces):
    parts = lax.all_to_all(pieces, "row", 0, 0)
    spread = pl.pallas_call(
        fold_body,
        name="fold",
        out_shape=jax.ShapeDtypeStruct(pieces.shape, BF),
        compiler_params=params(8),
        cost_estimate=cost(pieces.size, 4 * pieces.size),
    )(parts)
    return lax.all_to_all(spread, "row", 0, 0)


def sums_of(got, first, last):
    rows = got.shape[1]
    up = range(first // rows, (last + rows - 1) // rows)
    wide = [
        jnp.concatenate([got[u * SIDE + v] for v in range(SIDE)], axis=1).astype(F32) for u in up
    ]
    start = first - up[0] * rows
    return jnp.concatenate(wide, axis=0)[start : start + last - first]


def top_body(got, base, top, diag_a, top_b, sent):
    value = base[...] - sums_of(got, 0, PART)
    diag_a[...] = value
    total = sums_of(got, PART, 2 * PART)
    for _ in range(3):
        part = value.astype(BF)
        value = value - part.astype(F32)
        total = total + jnp.dot(part, top[...], preferred_element_type=F32)
    total = (-total).astype(BF)
    top_b[...] = total
    for c in range(COLS):
        sent[c] = jnp.concatenate([total[:, c * PART : (c + 1) * PART]] * 2, axis=1)


def top_part(got, base_a, factor_top):
    return pl.pallas_call(
        top_body,
        name="top_part",
        out_shape=[
            jax.ShapeDtypeStruct((PART, W), F32),
            jax.ShapeDtypeStruct((PART, W), BF),
            jax.ShapeDtypeStruct((COLS, PART, 2 * PART), BF),
        ],
        compiler_params=params(8),
        cost_estimate=cost(6 * PART * W * W, 2 * W * W),
    )(got, base_a, factor_top)


def last_body(got, base, taken, top, diag_b):
    across = taken[...].reshape(W, 2 * PART)
    cross = lax.dot_general(
        across, top[...], (((0,), (0,)), ((), ())), preferred_element_type=F32
    )
    diag_b[...] = base[...] - sums_of(got, 2 * PART, 3 * PART) - cross[:PART]


def last_part(got, base_b, taken, factor_top):
    return pl.pallas_call(
        last_body,
        name="last_part",
        out_shape=jax.ShapeDtypeStruct((PART, W), F32),
        compiler_params=params(8),
        cost_estimate=cost(4 * PART * W * W, 2 * W * W),
    )(got, base_b, taken, factor_top)


def send(value, **by):
    return lax.ppermute(value, BOTH, shifted(**by))


def on_device(
    trailing, rows_a, counts_a, factor_a, rows_b, counts_b, factor_b, factor_top, base_a, base_b
):
    place = jnp.stack([lax.axis_index("row"), lax.axis_index("col")]).astype(jnp.int32)
    lists = (rows_a, counts_a, rows_b, counts_b)
    chunk, top_t = prep(place, lists, factor_a, factor_b, factor_top)
    chunk = lax.ppermute(chunk, BOTH, spread_pairs())
    gathered = lax.all_gather(chunk, "row", axis=0)
    keep, give = product(place, gathered, trailing, top_t)
    own, one, two, three = pair_sum(place, keep, send(give, dc=1))
    slabs = [own, send(one, dx=1), send(two, dx=2), send(three, dx=-1)]
    columns, pieces = slots(place, lists, slabs, (factor_a, factor_b))
    column_a, column_b = whole_columns(lax.all_gather(columns, "col", axis=0))
    got = row_sum(pieces)
    diag_a, top_b, sent = top_part(got, base_a, factor_top)
    taken = lax.all_to_all(sent, "col", 0, 0)
    diag_b = last_part(got, base_b, taken, factor_top)
    return (column_a, diag_a, column_b, top_b, diag_b)


def solution(mesh):
    in_specs = (
        P("row", "col"),
        P(),
        P(),
        P("row", None),
        P(),
        P(),
        P("row", None),
        P(),
        P("col", None),
        P("col", None),
    )
    out_specs = (P("row", None), P("col", None), P("row", None), P("col", None), P("col", None))
    return jax.shard_map(
        on_device, mesh=mesh, in_specs=in_specs, out_specs=out_specs, check_vma=False
    )
```

```python
import functools

import jax
import jax.numpy as jnp
from jax import lax
from jax.experimental import pallas as pl
from jax.experimental.pallas import tpu as pltpu
from jax.sharding import PartitionSpec as P

BS = 128
W = 512
NB = 12
ROWS = NB * BS
SIDE = 4
PART = 64
COLS = 8
STEPS = (0, 1, -1, 2)
PAIR = 2 * PART
BOTH = ("row", "col")
MIB = 1024 * 1024
BF = jnp.bfloat16
F32 = jnp.float32


def device(z, y, x, core):
    return ((z % SIDE) * SIDE + y % SIDE) * 8 + (x % SIDE) * 2 + core % 2


def all_places():
    return [
        (z, y, x, core)
        for z in range(SIDE)
        for y in range(SIDE)
        for x in range(SIDE)
        for core in range(2)
    ]


def shifted(dz=0, dy=0, dx=0, dc=0):
    return [
        (device(z, y, x, c), device(z + dz, y + dy, x + dx, c + dc))
        for z, y, x, c in all_places()
    ]


def spread_pairs():
    pairs = []
    for z, y, x, core in all_places():
        plane = (z * SIDE + y) % 8
        to = device(z + core, y + x, plane // 2, plane % 2)
        pairs.append((device(z, y, x, core), to))
    return pairs


def params(mib=24, **more):
    return pltpu.CompilerParams(vmem_limit_bytes=mib * MIB, **more)


def cost(flops, moved):
    return pl.CostEstimate(flops=flops, bytes_accessed=moved, transcendentals=0)


def whole(shape):
    return pl.BlockSpec(shape, lambda *_: (0,) * len(shape))


def find_slot(rows, counts, owner, block):
    slot = jnp.int32(0)
    live = jnp.int32(0)
    for k in range(NB):
        hit = (rows[owner, k] == block) & (k < counts[owner])
        slot = jnp.where(hit, k, slot)
        live = jnp.where(hit, 1, live)
    return slot, live


def prep_body(place, rows_a, counts_a, rows_b, counts_b, fa, part_a, part_b, top, out_a, out_b, fix):
    owner = place[0]
    upper = place[1] % 2
    fix[...] = lax.dot_general(
        top[...], fa[...], (((0,), (1,)), ((), ())), preferred_element_type=F32
    )

    def half(value):
        return jnp.where(upper > 0, value[PART:], value[:PART])

    for block in range(NB):
        slot_a, live_a = find_slot(rows_a, counts_a, owner, block)
        slot_b, live_b = find_slot(rows_b, counts_b, owner, block)
        at_a = pl.ds(pl.multiple_of(slot_a * BS, BS), BS)
        at_b = pl.ds(pl.multiple_of(slot_b * BS, BS), BS)
        piece = half(part_a[at_a, :].T)
        out_a[block] = jnp.where(live_a > 0, piece, jnp.zeros_like(piece))
        moved = half(fix[:, at_a])
        piece = half(part_b[at_b, :].T).astype(F32)
        piece = jnp.where(live_b > 0, piece, jnp.zeros_like(piece))
        out_b[block] = (piece - jnp.where(live_a > 0, moved, jnp.zeros_like(moved))).astype(BF)


def prep(place, lists, factor_a, factor_b, factor_top):
    slice_spec = pl.BlockSpec((ROWS, BS), lambda i, place, *_: (0, place[1] // 2))
    out = jax.ShapeDtypeStruct((NB, PART, BS), BF)
    return pl.pallas_call(
        prep_body,
        name="prep",
        grid_spec=pltpu.PrefetchScalarGridSpec(
            num_scalar_prefetch=5,
            grid=(1,),
            in_specs=[
                whole((ROWS, W)),
                slice_spec,
                slice_spec,
                pl.BlockSpec((W, BS), lambda i, place, *_: (0, place[1] // 2)),
            ],
            out_specs=[whole((NB, PART, BS))] * 2,
            scratch_shapes=[pltpu.VMEM((BS, ROWS), F32)],
        ),
        out_shape=[out, out],
        compiler_params=params(56),
        cost_estimate=cost(2 * BS * ROWS * W, 2 * ROWS * (W + 4 * BS)),
    )(place, *lists, factor_a, factor_a, factor_b, factor_top)


def where(place):
    z, y, plane = place[0] // SIDE, place[0] % SIDE, place[1]
    u = (z - plane // SIDE + SIDE) % SIDE
    v = (y - plane % SIDE + SIDE) % SIDE
    return u, v


def turn(value, by):
    return (value + by + SIDE) % SIDE


def load_a(copies, buf, picks, u, spread, sems):
    for i, member in picks:
        copies.append((buf.at[member], spread.at[:, u // 2, i * PART : (i + 1) * PART, :]))


def load_b(copies, buf, picks, u, first, spread, sems):
    for i, member in picks:
        ui = turn(u, -STEPS[i])
        at = pl.ds(pl.multiple_of(first + (ui % 2) * PART, PART), PART)
        copies.append((buf.at[member], spread.at[:, ui // 2, at, :]))


def run_copies(copies, sems):
    started = [pltpu.make_async_copy(a, b, sems.at[i]) for i, (a, b) in enumerate(copies)]
    for copy in started:
        copy.start()
    for copy in started:
        copy.wait()


def multiply(spread, tile, first, last):
    left = jnp.concatenate(
        [spread[n, h, first:last, :] for n in range(NB) for h in range(2)], axis=1
    )
    return lax.dot_general(
        left, tile[...], (((1,), (1,)), ((), ())), preferred_element_type=F32
    ).astype(BF)


ALL = tuple((i, i) for i in range(SIDE))
FIRST = ((0, 0), (1, 1))
LAST = ((2, 0), (3, 1))


def early_body(place, a_down, a_up, b_own, b_down, b_up, tile, out, spread, sems):
    u, v = where(place)

    @pl.when(pl.program_id(0) == 0)
    def _():
        copies = []
        load_a(copies, a_down, ALL, turn(u, -1), spread, sems)
        load_a(copies, a_up, ALL, turn(u, 1), spread, sems)
        for t, buf in enumerate((b_own, b_down, b_up)):
            load_b(copies, buf, ALL, u, W // 2 + 2 * t * PART, spread, sems)
        run_copies(copies, sems)

    value = multiply(spread, tile, 0, W // 2)
    for i, step in enumerate(STEPS):
        out[2 * turn(v, -step) + (u + 1) % 2, :PART, :] = value[i * PART : (i + 1) * PART]
    for first, many in ((0, 2), (2, 1)):
        value = multiply(
            spread, tile, W // 2 + 2 * first * PART, W // 2 + 2 * (first + many) * PART
        )
        for j in range(2 * many):
            to = 2 * turn(v, -STEPS[first + j // 2]) + j % 2
            out[to, PART:, :] = value[j * PART : (j + 1) * PART]


def early_product(place, bufs, trailing):
    width = 2 * BS
    deep = trailing.shape[1]
    rows = W // 2 + 6 * PART
    return pl.pallas_call(
        early_body,
        name="early_product",
        grid_spec=pltpu.PrefetchScalarGridSpec(
            num_scalar_prefetch=1,
            grid=(ROWS // width,),
            in_specs=[pl.BlockSpec(memory_space=pl.ANY)] * 5
            + [pl.BlockSpec((width, deep), lambda i, *_: (i, 0))],
            out_specs=pl.BlockSpec((COLS, PAIR, width), lambda i, *_: (0, 0, i)),
            scratch_shapes=[
                pltpu.VMEM((NB, 2, rows, BS), BF),
                pltpu.SemaphoreType.DMA((20,)),
            ],
        ),
        out_shape=jax.ShapeDtypeStruct((COLS, PAIR, ROWS), BF),
        compiler_params=params(52, dimension_semantics=("arbitrary",)),
        cost_estimate=cost(2 * rows * ROWS * deep, 2 * ROWS * deep + 2 * rows * deep + 4 * W * ROWS),
    )(place, *bufs, trailing)


def late_body(
    place, a_own, a_far, a_far_more, b_far, b_far_more, tile, before, keep, give, spread, ready, sems
):
    u, v = where(place)
    core = place[1] % 2

    @pl.when(pl.program_id(0) == 0)
    def _():
        copies = []
        load_a(copies, a_own, ALL, u, spread, sems)
        load_a(copies, a_far, FIRST, turn(u, 2), spread, sems)
        load_a(copies, a_far_more, LAST, turn(u, 2), spread, sems)
        load_b(copies, b_far, FIRST, u, W // 2, spread, sems)
        load_b(copies, b_far_more, LAST, u, W // 2, spread, sems)
        run_copies(copies, sems)

    ready[...] = before[...]
    value = multiply(spread, tile, 0, W // 2)
    for i, step in enumerate(STEPS):
        ready[2 * turn(v, -step) + u % 2, :PART, :] = value[i * PART : (i + 1) * PART]
    value = multiply(spread, tile, W // 2, W // 2 + 2 * PART)
    for j in range(2):
        ready[2 * turn(v, 2) + j, PART:, :] = value[j * PART : (j + 1) * PART]
    for x in range(SIDE):
        keep[x] = ready[2 * x + core]
        give[x] = ready[2 * x + 1 - core]


def late_product(place, bufs, trailing, before):
    width = 2 * BS
    deep = trailing.shape[1]
    rows = W // 2 + 2 * PART
    out = jax.ShapeDtypeStruct((SIDE, PAIR, ROWS), BF)
    spec = pl.BlockSpec((SIDE, PAIR, width), lambda i, *_: (0, 0, i))
    return pl.pallas_call(
        late_body,
        name="late_product",
        grid_spec=pltpu.PrefetchScalarGridSpec(
            num_scalar_prefetch=1,
            grid=(ROWS // width,),
            in_specs=[pl.BlockSpec(memory_space=pl.ANY)] * 5
            + [
                pl.BlockSpec((width, deep), lambda i, *_: (i, 0)),
                pl.BlockSpec((COLS, PAIR, width), lambda i, *_: (0, 0, i)),
            ],
            out_specs=[spec, spec],
            scratch_shapes=[
                pltpu.VMEM((NB, 2, rows, BS), BF),
                pltpu.VMEM((COLS, PAIR, width), BF),
                pltpu.SemaphoreType.DMA((12,)),
            ],
        ),
        out_shape=[out, out],
        compiler_params=params(52, dimension_semantics=("arbitrary",)),
        cost_estimate=cost(2 * rows * ROWS * deep, 2 * ROWS * deep + 2 * rows * deep + 8 * W * ROWS),
    )(place, *bufs, trailing, before)


def pair_body(place, mine, taken, *outs):
    x = place[1] // 2
    for i in range(SIDE):
        at = (x + i) % SIDE
        outs[i][...] = (mine[at].astype(F32) + taken[at].astype(F32)).astype(BF)


def pair_sum(place, mine, taken):
    lanes = 4 * BS
    spec = pl.BlockSpec((SIDE, PAIR, lanes), lambda i, *_: (0, 0, i))
    return pl.pallas_call(
        pair_body,
        name="pair_sum",
        grid_spec=pltpu.PrefetchScalarGridSpec(
            num_scalar_prefetch=1,
            grid=(ROWS // lanes,),
            in_specs=[spec, spec],
            out_specs=[pl.BlockSpec((PAIR, lanes), lambda i, *_: (0, i))] * SIDE,
        ),
        out_shape=[jax.ShapeDtypeStruct((PAIR, ROWS), BF)] * SIDE,
        compiler_params=params(dimension_semantics=("arbitrary",)),
        cost_estimate=cost(W * ROWS, 6 * W * ROWS),
    )(place, mine, taken)


def slots_body(
    place, rows_a, counts_a, rows_b, counts_b, s0, s1, s2, s3, fa, fb, columns, pieces, natural, left
):
    owner = place[0]
    total = (s0[...].astype(F32) + s1[...].astype(F32)) + (
        s2[...].astype(F32) + s3[...].astype(F32)
    )
    natural[...] = (-total).astype(BF)
    for k in range(NB):
        at = slice(k * BS, (k + 1) * BS)
        block = natural[:PART, pl.ds(pl.multiple_of(rows_a[owner, k] * BS, BS), BS)]
        columns[:PART, at] = jnp.where(k < counts_a[owner], block, jnp.zeros_like(block))
        block = natural[:, pl.ds(pl.multiple_of(rows_b[owner, k] * BS, BS), BS)]
        block = jnp.where(k < counts_b[owner], block, jnp.zeros_like(block))
        left[:, at] = block
        columns[PART:, at] = block[PART:]
    one = jnp.dot(columns[:PART, :], fa[...], preferred_element_type=F32)
    two = jnp.dot(left[...], fb[...], preferred_element_type=F32)
    pieces[:PART, :] = one.astype(BF)
    pieces[PART:, :] = two.astype(BF)


def slots(place, lists, slabs, factors):
    return pl.pallas_call(
        slots_body,
        name="slots",
        grid_spec=pltpu.PrefetchScalarGridSpec(
            num_scalar_prefetch=5,
            grid=(1,),
            in_specs=[whole((PAIR, ROWS))] * SIDE + [whole((ROWS, W))] * 2,
            out_specs=[whole((PAIR, ROWS)), whole((3 * PART, W))],
            scratch_shapes=[pltpu.VMEM((PAIR, ROWS), BF)] * 2,
        ),
        out_shape=[
            jax.ShapeDtypeStruct((PAIR, ROWS), BF),
            jax.ShapeDtypeStruct((3 * PART, W), BF),
        ],
        compiler_params=params(),
        cost_estimate=cost(6 * PART * ROWS * W, 4 * ROWS * W + 10 * PAIR * ROWS),
    )(place, *lists, *slabs, *factors)


def column_body(place, *refs):
    slabs, column_a, column_b, wide = refs[:8], refs[8], refs[9], refs[10]
    core, x = place[1] % 2, place[1] // 2
    for i in range(8):
        at = 2 * turn(x, -STEPS[i % SIDE]) + (core if i < SIDE else 1 - core)
        wide[at] = slabs[i][...]
    for first, out in ((0, column_a), (PART, column_b)):
        out[...] = wide[:, first : first + PART, :].reshape(W, wide.shape[2]).T


def whole_columns(place, slabs):
    lanes = 2 * BS
    out = jax.ShapeDtypeStruct((ROWS, W), BF)
    return pl.pallas_call(
        column_body,
        name="whole_columns",
        grid_spec=pltpu.PrefetchScalarGridSpec(
            num_scalar_prefetch=1,
            grid=(ROWS // lanes,),
            in_specs=[pl.BlockSpec((PAIR, lanes), lambda i, *_: (0, i))] * 8,
            out_specs=[pl.BlockSpec((lanes, W), lambda i, *_: (i, 0))] * 2,
            scratch_shapes=[pltpu.VMEM((COLS, PAIR, lanes), BF)],
        ),
        out_shape=[out, out],
        compiler_params=params(dimension_semantics=("arbitrary",)),
        cost_estimate=cost(0, 8 * ROWS * W),
    )(place, *slabs)


def total_of(refs, rows):
    parts = [ref[rows, :].astype(F32) for ref in refs]
    return (parts[0] + parts[1]) + (parts[2] + parts[3])


def fold_body(one, two, three, four, out):
    out[...] = total_of((one, two, three, four), slice(None)).astype(BF)


def fold(parts):
    return pl.pallas_call(
        fold_body,
        name="fold",
        out_shape=jax.ShapeDtypeStruct(parts[0].shape, BF),
        compiler_params=params(8),
        cost_estimate=cost(4 * parts[0].size, 10 * parts[0].size),
    )(*parts)


def top_body(one, two, three, four, base, top, diag_a, top_b, sent):
    got = (one, two, three, four)
    value = base[...] - total_of(got, slice(0, PART))
    diag_a[...] = value
    total = total_of(got, slice(PART, 2 * PART))
    for _ in range(3):
        part = value.astype(BF)
        value = value - part.astype(F32)
        total = total + jnp.dot(part, top[...], preferred_element_type=F32)
    total = (-total).astype(BF)
    top_b[...] = total
    for c in range(COLS):
        sent[c] = jnp.concatenate([total[:, c * PART : (c + 1) * PART]] * 2, axis=1)


def top_part(got, base_a, factor_top):
    return pl.pallas_call(
        top_body,
        name="top_part",
        out_shape=[
            jax.ShapeDtypeStruct((PART, W), F32),
            jax.ShapeDtypeStruct((PART, W), BF),
            jax.ShapeDtypeStruct((COLS, PART, 2 * PART), BF),
        ],
        compiler_params=params(8),
        cost_estimate=cost(6 * PART * W * W, 2 * W * W),
    )(*got, base_a, factor_top)


def last_body(one, two, three, four, base, taken, top, diag_b):
    across = taken[...].reshape(W, 2 * PART)
    cross = lax.dot_general(
        across, top[...], (((0,), (0,)), ((), ())), preferred_element_type=F32
    )
    total = total_of((one, two, three, four), slice(2 * PART, 3 * PART))
    diag_b[...] = base[...] - total - cross[:PART]


def last_part(got, base_b, taken, factor_top):
    return pl.pallas_call(
        last_body,
        name="last_part",
        out_shape=jax.ShapeDtypeStruct((PART, W), F32),
        compiler_params=params(8),
        cost_estimate=cost(4 * PART * W * W, 2 * W * W),
    )(*got, base_b, taken, factor_top)


def send(value, **by):
    return lax.ppermute(value, BOTH, shifted(**by))


def around(value, axis):
    return [value] + [send(value, **{axis: step}) for step in STEPS[1:]]


def on_device(
    trailing, rows_a, counts_a, factor_a, rows_b, counts_b, factor_b, factor_top, base_a, base_b
):
    place = jnp.stack([lax.axis_index("row"), lax.axis_index("col")]).astype(jnp.int32)
    lists = (rows_a, counts_a, rows_b, counts_b)
    part_a, part_b = prep(place, lists, factor_a, factor_b, factor_top)
    part_a = lax.ppermute(part_a, BOTH, spread_pairs())
    part_b = lax.ppermute(part_b, BOTH, spread_pairs())
    a_own = jnp.stack(around(part_a, "dy"))
    b_own = jnp.stack(around(part_b, "dz"))
    a_down, a_up = send(a_own, dz=1), send(a_own, dz=-1)
    b_down, b_up = send(b_own, dy=1), send(b_own, dy=-1)
    a_far, a_far_more = send(a_down[:2], dz=1), send(a_up[2:], dz=-1)
    b_far, b_far_more = send(b_down[:2], dy=1), send(b_up[2:], dy=-1)
    before = early_product(place, (a_down, a_up, b_own, b_down, b_up), trailing)
    keep, give = late_product(
        place, (a_own, a_far, a_far_more, b_far, b_far_more), trailing, before
    )

    own, one, two, three = pair_sum(place, keep, send(give, dc=1))
    slabs = [own, send(one, dx=1), send(two, dx=2), send(three, dx=-1)]
    columns, pieces = slots(place, lists, slabs, (factor_a, factor_b))
    got = around(fold(around(pieces, "dy")), "dz")
    mine = around(columns, "dx")
    column_a, column_b = whole_columns(place, mine + [send(slab, dc=1) for slab in mine])
    diag_a, top_b, sent = top_part(got, base_a, factor_top)
    taken = lax.all_to_all(sent, "col", 0, 0)
    diag_b = last_part(got, base_b, taken, factor_top)
    return (column_a, diag_a, column_b, top_b, diag_b)


def solution(mesh):
    in_specs = (
        P("row", "col"),
        P(),
        P(),
        P("row", None),
        P(),
        P(),
        P("row", None),
        P(),
        P("col", None),
        P("col", None),
    )
    out_specs = (P("row", None), P("col", None), P("row", None), P("col", None), P("col", None))
    return jax.shard_map(
        on_device, mesh=mesh, in_specs=in_specs, out_specs=out_specs, check_vma=False
    )
```

```python
import functools

import jax
import jax.numpy as jnp
from jax import lax
from jax.experimental import pallas as pl
from jax.experimental.pallas import tpu as pltpu
from jax.sharding import PartitionSpec as P

BS = 128
W = 512
NB = 12
ROWS = NB * BS
SIDE = 4
PART = 64
COLS = 8
STEPS = (0, 1, -1, 2)
STRIP = 2 * BS
PAIR = 2 * PART
BOTH = ("row", "col")
MIB = 1024 * 1024
BF = jnp.bfloat16
F32 = jnp.float32


def device(z, y, x, core):
    return ((z % SIDE) * SIDE + y % SIDE) * 8 + (x % SIDE) * 2 + core % 2


def all_places():
    return [
        (z, y, x, core)
        for z in range(SIDE)
        for y in range(SIDE)
        for x in range(SIDE)
        for core in range(2)
    ]


def shifted(dz=0, dy=0, dx=0, dc=0):
    return [
        (device(z, y, x, c), device(z + dz, y + dy, x + dx, c + dc))
        for z, y, x, c in all_places()
    ]


def spread_pairs():
    pairs = []
    for z, y, x, core in all_places():
        plane = (z * SIDE + y) % 8
        to = device(z + core, y + x, plane // 2, plane % 2)
        pairs.append((device(z, y, x, core), to))
    return pairs


def params(mib=24, **more):
    return pltpu.CompilerParams(vmem_limit_bytes=mib * MIB, **more)


def cost(flops, moved):
    return pl.CostEstimate(flops=flops, bytes_accessed=moved, transcendentals=0)


def whole(shape):
    return pl.BlockSpec(shape, lambda *_: (0,) * len(shape))


def find_slot(rows, counts, owner, block):
    slot = jnp.int32(0)
    live = jnp.int32(0)
    for k in range(NB):
        hit = (rows[owner, k] == block) & (k < counts[owner])
        slot = jnp.where(hit, k, slot)
        live = jnp.where(hit, 1, live)
    return slot, live


def prep_body(place, rows_a, counts_a, rows_b, counts_b, fa, part_a, part_b, top, out_a, out_b, fix):
    owner = place[0]
    upper = place[1] % 2
    fix[...] = lax.dot_general(
        top[...], fa[...], (((0,), (1,)), ((), ())), preferred_element_type=F32
    )

    def half(value):
        return jnp.where(upper > 0, value[PART:], value[:PART])

    for block in range(NB):
        slot_a, live_a = find_slot(rows_a, counts_a, owner, block)
        slot_b, live_b = find_slot(rows_b, counts_b, owner, block)
        at_a = pl.ds(pl.multiple_of(slot_a * BS, BS), BS)
        at_b = pl.ds(pl.multiple_of(slot_b * BS, BS), BS)
        piece = half(part_a[at_a, :].T)
        out_a[block] = jnp.where(live_a > 0, piece, jnp.zeros_like(piece))
        moved = half(fix[:, at_a])
        piece = half(part_b[at_b, :].T).astype(F32)
        piece = jnp.where(live_b > 0, piece, jnp.zeros_like(piece))
        out_b[block] = (piece - jnp.where(live_a > 0, moved, jnp.zeros_like(moved))).astype(BF)


def prep(place, lists, factor_a, factor_b, factor_top):
    slice_spec = pl.BlockSpec((ROWS, BS), lambda i, place, *_: (0, place[1] // 2))
    out = jax.ShapeDtypeStruct((NB, PART, BS), BF)
    return pl.pallas_call(
        prep_body,
        name="prep",
        grid_spec=pltpu.PrefetchScalarGridSpec(
            num_scalar_prefetch=5,
            grid=(1,),
            in_specs=[
                whole((ROWS, W)),
                slice_spec,
                slice_spec,
                pl.BlockSpec((W, BS), lambda i, place, *_: (0, place[1] // 2)),
            ],
            out_specs=[whole((NB, PART, BS))] * 2,
            scratch_shapes=[pltpu.VMEM((BS, ROWS), F32)],
        ),
        out_shape=[out, out],
        compiler_params=params(56),
        cost_estimate=cost(2 * BS * ROWS * W, 2 * ROWS * (W + 4 * BS)),
    )(place, *lists, factor_a, factor_a, factor_b, factor_top)


def where(place):
    z, y, plane = place[0] // SIDE, place[0] % SIDE, place[1]
    u = (z - plane // SIDE + SIDE) % SIDE
    v = (y - plane % SIDE + SIDE) % SIDE
    return u, v


def turn(value, by):
    return (value + by + SIDE) % SIDE


def load_a(copies, buf, picks, u, spread, sems):
    for i, member in picks:
        copies.append((buf.at[member], spread.at[:, u // 2, i * PART : (i + 1) * PART, :]))


def load_b(copies, buf, picks, u, first, spread, sems):
    for i, member in picks:
        ui = turn(u, -STEPS[i])
        at = pl.ds(pl.multiple_of(first + (ui % 2) * PART, PART), PART)
        copies.append((buf.at[member], spread.at[:, ui // 2, at, :]))


def run_copies(copies, sems):
    started = [pltpu.make_async_copy(a, b, sems.at[i]) for i, (a, b) in enumerate(copies)]
    for copy in started:
        copy.start()
    for copy in started:
        copy.wait()


def multiply(spread, tile):
    left = jnp.concatenate([spread[n, h] for n in range(NB) for h in range(2)], axis=1)
    return lax.dot_general(
        left, tile, (((1,), (1,)), ((), ())), preferred_element_type=F32
    ).astype(BF)


def hold_body(source, _, target, sem):
    copy = pltpu.make_async_copy(source, target, sem)
    copy.start()
    copy.wait()


def hold(trailing, after):
    return pl.pallas_call(
        hold_body,
        name="hold",
        in_specs=[pl.BlockSpec(memory_space=pltpu.HBM), pl.BlockSpec(memory_space=pl.ANY)],
        out_specs=pl.BlockSpec(memory_space=pltpu.VMEM),
        out_shape=pltpu.VMEM(trailing.shape, BF),
        scratch_shapes=[pltpu.SemaphoreType.DMA],
        compiler_params=params(8),
        cost_estimate=cost(0, 2 * trailing.size),
    )(trailing, after)


def rows_of(tile, step):
    return tile[pl.ds(pl.multiple_of(step * STRIP, STRIP), STRIP), :]


ALL = tuple((i, i) for i in range(SIDE))
FIRST = ((0, 0), (1, 1))
LAST = ((2, 0), (3, 1))


def early_body(place, a_down, a_up, b_own, b_down, b_up, tile, out, spread, sems):
    u, v = where(place)

    @pl.when(pl.program_id(0) == 0)
    def _():
        copies = []
        load_a(copies, a_down, ALL, turn(u, -1), spread, sems)
        load_a(copies, a_up, ALL, turn(u, 1), spread, sems)
        for t, buf in enumerate((b_own, b_down, b_up)):
            load_b(copies, buf, ALL, u, W // 2 + 2 * t * PART, spread, sems)
        run_copies(copies, sems)

    value = multiply(spread, rows_of(tile, pl.program_id(0)))
    for i, step in enumerate(STEPS):
        out[2 * turn(v, -step) + (u + 1) % 2, :PART, :] = value[i * PART : (i + 1) * PART]
    for j in range(6):
        to = 2 * turn(v, -STEPS[j // 2]) + j % 2
        out[to, PART:, :] = value[W // 2 + j * PART : W // 2 + (j + 1) * PART]


def early_product(place, bufs, trailing):
    deep = trailing.shape[1]
    rows = W // 2 + 6 * PART
    return pl.pallas_call(
        early_body,
        name="early_product",
        grid_spec=pltpu.PrefetchScalarGridSpec(
            num_scalar_prefetch=1,
            grid=(ROWS // STRIP,),
            in_specs=[pl.BlockSpec(memory_space=pl.ANY)] * 5
            + [pl.BlockSpec(memory_space=pltpu.VMEM)],
            out_specs=pl.BlockSpec((COLS, PAIR, STRIP), lambda i, *_: (0, 0, i)),
            scratch_shapes=[
                pltpu.VMEM((NB, 2, rows, BS), BF),
                pltpu.SemaphoreType.DMA((20,)),
            ],
        ),
        out_shape=jax.ShapeDtypeStruct((COLS, PAIR, ROWS), BF),
        compiler_params=params(20, dimension_semantics=("arbitrary",)),
        cost_estimate=cost(2 * rows * ROWS * deep, 2 * rows * deep + 4 * W * ROWS),
    )(place, *bufs, trailing)


def late_body(
    half, place, a_own, a_far, a_far_more, b_far, b_far_more, tile, before, keep, give, spread, ready, sems
):
    u, v = where(place)
    core = place[1] % 2

    @pl.when(pl.program_id(0) == 0)
    def _():
        copies = []
        load_a(copies, a_own, ALL, u, spread, sems)
        load_a(copies, a_far, FIRST, turn(u, 2), spread, sems)
        load_a(copies, a_far_more, LAST, turn(u, 2), spread, sems)
        load_b(copies, b_far, FIRST, u, W // 2, spread, sems)
        load_b(copies, b_far_more, LAST, u, W // 2, spread, sems)
        run_copies(copies, sems)

    ready[...] = before[...]
    value = multiply(spread, rows_of(tile, half * HALF_STEPS + pl.program_id(0)))
    for i, step in enumerate(STEPS):
        ready[2 * turn(v, -step) + u % 2, :PART, :] = value[i * PART : (i + 1) * PART]
    for j in range(2):
        ready[2 * turn(v, 2) + j, PART:, :] = value[W // 2 + j * PART : W // 2 + (j + 1) * PART]
    for x in range(SIDE):
        keep[x] = ready[2 * x + core]
        give[x] = ready[2 * x + 1 - core]


HALF_STEPS = ROWS // STRIP // 2


def late_product(half, place, bufs, trailing, before):
    deep = trailing.shape[1]
    rows = W // 2 + 2 * PART
    out = jax.ShapeDtypeStruct((SIDE, PAIR, ROWS // 2), BF)
    spec = pl.BlockSpec((SIDE, PAIR, STRIP), lambda i, *_: (0, 0, i))
    return pl.pallas_call(
        functools.partial(late_body, half),
        name="late_product",
        grid_spec=pltpu.PrefetchScalarGridSpec(
            num_scalar_prefetch=1,
            grid=(HALF_STEPS,),
            in_specs=[pl.BlockSpec(memory_space=pl.ANY)] * 5
            + [
                pl.BlockSpec(memory_space=pltpu.VMEM),
                pl.BlockSpec((COLS, PAIR, STRIP), lambda i, *_: (0, 0, half * HALF_STEPS + i)),
            ],
            out_specs=[spec, spec],
            scratch_shapes=[
                pltpu.VMEM((NB, 2, rows, BS), BF),
                pltpu.VMEM((COLS, PAIR, STRIP), BF),
                pltpu.SemaphoreType.DMA((12,)),
            ],
        ),
        out_shape=[out, out],
        compiler_params=params(20, dimension_semantics=("arbitrary",)),
        cost_estimate=cost(rows * ROWS * deep, 2 * rows * deep + 4 * W * ROWS),
    )(place, *bufs, trailing, before)


def pair_body(place, mine, taken, *outs):
    x = place[1] // 2
    for i in range(SIDE):
        at = (x + i) % SIDE
        outs[i][...] = (mine[at].astype(F32) + taken[at].astype(F32)).astype(BF)


def pair_sum(place, mine, taken):
    lanes = 3 * BS
    width = mine.shape[2]
    spec = pl.BlockSpec((SIDE, PAIR, lanes), lambda i, *_: (0, 0, i))
    return pl.pallas_call(
        pair_body,
        name="pair_sum",
        grid_spec=pltpu.PrefetchScalarGridSpec(
            num_scalar_prefetch=1,
            grid=(width // lanes,),
            in_specs=[spec, spec],
            out_specs=[pl.BlockSpec((PAIR, lanes), lambda i, *_: (0, i))] * SIDE,
        ),
        out_shape=[jax.ShapeDtypeStruct((PAIR, width), BF)] * SIDE,
        compiler_params=params(dimension_semantics=("arbitrary",)),
        cost_estimate=cost(W * width, 6 * W * width),
    )(place, mine, taken)


def slots_body(
    place, rows_a, counts_a, rows_b, counts_b, *refs
):
    slabs, (fa, fb, columns, pieces, natural, left) = refs[:8], refs[8:]
    owner = place[0]
    width = ROWS // 2
    for half in range(2):
        total = total_of(slabs[half * SIDE : (half + 1) * SIDE], slice(None))
        natural[:, half * width : (half + 1) * width] = (-total).astype(BF)
    for k in range(NB):
        at = slice(k * BS, (k + 1) * BS)
        block = natural[:PART, pl.ds(pl.multiple_of(rows_a[owner, k] * BS, BS), BS)]
        columns[:PART, at] = jnp.where(k < counts_a[owner], block, jnp.zeros_like(block))
        block = natural[:, pl.ds(pl.multiple_of(rows_b[owner, k] * BS, BS), BS)]
        block = jnp.where(k < counts_b[owner], block, jnp.zeros_like(block))
        left[:, at] = block
        columns[PART:, at] = block[PART:]
    one = jnp.dot(columns[:PART, :], fa[...], preferred_element_type=F32)
    two = jnp.dot(left[...], fb[...], preferred_element_type=F32)
    pieces[:PART, :] = one.astype(BF)
    pieces[PART:, :] = two.astype(BF)


def slots(place, lists, slabs, factors):
    return pl.pallas_call(
        slots_body,
        name="slots",
        grid_spec=pltpu.PrefetchScalarGridSpec(
            num_scalar_prefetch=5,
            grid=(1,),
            in_specs=[whole((PAIR, ROWS // 2))] * 8 + [whole((ROWS, W))] * 2,
            out_specs=[whole((PAIR, ROWS)), whole((3 * PART, W))],
            scratch_shapes=[pltpu.VMEM((PAIR, ROWS), BF)] * 2,
        ),
        out_shape=[
            jax.ShapeDtypeStruct((PAIR, ROWS), BF),
            jax.ShapeDtypeStruct((3 * PART, W), BF),
        ],
        compiler_params=params(),
        cost_estimate=cost(6 * PART * ROWS * W, 4 * ROWS * W + 10 * PAIR * ROWS),
    )(place, *lists, *slabs, *factors)


def column_body(place, *refs):
    slabs, column_a, column_b, wide = refs[:8], refs[8], refs[9], refs[10]
    core, x = place[1] % 2, place[1] // 2
    for i in range(8):
        at = 2 * turn(x, -STEPS[i % SIDE]) + (core if i < SIDE else 1 - core)
        wide[at] = slabs[i][...]
    for first, out in ((0, column_a), (PART, column_b)):
        out[...] = wide[:, first : first + PART, :].reshape(W, wide.shape[2]).T


def whole_columns(place, slabs):
    lanes = 2 * BS
    out = jax.ShapeDtypeStruct((ROWS, W), BF)
    return pl.pallas_call(
        column_body,
        name="whole_columns",
        grid_spec=pltpu.PrefetchScalarGridSpec(
            num_scalar_prefetch=1,
            grid=(ROWS // lanes,),
            in_specs=[pl.BlockSpec((PAIR, lanes), lambda i, *_: (0, i))] * 8,
            out_specs=[pl.BlockSpec((lanes, W), lambda i, *_: (i, 0))] * 2,
            scratch_shapes=[pltpu.VMEM((COLS, PAIR, lanes), BF)],
        ),
        out_shape=[out, out],
        compiler_params=params(dimension_semantics=("arbitrary",)),
        cost_estimate=cost(0, 8 * ROWS * W),
    )(place, *slabs)


def total_of(refs, rows):
    parts = [ref[rows, :].astype(F32) for ref in refs]
    return (parts[0] + parts[1]) + (parts[2] + parts[3])


def fold_body(one, two, three, four, out):
    out[...] = total_of((one, two, three, four), slice(None)).astype(BF)


def fold(parts):
    return pl.pallas_call(
        fold_body,
        name="fold",
        out_shape=jax.ShapeDtypeStruct(parts[0].shape, BF),
        compiler_params=params(8),
        cost_estimate=cost(4 * parts[0].size, 10 * parts[0].size),
    )(*parts)


def top_body(one, two, three, four, base, top, diag_a, top_b, sent):
    got = (one, two, three, four)
    value = base[...] - total_of(got, slice(0, PART))
    diag_a[...] = value
    total = total_of(got, slice(PART, 2 * PART))
    for _ in range(3):
        part = value.astype(BF)
        value = value - part.astype(F32)
        total = total + jnp.dot(part, top[...], preferred_element_type=F32)
    total = (-total).astype(BF)
    top_b[...] = total
    for c in range(COLS):
        sent[c] = jnp.concatenate([total[:, c * PART : (c + 1) * PART]] * 2, axis=1)


def top_part(got, base_a, factor_top):
    return pl.pallas_call(
        top_body,
        name="top_part",
        out_shape=[
            jax.ShapeDtypeStruct((PART, W), F32),
            jax.ShapeDtypeStruct((PART, W), BF),
            jax.ShapeDtypeStruct((COLS, PART, 2 * PART), BF),
        ],
        compiler_params=params(8),
        cost_estimate=cost(6 * PART * W * W, 2 * W * W),
    )(*got, base_a, factor_top)


def last_body(one, two, three, four, base, taken, top, diag_b):
    across = taken[...].reshape(W, 2 * PART)
    cross = lax.dot_general(
        across, top[...], (((0,), (0,)), ((), ())), preferred_element_type=F32
    )
    total = total_of((one, two, three, four), slice(2 * PART, 3 * PART))
    diag_b[...] = base[...] - total - cross[:PART]


def last_part(got, base_b, taken, factor_top):
    return pl.pallas_call(
        last_body,
        name="last_part",
        out_shape=jax.ShapeDtypeStruct((PART, W), F32),
        compiler_params=params(8),
        cost_estimate=cost(4 * PART * W * W, 2 * W * W),
    )(*got, base_b, taken, factor_top)


def send(value, **by):
    return lax.ppermute(value, BOTH, shifted(**by))


def around(value, axis):
    return [value] + [send(value, **{axis: step}) for step in STEPS[1:]]


def on_device(
    trailing, rows_a, counts_a, factor_a, rows_b, counts_b, factor_b, factor_top, base_a, base_b
):
    place = jnp.stack([lax.axis_index("row"), lax.axis_index("col")]).astype(jnp.int32)
    lists = (rows_a, counts_a, rows_b, counts_b)
    part_a, part_b = prep(place, lists, factor_a, factor_b, factor_top)
    part_a = lax.ppermute(part_a, BOTH, spread_pairs())
    part_b = lax.ppermute(part_b, BOTH, spread_pairs())
    a_own = jnp.stack(around(part_a, "dy"))
    b_own = jnp.stack(around(part_b, "dz"))
    a_down, a_up = send(a_own, dz=1), send(a_own, dz=-1)
    b_down, b_up = send(b_own, dy=1), send(b_own, dy=-1)
    a_far, a_far_more = send(a_down[:2], dz=1), send(a_up[2:], dz=-1)
    b_far, b_far_more = send(b_down[:2], dy=1), send(b_up[2:], dy=-1)
    trailing = hold(trailing, a_own)
    before = early_product(place, (a_down, a_up, b_own, b_down, b_up), trailing)
    slabs = []
    for half in range(2):
        keep, give = late_product(
            half, place, (a_own, a_far, a_far_more, b_far, b_far_more), trailing, before
        )
        own, one, two, three = pair_sum(place, keep, send(give, dc=1))
        slabs += [own, send(one, dx=1), send(two, dx=2), send(three, dx=-1)]
    columns, pieces = slots(place, lists, slabs, (factor_a, factor_b))
    near, other = send(columns, dx=1), send(columns, dx=-1)
    folded = fold(around(pieces, "dy"))
    got = around(folded, "dz")
    own, near, other, got[1] = lax.optimization_barrier((columns, near, other, got[1]))
    mine = [own, near, other, send(own, dx=2)]
    column_a, column_b = whole_columns(place, mine + [send(slab, dc=1) for slab in mine])
    diag_a, top_b, sent = top_part(got, base_a, factor_top)
    taken = lax.all_to_all(sent, "col", 0, 0)
    diag_b = last_part(got, base_b, taken, factor_top)
    return (column_a, diag_a, column_b, top_b, diag_b)


def solution(mesh):
    in_specs = (
        P("row", "col"),
        P(),
        P(),
        P("row", None),
        P(),
        P(),
        P("row", None),
        P(),
        P("col", None),
        P("col", None),
    )
    out_specs = (P("row", None), P("col", None), P("row", None), P("col", None), P("col", None))
    return jax.shard_map(
        on_device, mesh=mesh, in_specs=in_specs, out_specs=out_specs, check_vma=False
    )
```

```python
import functools

import jax
import jax.numpy as jnp
from jax import lax
from jax.experimental import pallas as pl
from jax.experimental.pallas import tpu as pltpu
from jax.sharding import PartitionSpec as P

BS = 128
W = 512
NB = 12
ROWS = NB * BS
SIDE = 4
PART = 64
COLS = 8
STEPS = (0, 1, -1, 2)
STRIP = 2 * BS
PAIR = 2 * PART
BOTH = ("row", "col")
MIB = 1024 * 1024
BF = jnp.bfloat16
F32 = jnp.float32


def device(z, y, x, core):
    return ((z % SIDE) * SIDE + y % SIDE) * 8 + (x % SIDE) * 2 + core % 2


def all_places():
    return [
        (z, y, x, core)
        for z in range(SIDE)
        for y in range(SIDE)
        for x in range(SIDE)
        for core in range(2)
    ]


def shifted(dz=0, dy=0, dx=0, dc=0):
    return [
        (device(z, y, x, c), device(z + dz, y + dy, x + dx, c + dc))
        for z, y, x, c in all_places()
    ]


def spread_pairs():
    pairs = []
    for z, y, x, core in all_places():
        plane = (z * SIDE + y) % 8
        to = device(z + core, y + x, plane // 2, plane % 2)
        pairs.append((device(z, y, x, core), to))
    return pairs


def params(mib=24, **more):
    return pltpu.CompilerParams(vmem_limit_bytes=mib * MIB, **more)


def cost(flops, moved):
    return pl.CostEstimate(flops=flops, bytes_accessed=moved, transcendentals=0)


def whole(shape):
    return pl.BlockSpec(shape, lambda *_: (0,) * len(shape))


def find_slot(rows, counts, owner, block):
    slot = jnp.int32(0)
    live = jnp.int32(0)
    for k in range(NB):
        hit = (rows[owner, k] == block) & (k < counts[owner])
        slot = jnp.where(hit, k, slot)
        live = jnp.where(hit, 1, live)
    return slot, live


def prep_body(place, rows_a, counts_a, rows_b, counts_b, fa, part_a, part_b, top, out_a, out_b, fix):
    owner = place[0]
    upper = place[1] % 2
    fix[...] = lax.dot_general(
        top[...], fa[...], (((0,), (1,)), ((), ())), preferred_element_type=F32
    )

    def half(value):
        return jnp.where(upper > 0, value[PART:], value[:PART])

    for block in range(NB):
        slot_a, live_a = find_slot(rows_a, counts_a, owner, block)
        slot_b, live_b = find_slot(rows_b, counts_b, owner, block)
        at_a = pl.ds(pl.multiple_of(slot_a * BS, BS), BS)
        at_b = pl.ds(pl.multiple_of(slot_b * BS, BS), BS)
        piece = half(part_a[at_a, :].T)
        out_a[block] = jnp.where(live_a > 0, piece, jnp.zeros_like(piece))
        moved = half(fix[:, at_a])
        piece = half(part_b[at_b, :].T).astype(F32)
        piece = jnp.where(live_b > 0, piece, jnp.zeros_like(piece))
        out_b[block] = (piece - jnp.where(live_a > 0, moved, jnp.zeros_like(moved))).astype(BF)


def prep(place, lists, factor_a, factor_b, factor_top):
    slice_spec = pl.BlockSpec((ROWS, BS), lambda i, place, *_: (0, place[1] // 2))
    out = jax.ShapeDtypeStruct((NB, PART, BS), BF)
    return pl.pallas_call(
        prep_body,
        name="prep",
        grid_spec=pltpu.PrefetchScalarGridSpec(
            num_scalar_prefetch=5,
            grid=(1,),
            in_specs=[
                whole((ROWS, W)),
                slice_spec,
                slice_spec,
                pl.BlockSpec((W, BS), lambda i, place, *_: (0, place[1] // 2)),
            ],
            out_specs=[whole((NB, PART, BS))] * 2,
            scratch_shapes=[pltpu.VMEM((BS, ROWS), F32)],
        ),
        out_shape=[out, out],
        compiler_params=params(56),
        cost_estimate=cost(2 * BS * ROWS * W, 2 * ROWS * (W + 4 * BS)),
    )(place, *lists, factor_a, factor_a, factor_b, factor_top)


def where(place):
    z, y, plane = place[0] // SIDE, place[0] % SIDE, place[1]
    u = (z - plane // SIDE + SIDE) % SIDE
    v = (y - plane % SIDE + SIDE) % SIDE
    return u, v


def turn(value, by):
    return (value + by + SIDE) % SIDE


def load_a(copies, buf, u, spread):
    for i in range(SIDE):
        copies.append((buf.at[i], spread.at[:, u // 2, i * PART : (i + 1) * PART, :]))


def load_b(copies, buf, u, first, spread):
    for i in range(SIDE):
        ui = turn(u, -STEPS[i])
        at = pl.ds(pl.multiple_of(first + (ui % 2) * PART, PART), PART)
        copies.append((buf.at[i], spread.at[:, ui // 2, at, :]))


def run_copies(copies, sems):
    started = [pltpu.make_async_copy(a, b, sems.at[i]) for i, (a, b) in enumerate(copies)]
    for copy in started:
        copy.start()
    for copy in started:
        copy.wait()


def multiply(spread, tile):
    left = jnp.concatenate([spread[n, h] for n in range(NB) for h in range(2)], axis=1)
    return lax.dot_general(
        left, tile, (((1,), (1,)), ((), ())), preferred_element_type=F32
    ).astype(BF)


def hold_body(source, _, target, sem):
    copy = pltpu.make_async_copy(source, target, sem)
    copy.start()
    copy.wait()


def hold(trailing, after):
    return pl.pallas_call(
        hold_body,
        name="hold",
        in_specs=[pl.BlockSpec(memory_space=pltpu.HBM), pl.BlockSpec(memory_space=pl.ANY)],
        out_specs=pl.BlockSpec(memory_space=pltpu.VMEM),
        out_shape=pltpu.VMEM(trailing.shape, BF),
        scratch_shapes=[pltpu.SemaphoreType.DMA],
        compiler_params=params(8),
        cost_estimate=cost(0, 2 * trailing.size),
    )(trailing, after)


def rows_of(tile, step):
    return tile[pl.ds(pl.multiple_of(step * STRIP, STRIP), STRIP), :]


def early_body(place, a_down, a_up, b_own, b_down, b_up, tile, out, spread, sems):
    u, v = where(place)

    @pl.when(pl.program_id(0) == 0)
    def _():
        copies = []
        load_a(copies, a_down, turn(u, -1), spread)
        load_a(copies, a_up, turn(u, 1), spread)
        for t, buf in enumerate((b_own, b_down, b_up)):
            load_b(copies, buf, u, W // 2 + 2 * t * PART, spread)
        run_copies(copies, sems)

    value = multiply(spread, rows_of(tile, pl.program_id(0)))
    for i, step in enumerate(STEPS):
        out[2 * turn(v, -step) + (u + 1) % 2, :PART, :] = value[i * PART : (i + 1) * PART]
    for j in range(6):
        to = 2 * turn(v, -STEPS[j // 2]) + j % 2
        out[to, PART:, :] = value[W // 2 + j * PART : W // 2 + (j + 1) * PART]


def early_product(place, bufs, trailing):
    deep = trailing.shape[1]
    rows = W // 2 + 6 * PART
    return pl.pallas_call(
        early_body,
        name="early_product",
        grid_spec=pltpu.PrefetchScalarGridSpec(
            num_scalar_prefetch=1,
            grid=(ROWS // STRIP,),
            in_specs=[pl.BlockSpec(memory_space=pl.ANY)] * 5
            + [pl.BlockSpec(memory_space=pltpu.VMEM)],
            out_specs=pl.BlockSpec((COLS, PAIR, STRIP), lambda i, *_: (0, 0, i)),
            scratch_shapes=[
                pltpu.VMEM((NB, 2, rows, BS), BF),
                pltpu.SemaphoreType.DMA((20,)),
            ],
        ),
        out_shape=jax.ShapeDtypeStruct((COLS, PAIR, ROWS), BF),
        compiler_params=params(20, dimension_semantics=("arbitrary",)),
        cost_estimate=cost(2 * rows * ROWS * deep, 2 * rows * deep + 4 * W * ROWS),
    )(place, *bufs, trailing)


def late_body(
    half, place, a_own, a_far, b_far, tile, before, keep, give, spread, ready, sems
):
    u, v = where(place)
    core = place[1] % 2

    @pl.when(pl.program_id(0) == 0)
    def _():
        copies = []
        load_a(copies, a_own, u, spread)
        load_a(copies, a_far, turn(u, 2), spread)
        load_b(copies, b_far, u, W // 2, spread)
        run_copies(copies, sems)

    ready[...] = before[...]
    value = multiply(spread, rows_of(tile, half * HALF_STEPS + pl.program_id(0)))
    for i, step in enumerate(STEPS):
        ready[2 * turn(v, -step) + u % 2, :PART, :] = value[i * PART : (i + 1) * PART]
    for j in range(2):
        ready[2 * turn(v, 2) + j, PART:, :] = value[W // 2 + j * PART : W // 2 + (j + 1) * PART]
    for x in range(SIDE):
        keep[x] = ready[2 * x + core]
        give[x] = ready[2 * x + 1 - core]


HALF_STEPS = ROWS // STRIP // 2


def late_product(half, place, bufs, trailing, before):
    deep = trailing.shape[1]
    rows = W // 2 + 2 * PART
    out = jax.ShapeDtypeStruct((SIDE, PAIR, ROWS // 2), BF)
    spec = pl.BlockSpec((SIDE, PAIR, STRIP), lambda i, *_: (0, 0, i))
    return pl.pallas_call(
        functools.partial(late_body, half),
        name="late_product",
        grid_spec=pltpu.PrefetchScalarGridSpec(
            num_scalar_prefetch=1,
            grid=(HALF_STEPS,),
            in_specs=[pl.BlockSpec(memory_space=pl.ANY)] * 3
            + [
                pl.BlockSpec(memory_space=pltpu.VMEM),
                pl.BlockSpec((COLS, PAIR, STRIP), lambda i, *_: (0, 0, half * HALF_STEPS + i)),
            ],
            out_specs=[spec, spec],
            scratch_shapes=[
                pltpu.VMEM((NB, 2, rows, BS), BF),
                pltpu.VMEM((COLS, PAIR, STRIP), BF),
                pltpu.SemaphoreType.DMA((12,)),
            ],
        ),
        out_shape=[out, out],
        compiler_params=params(20, dimension_semantics=("arbitrary",)),
        cost_estimate=cost(rows * ROWS * deep, 2 * rows * deep + 4 * W * ROWS),
    )(place, *bufs, trailing, before)


def pair_body(place, mine, taken, *outs):
    x = place[1] // 2
    for i in range(SIDE):
        at = (x + i) % SIDE
        outs[i][...] = (mine[at].astype(F32) + taken[at].astype(F32)).astype(BF)


def pair_sum(place, mine, taken):
    lanes = 3 * BS
    width = mine.shape[2]
    spec = pl.BlockSpec((SIDE, PAIR, lanes), lambda i, *_: (0, 0, i))
    return pl.pallas_call(
        pair_body,
        name="pair_sum",
        grid_spec=pltpu.PrefetchScalarGridSpec(
            num_scalar_prefetch=1,
            grid=(width // lanes,),
            in_specs=[spec, spec],
            out_specs=[pl.BlockSpec((PAIR, lanes), lambda i, *_: (0, i))] * SIDE,
        ),
        out_shape=[jax.ShapeDtypeStruct((PAIR, width), BF)] * SIDE,
        compiler_params=params(dimension_semantics=("arbitrary",)),
        cost_estimate=cost(W * width, 6 * W * width),
    )(place, mine, taken)


def slots_body(
    place, rows_a, counts_a, rows_b, counts_b, *refs
):
    slabs, (fa, fb, columns, pieces, natural, left) = refs[:8], refs[8:]
    owner = place[0]
    width = ROWS // 2
    for half in range(2):
        total = total_of(slabs[half * SIDE : (half + 1) * SIDE], slice(None))
        natural[:, half * width : (half + 1) * width] = (-total).astype(BF)
    for k in range(NB):
        at = slice(k * BS, (k + 1) * BS)
        block = natural[:PART, pl.ds(pl.multiple_of(rows_a[owner, k] * BS, BS), BS)]
        columns[:PART, at] = jnp.where(k < counts_a[owner], block, jnp.zeros_like(block))
        block = natural[:, pl.ds(pl.multiple_of(rows_b[owner, k] * BS, BS), BS)]
        block = jnp.where(k < counts_b[owner], block, jnp.zeros_like(block))
        left[:, at] = block
        columns[PART:, at] = block[PART:]
    one = jnp.dot(columns[:PART, :], fa[...], preferred_element_type=F32)
    two = jnp.dot(left[...], fb[...], preferred_element_type=F32)
    pieces[:PART, :] = one.astype(BF)
    pieces[PART:, :] = two.astype(BF)


def slots(place, lists, slabs, factors):
    return pl.pallas_call(
        slots_body,
        name="slots",
        grid_spec=pltpu.PrefetchScalarGridSpec(
            num_scalar_prefetch=5,
            grid=(1,),
            in_specs=[whole((PAIR, ROWS // 2))] * 8 + [whole((ROWS, W))] * 2,
            out_specs=[whole((PAIR, ROWS)), whole((3 * PART, W))],
            scratch_shapes=[pltpu.VMEM((PAIR, ROWS), BF)] * 2,
        ),
        out_shape=[
            jax.ShapeDtypeStruct((PAIR, ROWS), BF),
            jax.ShapeDtypeStruct((3 * PART, W), BF),
        ],
        compiler_params=params(),
        cost_estimate=cost(6 * PART * ROWS * W, 4 * ROWS * W + 10 * PAIR * ROWS),
    )(place, *lists, *slabs, *factors)


def column_body(place, *refs):
    slabs, column_a, column_b, wide = refs[:8], refs[8], refs[9], refs[10]
    core, x = place[1] % 2, place[1] // 2
    for i in range(8):
        at = 2 * turn(x, -STEPS[i % SIDE]) + (core if i < SIDE else 1 - core)
        wide[at] = slabs[i][...]
    for first, out in ((0, column_a), (PART, column_b)):
        out[...] = wide[:, first : first + PART, :].reshape(W, wide.shape[2]).T


def whole_columns(place, slabs):
    lanes = 2 * BS
    out = jax.ShapeDtypeStruct((ROWS, W), BF)
    return pl.pallas_call(
        column_body,
        name="whole_columns",
        grid_spec=pltpu.PrefetchScalarGridSpec(
            num_scalar_prefetch=1,
            grid=(ROWS // lanes,),
            in_specs=[pl.BlockSpec((PAIR, lanes), lambda i, *_: (0, i))] * 8,
            out_specs=[pl.BlockSpec((lanes, W), lambda i, *_: (i, 0))] * 2,
            scratch_shapes=[pltpu.VMEM((COLS, PAIR, lanes), BF)],
        ),
        out_shape=[out, out],
        compiler_params=params(dimension_semantics=("arbitrary",)),
        cost_estimate=cost(0, 8 * ROWS * W),
    )(place, *slabs)


def total_of(refs, rows):
    parts = [ref[rows, :].astype(F32) for ref in refs]
    return (parts[0] + parts[1]) + (parts[2] + parts[3])


def fold_body(one, two, three, four, out):
    out[...] = total_of((one, two, three, four), slice(None)).astype(BF)


def fold(parts):
    return pl.pallas_call(
        fold_body,
        name="fold",
        out_shape=jax.ShapeDtypeStruct(parts[0].shape, BF),
        compiler_params=params(8),
        cost_estimate=cost(4 * parts[0].size, 10 * parts[0].size),
    )(*parts)


def top_body(one, two, three, four, base, top, diag_a, top_b, sent):
    got = (one, two, three, four)
    value = base[...] - total_of(got, slice(0, PART))
    diag_a[...] = value
    total = total_of(got, slice(PART, 2 * PART))
    for _ in range(3):
        part = value.astype(BF)
        value = value - part.astype(F32)
        total = total + jnp.dot(part, top[...], preferred_element_type=F32)
    total = (-total).astype(BF)
    top_b[...] = total
    for c in range(COLS):
        sent[c] = jnp.concatenate([total[:, c * PART : (c + 1) * PART]] * 2, axis=1)


def top_part(got, base_a, factor_top):
    return pl.pallas_call(
        top_body,
        name="top_part",
        out_shape=[
            jax.ShapeDtypeStruct((PART, W), F32),
            jax.ShapeDtypeStruct((PART, W), BF),
            jax.ShapeDtypeStruct((COLS, PART, 2 * PART), BF),
        ],
        compiler_params=params(8),
        cost_estimate=cost(6 * PART * W * W, 2 * W * W),
    )(*got, base_a, factor_top)


def last_body(one, two, three, four, base, taken, top, diag_b):
    across = taken[...].reshape(W, 2 * PART)
    cross = lax.dot_general(
        across, top[...], (((0,), (0,)), ((), ())), preferred_element_type=F32
    )
    total = total_of((one, two, three, four), slice(2 * PART, 3 * PART))
    diag_b[...] = base[...] - total - cross[:PART]


def last_part(got, base_b, taken, factor_top):
    return pl.pallas_call(
        last_body,
        name="last_part",
        out_shape=jax.ShapeDtypeStruct((PART, W), F32),
        compiler_params=params(8),
        cost_estimate=cost(4 * PART * W * W, 2 * W * W),
    )(*got, base_b, taken, factor_top)


def send(value, **by):
    return lax.ppermute(value, BOTH, shifted(**by))


def around(value, axis):
    return [value] + [send(value, **{axis: step}) for step in STEPS[1:]]


def on_device(
    trailing, rows_a, counts_a, factor_a, rows_b, counts_b, factor_b, factor_top, base_a, base_b
):
    place = jnp.stack([lax.axis_index("row"), lax.axis_index("col")]).astype(jnp.int32)
    lists = (rows_a, counts_a, rows_b, counts_b)
    part_a, part_b = prep(place, lists, factor_a, factor_b, factor_top)
    part_a = lax.ppermute(part_a, BOTH, spread_pairs())
    part_b = lax.ppermute(part_b, BOTH, spread_pairs())
    a_own = jnp.stack(around(part_a, "dy"))
    b_own = jnp.stack(around(part_b, "dz"))
    a_down, a_up = send(a_own, dz=1), send(a_own, dz=-1)
    b_down, b_up = send(b_own, dy=1), send(b_own, dy=-1)
    trailing = hold(trailing, a_own)
    a_next, b_next, _ = lax.optimization_barrier((a_down, b_down, trailing))
    a_far, b_far = send(a_next, dz=1), send(b_next, dy=1)
    before = early_product(place, (a_down, a_up, b_own, b_down, b_up), trailing)
    slabs = []
    for half in range(2):
        keep, give = late_product(
            half, place, (a_own, a_far, b_far), trailing, before
        )
        own, one, two, three = pair_sum(place, keep, send(give, dc=1))
        slabs += [own, send(one, dx=1), send(two, dx=2), send(three, dx=-1)]
    columns, pieces = slots(place, lists, slabs, (factor_a, factor_b))
    near, other = send(columns, dx=1), send(columns, dx=-1)
    folded = fold(around(pieces, "dy"))
    got = around(folded, "dz")
    far = send(lax.optimization_barrier((columns, folded))[0], dx=2)
    _, (own, near, other) = lax.optimization_barrier((got, (columns, near, other)))
    mates = [send(slab, dc=1) for slab in (own, near, other)]
    diag_a, top_b, sent = top_part(got, base_a, factor_top)
    far, _ = lax.optimization_barrier((far, sent))
    taken = lax.all_to_all(sent, "col", 0, 0)
    column_a, column_b = whole_columns(place, [own, near, other, far, *mates, send(far, dc=1)])
    base_b, _ = lax.optimization_barrier((base_b, column_a))
    diag_b = last_part(got, base_b, taken, factor_top)
    return (column_a, diag_a, column_b, top_b, diag_b)


def solution(mesh):
    in_specs = (
        P("row", "col"),
        P(),
        P(),
        P("row", None),
        P(),
        P(),
        P("row", None),
        P(),
        P("col", None),
        P("col", None),
    )
    out_specs = (P("row", None), P("col", None), P("row", None), P("col", None), P("col", None))
    return jax.shard_map(
        on_device, mesh=mesh, in_specs=in_specs, out_specs=out_specs, check_vma=False
    )
```

```python
import functools

import jax
import jax.numpy as jnp
from jax import lax
from jax.experimental import pallas as pl
from jax.experimental.pallas import tpu as pltpu
from jax.sharding import PartitionSpec as P

BS = 128
W = 512
NB = 12
ROWS = NB * BS
SIDE = 4
PART = 64
COLS = 8
STEPS = (0, 1, -1, 2)
STRIP = 2 * BS
PAIR = 2 * PART
BOTH = ("row", "col")
MIB = 1024 * 1024
BF = jnp.bfloat16
F32 = jnp.float32


def device(z, y, x, core):
    return ((z % SIDE) * SIDE + y % SIDE) * 8 + (x % SIDE) * 2 + core % 2


def all_places():
    return [
        (z, y, x, core)
        for z in range(SIDE)
        for y in range(SIDE)
        for x in range(SIDE)
        for core in range(2)
    ]


def shifted(dz=0, dy=0, dx=0, dc=0):
    return [
        (device(z, y, x, c), device(z + dz, y + dy, x + dx, c + dc))
        for z, y, x, c in all_places()
    ]


def spread_pairs():
    pairs = []
    for z, y, x, core in all_places():
        plane = (z * SIDE + y) % 8
        to = device(z + core, y + x, plane // 2, plane % 2)
        pairs.append((device(z, y, x, core), to))
    return pairs


def params(mib=24, **more):
    return pltpu.CompilerParams(vmem_limit_bytes=mib * MIB, **more)


def cost(flops, moved):
    return pl.CostEstimate(flops=flops, bytes_accessed=moved, transcendentals=0)


def whole(shape):
    return pl.BlockSpec(shape, lambda *_: (0,) * len(shape))


def find_slot(rows, counts, owner, block):
    slot = jnp.int32(0)
    live = jnp.int32(0)
    for k in range(NB):
        hit = (rows[owner, k] == block) & (k < counts[owner])
        slot = jnp.where(hit, k, slot)
        live = jnp.where(hit, 1, live)
    return slot, live


def half_of(value, upper):
    return jnp.where(upper > 0, value[PART:], value[:PART])


def prep_a_body(place, rows_a, counts_a, part_a, out_a):
    for block in range(NB):
        slot, live = find_slot(rows_a, counts_a, place[0], block)
        at = pl.ds(pl.multiple_of(slot * BS, BS), BS)
        piece = half_of(part_a[at, :].T, place[1] % 2)
        out_a[block] = jnp.where(live > 0, piece, jnp.zeros_like(piece))


def width_slice(rows):
    return pl.BlockSpec((rows, BS), lambda i, place, *_: (0, place[1] // 2))


def prep_a(place, lists, factor_a):
    return pl.pallas_call(
        prep_a_body,
        name="prep_a",
        grid_spec=pltpu.PrefetchScalarGridSpec(
            num_scalar_prefetch=3,
            grid=(1,),
            in_specs=[width_slice(ROWS)],
            out_specs=whole((NB, PART, BS)),
        ),
        out_shape=jax.ShapeDtypeStruct((NB, PART, BS), BF),
        compiler_params=params(56),
        cost_estimate=cost(0, 4 * ROWS * BS),
    )(place, *lists[:2], factor_a)


def prep_b_body(place, rows_a, counts_a, rows_b, counts_b, fa, part_b, top, out_b, fix):
    owner = place[0]
    upper = place[1] % 2
    fix[...] = lax.dot_general(
        top[...], fa[...], (((0,), (1,)), ((), ())), preferred_element_type=F32
    )
    for block in range(NB):
        slot_a, live_a = find_slot(rows_a, counts_a, owner, block)
        slot_b, live_b = find_slot(rows_b, counts_b, owner, block)
        at_a = pl.ds(pl.multiple_of(slot_a * BS, BS), BS)
        at_b = pl.ds(pl.multiple_of(slot_b * BS, BS), BS)
        moved = half_of(fix[:, at_a], upper)
        piece = half_of(part_b[at_b, :].T, upper).astype(F32)
        piece = jnp.where(live_b > 0, piece, jnp.zeros_like(piece))
        out_b[block] = (piece - jnp.where(live_a > 0, moved, jnp.zeros_like(moved))).astype(BF)


def prep_b(place, lists, factor_a, factor_b, factor_top):
    return pl.pallas_call(
        prep_b_body,
        name="prep_b",
        grid_spec=pltpu.PrefetchScalarGridSpec(
            num_scalar_prefetch=5,
            grid=(1,),
            in_specs=[whole((ROWS, W)), width_slice(ROWS), width_slice(W)],
            out_specs=whole((NB, PART, BS)),
            scratch_shapes=[pltpu.VMEM((BS, ROWS), F32)],
        ),
        out_shape=jax.ShapeDtypeStruct((NB, PART, BS), BF),
        compiler_params=params(56),
        cost_estimate=cost(2 * BS * ROWS * W, 2 * ROWS * (W + 4 * BS)),
    )(place, *lists, factor_a, factor_b, factor_top)


def where(place):
    z, y, plane = place[0] // SIDE, place[0] % SIDE, place[1]
    u = (z - plane // SIDE + SIDE) % SIDE
    v = (y - plane % SIDE + SIDE) % SIDE
    return u, v


def turn(value, by):
    return (value + by + SIDE) % SIDE


def load_a(copies, buf, u, spread, start=0, many=SIDE):
    for i in range(start, start + many):
        copies.append((buf.at[i - start], spread.at[:, u // 2, i * PART : (i + 1) * PART, :]))


def load_b(copies, buf, u, first, spread, start=0, many=SIDE):
    for i in range(start, start + many):
        ui = turn(u, -STEPS[i])
        at = pl.ds(pl.multiple_of(first + (ui % 2) * PART, PART), PART)
        copies.append((buf.at[i - start], spread.at[:, ui // 2, at, :]))


def run_copies(copies, sems):
    started = [pltpu.make_async_copy(a, b, sems.at[i]) for i, (a, b) in enumerate(copies)]
    for copy in started:
        copy.start()
    for copy in started:
        copy.wait()


def multiply(spread, tile):
    left = jnp.concatenate([spread[n, h] for n in range(NB) for h in range(2)], axis=1)
    return lax.dot_general(
        left, tile, (((1,), (1,)), ((), ())), preferred_element_type=F32
    ).astype(BF)


def hold_body(source, _, target, sem):
    copy = pltpu.make_async_copy(source, target, sem)
    copy.start()
    copy.wait()


def hold(trailing, after):
    return pl.pallas_call(
        hold_body,
        name="hold",
        in_specs=[pl.BlockSpec(memory_space=pltpu.HBM), pl.BlockSpec(memory_space=pl.ANY)],
        out_specs=pl.BlockSpec(memory_space=pltpu.VMEM),
        out_shape=pltpu.VMEM(trailing.shape, BF),
        scratch_shapes=[pltpu.SemaphoreType.DMA],
        compiler_params=params(8),
        cost_estimate=cost(0, 2 * trailing.size),
    )(trailing, after)


def rows_of(tile, step):
    return tile[pl.ds(pl.multiple_of(step * STRIP, STRIP), STRIP), :]


def early_body(place, a_down, a_up, b_own, b_down, b_up, tile, out, spread, sems):
    u, v = where(place)

    @pl.when(pl.program_id(0) == 0)
    def _():
        copies = []
        load_a(copies, a_down, turn(u, -1), spread)
        load_a(copies, a_up, turn(u, 1), spread)
        for t, buf in enumerate((b_own, b_down, b_up)):
            load_b(copies, buf, u, W // 2 + 2 * t * PART, spread)
        run_copies(copies, sems)

    value = multiply(spread, rows_of(tile, pl.program_id(0)))
    for i, step in enumerate(STEPS):
        out[2 * turn(v, -step) + (u + 1) % 2, :PART, :] = value[i * PART : (i + 1) * PART]
    for j in range(6):
        to = 2 * turn(v, -STEPS[j // 2]) + j % 2
        out[to, PART:, :] = value[W // 2 + j * PART : W // 2 + (j + 1) * PART]


def early_product(place, bufs, trailing):
    deep = trailing.shape[1]
    rows = W // 2 + 6 * PART
    return pl.pallas_call(
        early_body,
        name="early_product",
        grid_spec=pltpu.PrefetchScalarGridSpec(
            num_scalar_prefetch=1,
            grid=(ROWS // STRIP,),
            in_specs=[pl.BlockSpec(memory_space=pl.ANY)] * 5
            + [pl.BlockSpec(memory_space=pltpu.VMEM)],
            out_specs=pl.BlockSpec((COLS, PAIR, STRIP), lambda i, *_: (0, 0, i)),
            scratch_shapes=[
                pltpu.VMEM((NB, 2, rows, BS), BF),
                pltpu.SemaphoreType.DMA((20,)),
            ],
        ),
        out_shape=jax.ShapeDtypeStruct((COLS, PAIR, ROWS), BF),
        compiler_params=params(20, dimension_semantics=("arbitrary",)),
        cost_estimate=cost(2 * rows * ROWS * deep, 2 * rows * deep + 4 * W * ROWS),
    )(place, *bufs, trailing)


def late_body(
    half, place, a_own, a_far, a_far_more, b_far, b_far_more, tile, before, keep, give, spread, ready, sems
):
    u, v = where(place)
    core = place[1] % 2

    @pl.when(pl.program_id(0) == 0)
    def _():
        copies = []
        load_a(copies, a_own, u, spread)
        load_a(copies, a_far, turn(u, 2), spread, 0, 2)
        load_a(copies, a_far_more, turn(u, 2), spread, 2, 2)
        load_b(copies, b_far, u, W // 2, spread, 0, 2)
        load_b(copies, b_far_more, u, W // 2, spread, 2, 2)
        run_copies(copies, sems)

    ready[...] = before[...]
    value = multiply(spread, rows_of(tile, half * HALF_STEPS + pl.program_id(0)))
    for i, step in enumerate(STEPS):
        ready[2 * turn(v, -step) + u % 2, :PART, :] = value[i * PART : (i + 1) * PART]
    for j in range(2):
        ready[2 * turn(v, 2) + j, PART:, :] = value[W // 2 + j * PART : W // 2 + (j + 1) * PART]
    for x in range(SIDE):
        keep[x] = ready[2 * x + core]
        give[x] = ready[2 * x + 1 - core]


HALF_STEPS = ROWS // STRIP // 2


def late_product(half, place, bufs, trailing, before):
    deep = trailing.shape[1]
    rows = W // 2 + 2 * PART
    out = jax.ShapeDtypeStruct((SIDE, PAIR, ROWS // 2), BF)
    spec = pl.BlockSpec((SIDE, PAIR, STRIP), lambda i, *_: (0, 0, i))
    return pl.pallas_call(
        functools.partial(late_body, half),
        name="late_product",
        grid_spec=pltpu.PrefetchScalarGridSpec(
            num_scalar_prefetch=1,
            grid=(HALF_STEPS,),
            in_specs=[pl.BlockSpec(memory_space=pl.ANY)] * 5
            + [
                pl.BlockSpec(memory_space=pltpu.VMEM),
                pl.BlockSpec((COLS, PAIR, STRIP), lambda i, *_: (0, 0, half * HALF_STEPS + i)),
            ],
            out_specs=[spec, spec],
            scratch_shapes=[
                pltpu.VMEM((NB, 2, rows, BS), BF),
                pltpu.VMEM((COLS, PAIR, STRIP), BF),
                pltpu.SemaphoreType.DMA((12,)),
            ],
        ),
        out_shape=[out, out],
        compiler_params=params(20, dimension_semantics=("arbitrary",)),
        cost_estimate=cost(rows * ROWS * deep, 2 * rows * deep + 4 * W * ROWS),
    )(place, *bufs, trailing, before)


def pair_body(joined, place, mine, taken, *refs):
    before, outs = refs[: joined], refs[joined:]
    x = place[1] // 2
    for i in range(SIDE):
        at = (x + i) % SIDE
        total = (mine[at].astype(F32) + taken[at].astype(F32)).astype(BF)
        if joined and i == 2:
            outs[i][0] = before[0][...]
            outs[i][1] = total
        else:
            outs[i][...] = total


def pair_sum(place, mine, taken, *before):
    lanes = 3 * BS
    width = mine.shape[2]
    spec = pl.BlockSpec((SIDE, PAIR, lanes), lambda i, *_: (0, 0, i))
    one = pl.BlockSpec((PAIR, lanes), lambda i, *_: (0, i))
    two = pl.BlockSpec((2, PAIR, lanes), lambda i, *_: (0, 0, i))
    shape = jax.ShapeDtypeStruct((PAIR, width), BF)
    double = jax.ShapeDtypeStruct((2, PAIR, width), BF)
    joined = len(before)
    return pl.pallas_call(
        functools.partial(pair_body, joined),
        name="pair_sum",
        grid_spec=pltpu.PrefetchScalarGridSpec(
            num_scalar_prefetch=1,
            grid=(width // lanes,),
            in_specs=[spec, spec] + [one] * joined,
            out_specs=[one, one, two if joined else one, one],
        ),
        out_shape=[shape, shape, double if joined else shape, shape],
        compiler_params=params(dimension_semantics=("arbitrary",)),
        cost_estimate=cost(W * width, 6 * W * width),
    )(place, mine, taken, *before)


def slots_body(
    place, rows_a, counts_a, rows_b, counts_b, *refs
):
    slabs, far, (fa, fb, columns, pieces, natural, left) = refs[:6], refs[6], refs[7:]
    owner = place[0]
    width = ROWS // 2
    for half in range(2):
        total = total_of((*slabs[half * 3 : half * 3 + 3], far.at[half]), slice(None))
        natural[:, half * width : (half + 1) * width] = (-total).astype(BF)
    for k in range(NB):
        at = slice(k * BS, (k + 1) * BS)
        block = natural[:PART, pl.ds(pl.multiple_of(rows_a[owner, k] * BS, BS), BS)]
        columns[:PART, at] = jnp.where(k < counts_a[owner], block, jnp.zeros_like(block))
        block = natural[:, pl.ds(pl.multiple_of(rows_b[owner, k] * BS, BS), BS)]
        block = jnp.where(k < counts_b[owner], block, jnp.zeros_like(block))
        left[:, at] = block
        columns[PART:, at] = block[PART:]
    one = jnp.dot(columns[:PART, :], fa[...], preferred_element_type=F32)
    two = jnp.dot(left[...], fb[...], preferred_element_type=F32)
    pieces[:PART, :] = one.astype(BF)
    pieces[PART:, :] = two.astype(BF)


def slots(place, lists, slabs, factors):
    return pl.pallas_call(
        slots_body,
        name="slots",
        grid_spec=pltpu.PrefetchScalarGridSpec(
            num_scalar_prefetch=5,
            grid=(1,),
            in_specs=[whole((PAIR, ROWS // 2))] * 6
            + [whole((2, PAIR, ROWS // 2))]
            + [whole((ROWS, W))] * 2,
            out_specs=[whole((PAIR, ROWS)), whole((3 * PART, W))],
            scratch_shapes=[pltpu.VMEM((PAIR, ROWS), BF)] * 2,
        ),
        out_shape=[
            jax.ShapeDtypeStruct((PAIR, ROWS), BF),
            jax.ShapeDtypeStruct((3 * PART, W), BF),
        ],
        compiler_params=params(),
        cost_estimate=cost(6 * PART * ROWS * W, 4 * ROWS * W + 10 * PAIR * ROWS),
    )(place, *lists, *slabs, *factors)


def column_body(place, *refs):
    slabs, column_a, column_b, wide = refs[:8], refs[8], refs[9], refs[10]
    core, x = place[1] % 2, place[1] // 2
    for i in range(8):
        at = 2 * turn(x, -STEPS[i % SIDE]) + (core if i < SIDE else 1 - core)
        wide[at] = slabs[i][...]
    for first, out in ((0, column_a), (PART, column_b)):
        out[...] = wide[:, first : first + PART, :].reshape(W, wide.shape[2]).T


def whole_columns(place, slabs):
    lanes = 2 * BS
    out = jax.ShapeDtypeStruct((ROWS, W), BF)
    return pl.pallas_call(
        column_body,
        name="whole_columns",
        grid_spec=pltpu.PrefetchScalarGridSpec(
            num_scalar_prefetch=1,
            grid=(ROWS // lanes,),
            in_specs=[pl.BlockSpec((PAIR, lanes), lambda i, *_: (0, i))] * 8,
            out_specs=[pl.BlockSpec((lanes, W), lambda i, *_: (i, 0))] * 2,
            scratch_shapes=[pltpu.VMEM((COLS, PAIR, lanes), BF)],
        ),
        out_shape=[out, out],
        compiler_params=params(dimension_semantics=("arbitrary",)),
        cost_estimate=cost(0, 8 * ROWS * W),
    )(place, *slabs)


def total_of(refs, rows):
    parts = [ref[rows, :].astype(F32) for ref in refs]
    return (parts[0] + parts[1]) + (parts[2] + parts[3])


def fold_body(one, two, three, four, out):
    out[...] = total_of((one, two, three, four), slice(None)).astype(BF)


def fold(parts):
    return pl.pallas_call(
        fold_body,
        name="fold",
        out_shape=jax.ShapeDtypeStruct(parts[0].shape, BF),
        compiler_params=params(8),
        cost_estimate=cost(4 * parts[0].size, 10 * parts[0].size),
    )(*parts)


def top_body(one, two, three, four, base, top, diag_a, top_b, sent):
    got = (one, two, three, four)
    value = base[...] - total_of(got, slice(0, PART))
    diag_a[...] = value
    total = total_of(got, slice(PART, 2 * PART))
    for _ in range(3):
        part = value.astype(BF)
        value = value - part.astype(F32)
        total = total + jnp.dot(part, top[...], preferred_element_type=F32)
    total = (-total).astype(BF)
    top_b[...] = total
    for c in range(COLS):
        sent[c] = jnp.concatenate([total[:, c * PART : (c + 1) * PART]] * 2, axis=1)


def top_part(got, base_a, factor_top):
    return pl.pallas_call(
        top_body,
        name="top_part",
        out_shape=[
            jax.ShapeDtypeStruct((PART, W), F32),
            jax.ShapeDtypeStruct((PART, W), BF),
            jax.ShapeDtypeStruct((COLS, PART, 2 * PART), BF),
        ],
        compiler_params=params(8),
        cost_estimate=cost(6 * PART * W * W, 2 * W * W),
    )(*got, base_a, factor_top)


def last_body(one, two, three, four, base, taken, top, diag_b):
    across = taken[...].reshape(W, 2 * PART)
    cross = lax.dot_general(
        across, top[...], (((0,), (0,)), ((), ())), preferred_element_type=F32
    )
    total = total_of((one, two, three, four), slice(2 * PART, 3 * PART))
    diag_b[...] = base[...] - total - cross[:PART]


def last_part(got, base_b, taken, factor_top):
    return pl.pallas_call(
        last_body,
        name="last_part",
        out_shape=jax.ShapeDtypeStruct((PART, W), F32),
        compiler_params=params(8),
        cost_estimate=cost(4 * PART * W * W, 2 * W * W),
    )(*got, base_b, taken, factor_top)


def send(value, **by):
    return lax.ppermute(value, BOTH, shifted(**by))


def around(value, axis):
    return [value] + [send(value, **{axis: step}) for step in STEPS[1:]]


def on_device(
    trailing, rows_a, counts_a, factor_a, rows_b, counts_b, factor_b, factor_top, base_a, base_b
):
    place = jnp.stack([lax.axis_index("row"), lax.axis_index("col")]).astype(jnp.int32)
    lists = (rows_a, counts_a, rows_b, counts_b)
    part_a = lax.ppermute(prep_a(place, lists, factor_a), BOTH, spread_pairs())
    part_b = prep_b(place, lists, factor_a, factor_b, factor_top)
    part_b = lax.ppermute(part_b, BOTH, spread_pairs())
    a_own = jnp.stack(around(part_a, "dy"))
    b_own = jnp.stack(around(part_b, "dz"))
    a_down, a_up = send(a_own, dz=1), send(a_own, dz=-1)
    b_down, b_up = send(b_own, dy=1), send(b_own, dy=-1)
    trailing = hold(trailing, a_own)
    a_next, b_next, _ = lax.optimization_barrier((a_down, b_down, trailing))
    a_far, b_far = send(a_next[:2], dz=1), send(b_next[:2], dy=1)
    a_far_more, b_far_more = send(a_up[2:], dz=-1), send(b_up[2:], dy=-1)
    before = early_product(place, (a_down, a_up, b_own, b_down, b_up), trailing)
    slabs, far = [], ()
    for half in range(2):
        keep, give = late_product(
            half, place, (a_own, a_far, a_far_more, b_far, b_far_more), trailing, before
        )
        own, one, *far, three = pair_sum(place, keep, send(give, dc=1), *far)
        slabs += [own, send(one, dx=1), send(three, dx=-1)]
    slabs.append(send(far[0], dx=2))
    columns, pieces = slots(place, lists, slabs, (factor_a, factor_b))
    near, other = send(columns, dx=1), send(columns, dx=-1)
    first, near, other = lax.optimization_barrier((around(pieces, "dy"), near, other))
    folded = fold(first)
    got = around(folded, "dz")
    far = send(lax.optimization_barrier((columns, folded))[0], dx=2)
    _, (own, near, other) = lax.optimization_barrier((got, (columns, near, other)))
    mates = [send(slab, dc=1) for slab in (own, near, other)]
    diag_a, top_b, sent = top_part(got, base_a, factor_top)
    far, _ = lax.optimization_barrier((far, sent))
    taken = lax.all_to_all(sent, "col", 0, 0)
    column_a, column_b = whole_columns(place, [own, near, other, far, *mates, send(far, dc=1)])
    base_b, _ = lax.optimization_barrier((base_b, column_a))
    diag_b = last_part(got, base_b, taken, factor_top)
    return (column_a, diag_a, column_b, top_b, diag_b)


def solution(mesh):
    in_specs = (
        P("row", "col"),
        P(),
        P(),
        P("row", None),
        P(),
        P(),
        P("row", None),
        P(),
        P("col", None),
        P("col", None),
    )
    out_specs = (P("row", None), P("col", None), P("row", None), P("col", None), P("col", None))
    return jax.shard_map(
        on_device, mesh=mesh, in_specs=in_specs, out_specs=out_specs, check_vma=False
    )
```

```python
import functools

import jax
import jax.numpy as jnp
from jax import lax
from jax.experimental import pallas as pl
from jax.experimental.pallas import tpu as pltpu
from jax.sharding import PartitionSpec as P

BS = 128
W = 512
NB = 12
ROWS = NB * BS
SIDE = 4
PART = 64
COLS = 8
STEPS = (0, 1, -1, 2)
STRIP = 2 * BS
PAIR = 2 * PART
BOTH = ("row", "col")
MIB = 1024 * 1024
BF = jnp.bfloat16
F32 = jnp.float32


def device(z, y, x, core):
    return ((z % SIDE) * SIDE + y % SIDE) * 8 + (x % SIDE) * 2 + core % 2


def all_places():
    return [
        (z, y, x, core)
        for z in range(SIDE)
        for y in range(SIDE)
        for x in range(SIDE)
        for core in range(2)
    ]


def shifted(dz=0, dy=0, dx=0, dc=0):
    return [
        (device(z, y, x, c), device(z + dz, y + dy, x + dx, c + dc))
        for z, y, x, c in all_places()
    ]


def spread_pairs():
    pairs = []
    for z, y, x, core in all_places():
        plane = (z * SIDE + y) % 8
        to = device(z + core, y + x, plane // 2, plane % 2)
        pairs.append((device(z, y, x, core), to))
    return pairs


def params(mib=24, **more):
    return pltpu.CompilerParams(vmem_limit_bytes=mib * MIB, **more)


def cost(flops, moved):
    return pl.CostEstimate(flops=flops, bytes_accessed=moved, transcendentals=0)


def whole(shape):
    return pl.BlockSpec(shape, lambda *_: (0,) * len(shape))


def half_of(value, upper):
    return jnp.where(upper > 0, value[PART:], value[:PART])


def prep_a_body(place, rows_a, counts_a, part_a, out_a):
    owner = place[0]
    out_a[...] = jnp.zeros_like(out_a)
    for k in range(NB):
        piece = half_of(part_a[k * BS : (k + 1) * BS, :].T, place[1] % 2)

        @pl.when(k < counts_a[owner])
        def _():
            out_a[rows_a[owner, k]] = piece


def width_slice(rows):
    return pl.BlockSpec((rows, BS), lambda i, place, *_: (0, place[1] // 2))


def prep_a(place, lists, factor_a):
    return pl.pallas_call(
        prep_a_body,
        name="prep_a",
        grid_spec=pltpu.PrefetchScalarGridSpec(
            num_scalar_prefetch=3,
            grid=(1,),
            in_specs=[width_slice(ROWS)],
            out_specs=whole((NB, PART, BS)),
        ),
        out_shape=jax.ShapeDtypeStruct((NB, PART, BS), BF),
        compiler_params=params(56),
        cost_estimate=cost(0, 4 * ROWS * BS),
    )(place, *lists[:2], factor_a)


def prep_b_body(place, rows_a, counts_a, rows_b, counts_b, fa, part_b, top, out_b, mixed):
    owner = place[0]
    upper = place[1] % 2
    moved = half_of(
        lax.dot_general(top[...], fa[...], (((0,), (1,)), ((), ())), preferred_element_type=F32),
        upper,
    )
    mixed[...] = jnp.zeros_like(mixed)
    for k in range(NB):

        @pl.when(k < counts_a[owner])
        def _():
            mixed[rows_a[owner, k]] = -moved[:, k * BS : (k + 1) * BS]

    for k in range(NB):
        piece = half_of(part_b[k * BS : (k + 1) * BS, :].T, upper).astype(F32)

        @pl.when(k < counts_b[owner])
        def _():
            mixed[rows_b[owner, k]] += piece

    out_b[...] = mixed[...].astype(BF)


def prep_b(place, lists, factor_a, factor_b, factor_top):
    return pl.pallas_call(
        prep_b_body,
        name="prep_b",
        grid_spec=pltpu.PrefetchScalarGridSpec(
            num_scalar_prefetch=5,
            grid=(1,),
            in_specs=[whole((ROWS, W)), width_slice(ROWS), width_slice(W)],
            out_specs=whole((NB, PART, BS)),
            scratch_shapes=[pltpu.VMEM((NB, PART, BS), F32)],
        ),
        out_shape=jax.ShapeDtypeStruct((NB, PART, BS), BF),
        compiler_params=params(56),
        cost_estimate=cost(2 * BS * ROWS * W, 2 * ROWS * (W + 4 * BS)),
    )(place, *lists, factor_a, factor_b, factor_top)


def where(place):
    z, y, plane = place[0] // SIDE, place[0] % SIDE, place[1]
    u = (z - plane // SIDE + SIDE) % SIDE
    v = (y - plane % SIDE + SIDE) % SIDE
    return u, v


def turn(value, by):
    return (value + by + SIDE) % SIDE


def load_a(copies, buf, u, spread, start=0, many=SIDE):
    for i in range(start, start + many):
        copies.append((buf.at[i - start], spread.at[:, u // 2, i * PART : (i + 1) * PART, :]))


def load_b(copies, buf, u, first, spread, start=0, many=SIDE):
    for i in range(start, start + many):
        ui = turn(u, -STEPS[i])
        at = pl.ds(pl.multiple_of(first + (ui % 2) * PART, PART), PART)
        copies.append((buf.at[i - start], spread.at[:, ui // 2, at, :]))


def run_copies(copies, sems):
    started = [pltpu.make_async_copy(a, b, sems.at[i]) for i, (a, b) in enumerate(copies)]
    for copy in started:
        copy.start()
    for copy in started:
        copy.wait()


def multiply(spread, tile):
    left = jnp.concatenate([spread[n, h] for n in range(NB) for h in range(2)], axis=1)
    return lax.dot_general(
        left, tile, (((1,), (1,)), ((), ())), preferred_element_type=F32
    ).astype(BF)


def hold_body(source, _, target, sem):
    copy = pltpu.make_async_copy(source, target, sem)
    copy.start()
    copy.wait()


def hold(trailing, after):
    return pl.pallas_call(
        hold_body,
        name="hold",
        in_specs=[pl.BlockSpec(memory_space=pltpu.HBM), pl.BlockSpec(memory_space=pl.ANY)],
        out_specs=pl.BlockSpec(memory_space=pltpu.VMEM),
        out_shape=pltpu.VMEM(trailing.shape, BF),
        scratch_shapes=[pltpu.SemaphoreType.DMA],
        compiler_params=params(8),
        cost_estimate=cost(0, 2 * trailing.size),
    )(trailing, after)


def rows_of(tile, step):
    return tile[pl.ds(pl.multiple_of(step * STRIP, STRIP), STRIP), :]


def early_body(place, a_down, a_up, b_own, b_down, b_up, tile, out, spread, sems):
    u, v = where(place)

    @pl.when(pl.program_id(0) == 0)
    def _():
        copies = []
        load_a(copies, a_down, turn(u, -1), spread)
        load_a(copies, a_up, turn(u, 1), spread)
        for t, buf in enumerate((b_own, b_down, b_up)):
            load_b(copies, buf, u, W // 2 + 2 * t * PART, spread)
        run_copies(copies, sems)

    value = multiply(spread, rows_of(tile, pl.program_id(0)))
    for i, step in enumerate(STEPS):
        out[2 * turn(v, -step) + (u + 1) % 2, :PART, :] = value[i * PART : (i + 1) * PART]
    for j in range(6):
        to = 2 * turn(v, -STEPS[j // 2]) + j % 2
        out[to, PART:, :] = value[W // 2 + j * PART : W // 2 + (j + 1) * PART]


def early_product(place, bufs, trailing):
    deep = trailing.shape[1]
    rows = W // 2 + 6 * PART
    return pl.pallas_call(
        early_body,
        name="early_product",
        grid_spec=pltpu.PrefetchScalarGridSpec(
            num_scalar_prefetch=1,
            grid=(ROWS // STRIP,),
            in_specs=[pl.BlockSpec(memory_space=pl.ANY)] * 5
            + [pl.BlockSpec(memory_space=pltpu.VMEM)],
            out_specs=pl.BlockSpec((COLS, PAIR, STRIP), lambda i, *_: (0, 0, i)),
            scratch_shapes=[
                pltpu.VMEM((NB, 2, rows, BS), BF),
                pltpu.SemaphoreType.DMA((20,)),
            ],
        ),
        out_shape=jax.ShapeDtypeStruct((COLS, PAIR, ROWS), BF),
        compiler_params=params(20, dimension_semantics=("arbitrary",)),
        cost_estimate=cost(2 * rows * ROWS * deep, 2 * rows * deep + 4 * W * ROWS),
    )(place, *bufs, trailing)


def late_body(
    half, place, a_own, a_far, a_far_more, b_far, b_far_more, tile, before, keep, give, spread, ready, sems
):
    u, v = where(place)
    core = place[1] % 2

    @pl.when(pl.program_id(0) == 0)
    def _():
        copies = []
        load_a(copies, a_own, u, spread)
        load_a(copies, a_far, turn(u, 2), spread, 0, 2)
        load_a(copies, a_far_more, turn(u, 2), spread, 2, 2)
        load_b(copies, b_far, u, W // 2, spread, 0, 2)
        load_b(copies, b_far_more, u, W // 2, spread, 2, 2)
        run_copies(copies, sems)

    ready[...] = before[...]
    value = multiply(spread, rows_of(tile, half * HALF_STEPS + pl.program_id(0)))
    for i, step in enumerate(STEPS):
        ready[2 * turn(v, -step) + u % 2, :PART, :] = value[i * PART : (i + 1) * PART]
    for j in range(2):
        ready[2 * turn(v, 2) + j, PART:, :] = value[W // 2 + j * PART : W // 2 + (j + 1) * PART]
    for x in range(SIDE):
        keep[x] = ready[2 * x + core]
        give[x] = ready[2 * x + 1 - core]


HALF_STEPS = ROWS // STRIP // 2


def late_product(half, place, bufs, trailing, before):
    deep = trailing.shape[1]
    rows = W // 2 + 2 * PART
    out = jax.ShapeDtypeStruct((SIDE, PAIR, ROWS // 2), BF)
    spec = pl.BlockSpec((SIDE, PAIR, STRIP), lambda i, *_: (0, 0, i))
    return pl.pallas_call(
        functools.partial(late_body, half),
        name="late_product",
        grid_spec=pltpu.PrefetchScalarGridSpec(
            num_scalar_prefetch=1,
            grid=(HALF_STEPS,),
            in_specs=[pl.BlockSpec(memory_space=pl.ANY)] * 5
            + [
                pl.BlockSpec(memory_space=pltpu.VMEM),
                pl.BlockSpec((COLS, PAIR, STRIP), lambda i, *_: (0, 0, half * HALF_STEPS + i)),
            ],
            out_specs=[spec, spec],
            scratch_shapes=[
                pltpu.VMEM((NB, 2, rows, BS), BF),
                pltpu.VMEM((COLS, PAIR, STRIP), BF),
                pltpu.SemaphoreType.DMA((12,)),
            ],
        ),
        out_shape=[out, out],
        compiler_params=params(20, dimension_semantics=("arbitrary",)),
        cost_estimate=cost(rows * ROWS * deep, 2 * rows * deep + 4 * W * ROWS),
    )(place, *bufs, trailing, before)


def pair_body(place, mine, taken, *outs):
    x = place[1] // 2
    for i in range(SIDE):
        at = (x + i) % SIDE
        outs[i][...] = (mine[at].astype(F32) + taken[at].astype(F32)).astype(BF)


def pair_sum(place, mine, taken):
    lanes = 3 * BS
    width = mine.shape[2]
    spec = pl.BlockSpec((SIDE, PAIR, lanes), lambda i, *_: (0, 0, i))
    return pl.pallas_call(
        pair_body,
        name="pair_sum",
        grid_spec=pltpu.PrefetchScalarGridSpec(
            num_scalar_prefetch=1,
            grid=(width // lanes,),
            in_specs=[spec, spec],
            out_specs=[pl.BlockSpec((PAIR, lanes), lambda i, *_: (0, i))] * SIDE,
        ),
        out_shape=[jax.ShapeDtypeStruct((PAIR, width), BF)] * SIDE,
        compiler_params=params(dimension_semantics=("arbitrary",)),
        cost_estimate=cost(W * width, 6 * W * width),
    )(place, mine, taken)


def slots_body(
    place, rows_a, counts_a, rows_b, counts_b, *refs
):
    slabs, (fa, fb, columns, pieces, natural, left) = refs[:8], refs[8:]
    owner = place[0]
    width = ROWS // 2
    for half in range(2):
        total = total_of(slabs[half * SIDE : (half + 1) * SIDE], slice(None))
        natural[:, half * width : (half + 1) * width] = (-total).astype(BF)
    for k in range(NB):
        at = slice(k * BS, (k + 1) * BS)
        block = natural[:PART, pl.ds(pl.multiple_of(rows_a[owner, k] * BS, BS), BS)]
        columns[:PART, at] = jnp.where(k < counts_a[owner], block, jnp.zeros_like(block))
        block = natural[:, pl.ds(pl.multiple_of(rows_b[owner, k] * BS, BS), BS)]
        block = jnp.where(k < counts_b[owner], block, jnp.zeros_like(block))
        left[:, at] = block
        columns[PART:, at] = block[PART:]
    one = jnp.dot(columns[:PART, :], fa[...], preferred_element_type=F32)
    two = jnp.dot(left[...], fb[...], preferred_element_type=F32)
    pieces[:PART, :] = one.astype(BF)
    pieces[PART:, :] = two.astype(BF)


def slots(place, lists, slabs, factors):
    return pl.pallas_call(
        slots_body,
        name="slots",
        grid_spec=pltpu.PrefetchScalarGridSpec(
            num_scalar_prefetch=5,
            grid=(1,),
            in_specs=[whole((PAIR, ROWS // 2))] * 8 + [whole((ROWS, W))] * 2,
            out_specs=[whole((PAIR, ROWS)), whole((3 * PART, W))],
            scratch_shapes=[pltpu.VMEM((PAIR, ROWS), BF)] * 2,
        ),
        out_shape=[
            jax.ShapeDtypeStruct((PAIR, ROWS), BF),
            jax.ShapeDtypeStruct((3 * PART, W), BF),
        ],
        compiler_params=params(),
        cost_estimate=cost(6 * PART * ROWS * W, 4 * ROWS * W + 10 * PAIR * ROWS),
    )(place, *lists, *slabs, *factors)


def column_body(place, *refs):
    slabs, column_a, column_b, wide = refs[:8], refs[8], refs[9], refs[10]
    core, x = place[1] % 2, place[1] // 2
    for i in range(8):
        at = 2 * turn(x, -STEPS[i % SIDE]) + (core if i < SIDE else 1 - core)
        wide[at] = slabs[i][...]
    for first, out in ((0, column_a), (PART, column_b)):
        out[...] = wide[:, first : first + PART, :].reshape(W, wide.shape[2]).T


def whole_columns(place, slabs):
    lanes = 4 * BS
    out = jax.ShapeDtypeStruct((ROWS, W), BF)
    return pl.pallas_call(
        column_body,
        name="whole_columns",
        grid_spec=pltpu.PrefetchScalarGridSpec(
            num_scalar_prefetch=1,
            grid=(ROWS // lanes,),
            in_specs=[pl.BlockSpec((PAIR, lanes), lambda i, *_: (0, i))] * 8,
            out_specs=[pl.BlockSpec((lanes, W), lambda i, *_: (i, 0))] * 2,
            scratch_shapes=[pltpu.VMEM((COLS, PAIR, lanes), BF)],
        ),
        out_shape=[out, out],
        compiler_params=params(dimension_semantics=("arbitrary",)),
        cost_estimate=cost(0, 8 * ROWS * W),
    )(place, *slabs)


def total_of(refs, rows):
    parts = [ref[rows, :].astype(F32) for ref in refs]
    return (parts[0] + parts[1]) + (parts[2] + parts[3])


def fold_body(one, two, three, four, out):
    out[...] = total_of((one, two, three, four), slice(None)).astype(BF)


def fold(parts):
    return pl.pallas_call(
        fold_body,
        name="fold",
        out_shape=jax.ShapeDtypeStruct(parts[0].shape, BF),
        compiler_params=params(8),
        cost_estimate=cost(4 * parts[0].size, 10 * parts[0].size),
    )(*parts)


def top_body(one, two, three, four, base, top, diag_a, top_b, sent):
    got = (one, two, three, four)
    value = base[...] - total_of(got, slice(0, PART))
    diag_a[...] = value
    total = total_of(got, slice(PART, 2 * PART))
    for _ in range(3):
        part = value.astype(BF)
        value = value - part.astype(F32)
        total = total + jnp.dot(part, top[...], preferred_element_type=F32)
    total = (-total).astype(BF)
    top_b[...] = total
    for c in range(COLS):
        sent[c] = jnp.concatenate([total[:, c * PART : (c + 1) * PART]] * 2, axis=1)


def top_part(got, base_a, factor_top):
    return pl.pallas_call(
        top_body,
        name="top_part",
        out_shape=[
            jax.ShapeDtypeStruct((PART, W), F32),
            jax.ShapeDtypeStruct((PART, W), BF),
            jax.ShapeDtypeStruct((COLS, PART, 2 * PART), BF),
        ],
        compiler_params=params(8),
        cost_estimate=cost(6 * PART * W * W, 2 * W * W),
    )(*got, base_a, factor_top)


def last_body(one, two, three, four, base, taken, top, diag_b):
    across = taken[...].reshape(W, 2 * PART)
    cross = lax.dot_general(
        across, top[...], (((0,), (0,)), ((), ())), preferred_element_type=F32
    )
    total = total_of((one, two, three, four), slice(2 * PART, 3 * PART))
    diag_b[...] = base[...] - total - cross[:PART]


def last_part(got, base_b, taken, factor_top):
    return pl.pallas_call(
        last_body,
        name="last_part",
        out_shape=jax.ShapeDtypeStruct((PART, W), F32),
        compiler_params=params(8),
        cost_estimate=cost(4 * PART * W * W, 2 * W * W),
    )(*got, base_b, taken, factor_top)


def send(value, **by):
    return lax.ppermute(value, BOTH, shifted(**by))


def around(value, axis):
    return [value] + [send(value, **{axis: step}) for step in STEPS[1:]]


def on_device(
    trailing, rows_a, counts_a, factor_a, rows_b, counts_b, factor_b, factor_top, base_a, base_b
):
    place = jnp.stack([lax.axis_index("row"), lax.axis_index("col")]).astype(jnp.int32)
    lists = (rows_a, counts_a, rows_b, counts_b)
    part_a = lax.ppermute(prep_a(place, lists, factor_a), BOTH, spread_pairs())
    part_b = prep_b(place, lists, factor_a, factor_b, factor_top)
    part_b = lax.ppermute(part_b, BOTH, spread_pairs())
    a_own = jnp.stack(around(part_a, "dy"))
    b_own = jnp.stack(around(part_b, "dz"))
    a_down, a_up = send(a_own, dz=1), send(a_own, dz=-1)
    b_down, b_up = send(b_own, dy=1), send(b_own, dy=-1)
    trailing = hold(trailing, a_own)
    a_next, b_next, _ = lax.optimization_barrier((a_down, b_down, trailing))
    a_far, b_far = send(a_next[:2], dz=1), send(b_next[:2], dy=1)
    a_far_more, b_far_more = send(a_up[2:], dz=-1), send(b_up[2:], dy=-1)
    before = early_product(place, (a_down, a_up, b_own, b_down, b_up), trailing)
    slabs = []
    for half in range(2):
        keep, give = late_product(
            half, place, (a_own, a_far, a_far_more, b_far, b_far_more), trailing, before
        )
        own, one, two, three = pair_sum(place, keep, send(give, dc=1))
        slabs += [own, send(one, dx=1), send(two, dx=2), send(three, dx=-1)]
    columns, pieces = slots(place, lists, slabs, (factor_a, factor_b))
    near, other = send(columns, dx=1), send(columns, dx=-1)
    first, near, other = lax.optimization_barrier((around(pieces, "dy"), near, other))
    folded = fold(first)
    got = around(folded, "dz")
    far = send(lax.optimization_barrier((columns, folded))[0], dx=2)
    _, (own, near, other) = lax.optimization_barrier((got, (columns, near, other)))
    mates = [send(slab, dc=1) for slab in (own, near, other)]
    diag_a, top_b, sent = top_part(got, base_a, factor_top)
    far, _ = lax.optimization_barrier((far, sent))
    taken = lax.all_to_all(sent, "col", 0, 0)
    column_a, column_b = whole_columns(place, [own, near, other, far, *mates, send(far, dc=1)])
    base_b, _ = lax.optimization_barrier((base_b, column_a))
    diag_b = last_part(got, base_b, taken, factor_top)
    return (column_a, diag_a, column_b, top_b, diag_b)


def solution(mesh):
    in_specs = (
        P("row", "col"),
        P(),
        P(),
        P("row", None),
        P(),
        P(),
        P("row", None),
        P(),
        P("col", None),
        P("col", None),
    )
    out_specs = (P("row", None), P("col", None), P("row", None), P("col", None), P("col", None))
    return jax.shard_map(
        on_device, mesh=mesh, in_specs=in_specs, out_specs=out_specs, check_vma=False
    )
```

```python
import functools

import jax
import jax.numpy as jnp
from jax import lax
from jax.experimental import pallas as pl
from jax.experimental.pallas import tpu as pltpu
from jax.sharding import PartitionSpec as P

BS = 128
W = 512
NB = 12
ROWS = NB * BS
SIDE = 4
PART = 64
COLS = 8
STEPS = (0, 1, -1, 2)
STRIP = 2 * BS
PAIR = 2 * PART
BOTH = ("row", "col")
MIB = 1024 * 1024
BF = jnp.bfloat16
F32 = jnp.float32


def device(z, y, x, core):
    return ((z % SIDE) * SIDE + y % SIDE) * 8 + (x % SIDE) * 2 + core % 2


def all_places():
    return [
        (z, y, x, core)
        for z in range(SIDE)
        for y in range(SIDE)
        for x in range(SIDE)
        for core in range(2)
    ]


def shifted(dz=0, dy=0, dx=0, dc=0):
    return [
        (device(z, y, x, c), device(z + dz, y + dy, x + dx, c + dc))
        for z, y, x, c in all_places()
    ]


def spread_pairs():
    pairs = []
    for z, y, x, core in all_places():
        plane = (z * SIDE + y) % 8
        to = device(z + core, y + x, plane // 2, plane % 2)
        pairs.append((device(z, y, x, core), to))
    return pairs


def params(mib=24, **more):
    return pltpu.CompilerParams(vmem_limit_bytes=mib * MIB, **more)


def cost(flops, moved):
    return pl.CostEstimate(flops=flops, bytes_accessed=moved, transcendentals=0)


def whole(shape):
    return pl.BlockSpec(shape, lambda *_: (0,) * len(shape))


def find_slot(rows, counts, owner, block):
    slot = jnp.int32(0)
    live = jnp.int32(0)
    for k in range(NB):
        hit = (rows[owner, k] == block) & (k < counts[owner])
        slot = jnp.where(hit, k, slot)
        live = jnp.where(hit, 1, live)
    return slot, live


def half_of(value, upper):
    return jnp.where(upper > 0, value[PART:], value[:PART])


def prep_a_body(place, rows_a, counts_a, part_a, out_a):
    for block in range(NB):
        slot, live = find_slot(rows_a, counts_a, place[0], block)
        at = pl.ds(pl.multiple_of(slot * BS, BS), BS)
        piece = half_of(part_a[at, :].T, place[1] % 2)
        out_a[block] = jnp.where(live > 0, piece, jnp.zeros_like(piece))


def width_slice(rows):
    return pl.BlockSpec((rows, BS), lambda i, place, *_: (0, place[1] // 2))


def prep_a(place, lists, factor_a):
    return pl.pallas_call(
        prep_a_body,
        name="prep_a",
        grid_spec=pltpu.PrefetchScalarGridSpec(
            num_scalar_prefetch=3,
            grid=(1,),
            in_specs=[width_slice(ROWS)],
            out_specs=whole((NB, PART, BS)),
        ),
        out_shape=jax.ShapeDtypeStruct((NB, PART, BS), BF),
        compiler_params=params(56),
        cost_estimate=cost(0, 4 * ROWS * BS),
    )(place, *lists[:2], factor_a)


def prep_b_body(place, rows_a, counts_a, rows_b, counts_b, fa, part_b, top, out_b, fix):
    owner = place[0]
    upper = place[1] % 2
    fix[...] = lax.dot_general(
        top[...], fa[...], (((0,), (1,)), ((), ())), preferred_element_type=F32
    )
    for block in range(NB):
        slot_a, live_a = find_slot(rows_a, counts_a, owner, block)
        slot_b, live_b = find_slot(rows_b, counts_b, owner, block)
        at_a = pl.ds(pl.multiple_of(slot_a * BS, BS), BS)
        at_b = pl.ds(pl.multiple_of(slot_b * BS, BS), BS)
        moved = half_of(fix[:, at_a], upper)
        piece = half_of(part_b[at_b, :].T, upper).astype(F32)
        piece = jnp.where(live_b > 0, piece, jnp.zeros_like(piece))
        out_b[block] = (piece - jnp.where(live_a > 0, moved, jnp.zeros_like(moved))).astype(BF)


def prep_b(place, lists, factor_a, factor_b, factor_top):
    return pl.pallas_call(
        prep_b_body,
        name="prep_b",
        grid_spec=pltpu.PrefetchScalarGridSpec(
            num_scalar_prefetch=5,
            grid=(1,),
            in_specs=[whole((ROWS, W)), width_slice(ROWS), width_slice(W)],
            out_specs=whole((NB, PART, BS)),
            scratch_shapes=[pltpu.VMEM((BS, ROWS), F32)],
        ),
        out_shape=jax.ShapeDtypeStruct((NB, PART, BS), BF),
        compiler_params=params(56),
        cost_estimate=cost(2 * BS * ROWS * W, 2 * ROWS * (W + 4 * BS)),
    )(place, *lists, factor_a, factor_b, factor_top)


def where(place):
    z, y, plane = place[0] // SIDE, place[0] % SIDE, place[1]
    u = (z - plane // SIDE + SIDE) % SIDE
    v = (y - plane % SIDE + SIDE) % SIDE
    return u, v


def turn(value, by):
    return (value + by + SIDE) % SIDE


def load_a(copies, buf, u, spread, start=0, many=SIDE):
    for i in range(start, start + many):
        copies.append((buf.at[i - start], spread.at[:, u // 2, i * PART : (i + 1) * PART, :]))


def load_b(copies, buf, u, first, spread, start=0, many=SIDE):
    for i in range(start, start + many):
        ui = turn(u, -STEPS[i])
        at = pl.ds(pl.multiple_of(first + (ui % 2) * PART, PART), PART)
        copies.append((buf.at[i - start], spread.at[:, ui // 2, at, :]))


def run_copies(copies, sems):
    started = [pltpu.make_async_copy(a, b, sems.at[i]) for i, (a, b) in enumerate(copies)]
    for copy in started:
        copy.start()
    for copy in started:
        copy.wait()


def multiply(spread, tile):
    left = jnp.concatenate([spread[n, h] for n in range(NB) for h in range(2)], axis=1)
    return lax.dot_general(
        left, tile, (((1,), (1,)), ((), ())), preferred_element_type=F32
    ).astype(BF)


def hold_body(source, _, target, sem):
    copy = pltpu.make_async_copy(source, target, sem)
    copy.start()
    copy.wait()


def hold(trailing, after):
    return pl.pallas_call(
        hold_body,
        name="hold",
        in_specs=[pl.BlockSpec(memory_space=pltpu.HBM), pl.BlockSpec(memory_space=pl.ANY)],
        out_specs=pl.BlockSpec(memory_space=pltpu.VMEM),
        out_shape=pltpu.VMEM(trailing.shape, BF),
        scratch_shapes=[pltpu.SemaphoreType.DMA],
        compiler_params=params(8),
        cost_estimate=cost(0, 2 * trailing.size),
    )(trailing, after)


def rows_of(tile, step):
    return tile[pl.ds(pl.multiple_of(step * STRIP, STRIP), STRIP), :]


def half_multiply(spread, tile, step, h):
    rows = pl.ds(pl.multiple_of(step * STRIP, STRIP), STRIP)
    left = jnp.concatenate([spread[n] for n in range(NB)], axis=1)
    right = jnp.concatenate(
        [tile[rows, pl.ds(pl.multiple_of((2 * n + h) * BS, BS), BS)] for n in range(NB)], axis=1
    )
    return lax.dot_general(left, right, (((1,), (1,)), ((), ())), preferred_element_type=F32)


def load_half(copies, buf, spread, start=0, many=SIDE):
    for i in range(start, start + many):
        copies.append((buf.at[i - start], spread.at[:, i * PART : (i + 1) * PART, :]))


def own_body(place, a_own, b_own, tile, half_a, whole_b, spread_a, spread_b, sems):
    u, _ = where(place)

    @pl.when(pl.program_id(0) == 0)
    def _():
        copies = []
        load_half(copies, a_own, spread_a)
        load_b(copies, b_own, u, 0, spread_b)
        run_copies(copies, sems)

    half_a[...] = half_multiply(spread_a, tile, pl.program_id(0), u // 2)
    whole_b[...] = multiply(spread_b, rows_of(tile, pl.program_id(0)))


def own_product(place, a_own, b_own, trailing):
    deep = trailing.shape[1]
    return pl.pallas_call(
        own_body,
        name="own_product",
        grid_spec=pltpu.PrefetchScalarGridSpec(
            num_scalar_prefetch=1,
            grid=(ROWS // STRIP,),
            in_specs=[pl.BlockSpec(memory_space=pl.ANY)] * 2
            + [pl.BlockSpec(memory_space=pltpu.VMEM)],
            out_specs=[
                pl.BlockSpec((W // 2, STRIP), lambda i, *_: (0, i)),
                pl.BlockSpec((2 * PART, STRIP), lambda i, *_: (0, i)),
            ],
            scratch_shapes=[
                pltpu.VMEM((NB, W // 2, BS), BF),
                pltpu.VMEM((NB, 2, 2 * PART, BS), BF),
                pltpu.SemaphoreType.DMA((8,)),
            ],
        ),
        out_shape=[
            jax.ShapeDtypeStruct((W // 2, ROWS), F32),
            jax.ShapeDtypeStruct((2 * PART, ROWS), BF),
        ],
        compiler_params=params(20, dimension_semantics=("arbitrary",)),
        cost_estimate=cost(4 * PART * ROWS * deep + W // 2 * ROWS * deep, 8 * W * ROWS),
    )(place, a_own, b_own, trailing)


def early_body(place, a_down, a_up, b_down, b_up, tile, whole_b, out, spread, sems):
    u, v = where(place)

    @pl.when(pl.program_id(0) == 0)
    def _():
        copies = []
        load_a(copies, a_down, turn(u, -1), spread)
        load_a(copies, a_up, turn(u, 1), spread)
        for t, buf in enumerate((b_down, b_up)):
            load_b(copies, buf, u, W // 2 + 2 * t * PART, spread)
        run_copies(copies, sems)

    value = multiply(spread, rows_of(tile, pl.program_id(0)))
    for i, step in enumerate(STEPS):
        out[2 * turn(v, -step) + (u + 1) % 2, :PART, :] = value[i * PART : (i + 1) * PART]
    for j in range(4):
        to = 2 * turn(v, -STEPS[1 + j // 2]) + j % 2
        out[to, PART:, :] = value[W // 2 + j * PART : W // 2 + (j + 1) * PART]
    for j in range(2):
        out[2 * v + j, PART:, :] = whole_b[j * PART : (j + 1) * PART, :]


def early_product(place, bufs, trailing, whole_b):
    deep = trailing.shape[1]
    rows = W // 2 + 4 * PART
    return pl.pallas_call(
        early_body,
        name="early_product",
        grid_spec=pltpu.PrefetchScalarGridSpec(
            num_scalar_prefetch=1,
            grid=(ROWS // STRIP,),
            in_specs=[pl.BlockSpec(memory_space=pl.ANY)] * 4
            + [
                pl.BlockSpec(memory_space=pltpu.VMEM),
                pl.BlockSpec((2 * PART, STRIP), lambda i, *_: (0, i)),
            ],
            out_specs=pl.BlockSpec((COLS, PAIR, STRIP), lambda i, *_: (0, 0, i)),
            scratch_shapes=[
                pltpu.VMEM((NB, 2, rows, BS), BF),
                pltpu.SemaphoreType.DMA((16,)),
            ],
        ),
        out_shape=jax.ShapeDtypeStruct((COLS, PAIR, ROWS), BF),
        compiler_params=params(20, dimension_semantics=("arbitrary",)),
        cost_estimate=cost(2 * rows * ROWS * deep, 2 * rows * deep + 4 * W * ROWS),
    )(place, *bufs, trailing, whole_b)


def late_body(
    half, place, a_far, a_far_more, b_far, b_far_more, tile, before, half_a, keep, give, spread_a, spread_b, ready, sems
):
    u, v = where(place)
    core = place[1] % 2

    @pl.when(pl.program_id(0) == 0)
    def _():
        copies = []
        load_half(copies, a_far, spread_a, 0, 2)
        load_half(copies, a_far_more, spread_a, 2, 2)
        load_b(copies, b_far, u, 0, spread_b, 0, 2)
        load_b(copies, b_far_more, u, 0, spread_b, 2, 2)
        run_copies(copies, sems)

    ready[...] = before[...]
    step = half * HALF_STEPS + pl.program_id(0)
    value = half_multiply(spread_a, tile, step, turn(u, 2) // 2)
    value = (value + half_a[...]).astype(BF)
    for i, far in enumerate(STEPS):
        ready[2 * turn(v, -far) + u % 2, :PART, :] = value[i * PART : (i + 1) * PART]
    value = multiply(spread_b, rows_of(tile, step))
    for j in range(2):
        ready[2 * turn(v, 2) + j, PART:, :] = value[j * PART : (j + 1) * PART]
    for x in range(SIDE):
        keep[x] = ready[2 * x + core]
        give[x] = ready[2 * x + 1 - core]


HALF_STEPS = ROWS // STRIP // 2


def late_product(half, place, bufs, trailing, before, half_a):
    deep = trailing.shape[1]
    rows = W // 4 + 2 * PART
    out = jax.ShapeDtypeStruct((SIDE, PAIR, ROWS // 2), BF)
    spec = pl.BlockSpec((SIDE, PAIR, STRIP), lambda i, *_: (0, 0, i))
    return pl.pallas_call(
        functools.partial(late_body, half),
        name="late_product",
        grid_spec=pltpu.PrefetchScalarGridSpec(
            num_scalar_prefetch=1,
            grid=(HALF_STEPS,),
            in_specs=[pl.BlockSpec(memory_space=pl.ANY)] * 4
            + [
                pl.BlockSpec(memory_space=pltpu.VMEM),
                pl.BlockSpec((COLS, PAIR, STRIP), lambda i, *_: (0, 0, half * HALF_STEPS + i)),
                pl.BlockSpec((W // 2, STRIP), lambda i, *_: (0, half * HALF_STEPS + i)),
            ],
            out_specs=[spec, spec],
            scratch_shapes=[
                pltpu.VMEM((NB, W // 2, BS), BF),
                pltpu.VMEM((NB, 2, 2 * PART, BS), BF),
                pltpu.VMEM((COLS, PAIR, STRIP), BF),
                pltpu.SemaphoreType.DMA((8,)),
            ],
        ),
        out_shape=[out, out],
        compiler_params=params(20, dimension_semantics=("arbitrary",)),
        cost_estimate=cost(rows * ROWS * deep, 2 * rows * deep + 4 * W * ROWS),
    )(place, *bufs, trailing, before, half_a)


def pair_body(place, mine, taken, *outs):
    x = place[1] // 2
    for i in range(SIDE):
        at = (x + i) % SIDE
        outs[i][...] = (mine[at].astype(F32) + taken[at].astype(F32)).astype(BF)


def pair_sum(place, mine, taken):
    lanes = 3 * BS
    width = mine.shape[2]
    spec = pl.BlockSpec((SIDE, PAIR, lanes), lambda i, *_: (0, 0, i))
    return pl.pallas_call(
        pair_body,
        name="pair_sum",
        grid_spec=pltpu.PrefetchScalarGridSpec(
            num_scalar_prefetch=1,
            grid=(width // lanes,),
            in_specs=[spec, spec],
            out_specs=[pl.BlockSpec((PAIR, lanes), lambda i, *_: (0, i))] * SIDE,
        ),
        out_shape=[jax.ShapeDtypeStruct((PAIR, width), BF)] * SIDE,
        compiler_params=params(dimension_semantics=("arbitrary",)),
        cost_estimate=cost(W * width, 6 * W * width),
    )(place, mine, taken)


def slots_body(
    place, rows_a, counts_a, rows_b, counts_b, *refs
):
    slabs, (fa, fb, columns, pieces, natural, left) = refs[:8], refs[8:]
    owner = place[0]
    width = ROWS // 2
    for half in range(2):
        total = total_of(slabs[half * SIDE : (half + 1) * SIDE], slice(None))
        natural[:, half * width : (half + 1) * width] = (-total).astype(BF)
    for k in range(NB):
        at = slice(k * BS, (k + 1) * BS)
        block = natural[:PART, pl.ds(pl.multiple_of(rows_a[owner, k] * BS, BS), BS)]
        columns[:PART, at] = jnp.where(k < counts_a[owner], block, jnp.zeros_like(block))
        block = natural[:, pl.ds(pl.multiple_of(rows_b[owner, k] * BS, BS), BS)]
        block = jnp.where(k < counts_b[owner], block, jnp.zeros_like(block))
        left[:, at] = block
        columns[PART:, at] = block[PART:]
    one = jnp.dot(columns[:PART, :], fa[...], preferred_element_type=F32)
    two = jnp.dot(left[...], fb[...], preferred_element_type=F32)
    pieces[:PART, :] = one.astype(BF)
    pieces[PART:, :] = two.astype(BF)


def slots(place, lists, slabs, factors):
    return pl.pallas_call(
        slots_body,
        name="slots",
        grid_spec=pltpu.PrefetchScalarGridSpec(
            num_scalar_prefetch=5,
            grid=(1,),
            in_specs=[whole((PAIR, ROWS // 2))] * 8 + [whole((ROWS, W))] * 2,
            out_specs=[whole((PAIR, ROWS)), whole((3 * PART, W))],
            scratch_shapes=[pltpu.VMEM((PAIR, ROWS), BF)] * 2,
        ),
        out_shape=[
            jax.ShapeDtypeStruct((PAIR, ROWS), BF),
            jax.ShapeDtypeStruct((3 * PART, W), BF),
        ],
        compiler_params=params(),
        cost_estimate=cost(6 * PART * ROWS * W, 4 * ROWS * W + 10 * PAIR * ROWS),
    )(place, *lists, *slabs, *factors)


def column_body(place, *refs):
    slabs, column_a, column_b, wide = refs[:8], refs[8], refs[9], refs[10]
    core, x = place[1] % 2, place[1] // 2
    for i in range(8):
        at = 2 * turn(x, -STEPS[i % SIDE]) + (core if i < SIDE else 1 - core)
        wide[at] = slabs[i][...]
    for first, out in ((0, column_a), (PART, column_b)):
        out[...] = wide[:, first : first + PART, :].reshape(W, wide.shape[2]).T


def whole_columns(place, slabs):
    lanes = 4 * BS
    out = jax.ShapeDtypeStruct((ROWS, W), BF)
    return pl.pallas_call(
        column_body,
        name="whole_columns",
        grid_spec=pltpu.PrefetchScalarGridSpec(
            num_scalar_prefetch=1,
            grid=(ROWS // lanes,),
            in_specs=[pl.BlockSpec((PAIR, lanes), lambda i, *_: (0, i))] * 8,
            out_specs=[pl.BlockSpec((lanes, W), lambda i, *_: (i, 0))] * 2,
            scratch_shapes=[pltpu.VMEM((COLS, PAIR, lanes), BF)],
        ),
        out_shape=[out, out],
        compiler_params=params(dimension_semantics=("arbitrary",)),
        cost_estimate=cost(0, 8 * ROWS * W),
    )(place, *slabs)


def total_of(refs, rows):
    parts = [ref[rows, :].astype(F32) for ref in refs]
    return (parts[0] + parts[1]) + (parts[2] + parts[3])


def fold_body(one, two, three, four, out):
    out[...] = total_of((one, two, three, four), slice(None)).astype(BF)


def fold(parts):
    return pl.pallas_call(
        fold_body,
        name="fold",
        out_shape=jax.ShapeDtypeStruct(parts[0].shape, BF),
        compiler_params=params(8),
        cost_estimate=cost(4 * parts[0].size, 10 * parts[0].size),
    )(*parts)


def top_body(one, two, three, four, base, top, diag_a, top_b, sent):
    got = (one, two, three, four)
    value = base[...] - total_of(got, slice(0, PART))
    diag_a[...] = value
    total = total_of(got, slice(PART, 2 * PART))
    for _ in range(3):
        part = value.astype(BF)
        value = value - part.astype(F32)
        total = total + jnp.dot(part, top[...], preferred_element_type=F32)
    total = (-total).astype(BF)
    top_b[...] = total
    for c in range(COLS):
        sent[c] = jnp.concatenate([total[:, c * PART : (c + 1) * PART]] * 2, axis=1)


def top_part(got, base_a, factor_top):
    return pl.pallas_call(
        top_body,
        name="top_part",
        out_shape=[
            jax.ShapeDtypeStruct((PART, W), F32),
            jax.ShapeDtypeStruct((PART, W), BF),
            jax.ShapeDtypeStruct((COLS, PART, 2 * PART), BF),
        ],
        compiler_params=params(8),
        cost_estimate=cost(6 * PART * W * W, 2 * W * W),
    )(*got, base_a, factor_top)


def last_body(one, two, three, four, base, taken, top, diag_b):
    across = taken[...].reshape(W, 2 * PART)
    cross = lax.dot_general(
        across, top[...], (((0,), (0,)), ((), ())), preferred_element_type=F32
    )
    total = total_of((one, two, three, four), slice(2 * PART, 3 * PART))
    diag_b[...] = base[...] - total - cross[:PART]


def last_part(got, base_b, taken, factor_top):
    return pl.pallas_call(
        last_body,
        name="last_part",
        out_shape=jax.ShapeDtypeStruct((PART, W), F32),
        compiler_params=params(8),
        cost_estimate=cost(4 * PART * W * W, 2 * W * W),
    )(*got, base_b, taken, factor_top)


def send(value, **by):
    return lax.ppermute(value, BOTH, shifted(**by))


def around(value, axis):
    return [value] + [send(value, **{axis: step}) for step in STEPS[1:]]


def on_device(
    trailing, rows_a, counts_a, factor_a, rows_b, counts_b, factor_b, factor_top, base_a, base_b
):
    place = jnp.stack([lax.axis_index("row"), lax.axis_index("col")]).astype(jnp.int32)
    lists = (rows_a, counts_a, rows_b, counts_b)
    part_a = lax.ppermute(prep_a(place, lists, factor_a), BOTH, spread_pairs())
    part_b = prep_b(place, lists, factor_a, factor_b, factor_top)
    part_b, _ = lax.optimization_barrier((part_b, part_a))
    part_b = lax.ppermute(part_b, BOTH, spread_pairs())
    a_own = jnp.stack(around(part_a, "dy"))
    b_own = jnp.stack(around(part_b, "dz"))
    a_down, a_up = send(a_own, dz=1), send(a_own, dz=-1)
    b_down, b_up = send(b_own, dy=1), send(b_own, dy=-1)
    trailing = hold(trailing, a_own)
    half_a, whole_b = own_product(place, a_own, b_own, trailing)
    a_next, b_next, _ = lax.optimization_barrier((a_down, b_down, half_a))
    a_far, b_far = send(a_next[:2], dz=1), send(b_next[:2], dy=1)
    a_far_more, b_far_more = send(a_up[2:], dz=-1), send(b_up[2:], dy=-1)
    before = early_product(place, (a_down, a_up, b_down, b_up), trailing, whole_b)
    slabs = []
    for half in range(2):
        keep, give = late_product(
            half, place, (a_far, a_far_more, b_far, b_far_more), trailing, before, half_a
        )
        own, one, two, three = pair_sum(place, keep, send(give, dc=1))
        slabs += [own, send(one, dx=1), send(two, dx=2), send(three, dx=-1)]
    columns, pieces = slots(place, lists, slabs, (factor_a, factor_b))
    near, other = send(columns, dx=1), send(columns, dx=-1)
    first, near, other = lax.optimization_barrier((around(pieces, "dy"), near, other))
    folded = fold(first)
    got = around(folded, "dz")
    far = send(lax.optimization_barrier((columns, folded))[0], dx=2)
    _, (own, near, other) = lax.optimization_barrier((got, (columns, near, other)))
    mates = [send(slab, dc=1) for slab in (own, near, other)]
    diag_a, top_b, sent = top_part(got, base_a, factor_top)
    far, _ = lax.optimization_barrier((far, sent))
    taken = lax.all_to_all(sent, "col", 0, 0)
    column_a, column_b = whole_columns(place, [own, near, other, far, *mates, send(far, dc=1)])
    base_b, _ = lax.optimization_barrier((base_b, column_a))
    diag_b = last_part(got, base_b, taken, factor_top)
    return (column_a, diag_a, column_b, top_b, diag_b)


def solution(mesh):
    in_specs = (
        P("row", "col"),
        P(),
        P(),
        P("row", None),
        P(),
        P(),
        P("row", None),
        P(),
        P("col", None),
        P("col", None),
    )
    out_specs = (P("row", None), P("col", None), P("row", None), P("col", None), P("col", None))
    return jax.shard_map(
        on_device, mesh=mesh, in_specs=in_specs, out_specs=out_specs, check_vma=False
    )
```

```python
import functools

import jax
import jax.numpy as jnp
from jax import lax
from jax.experimental import pallas as pl
from jax.experimental.pallas import tpu as pltpu
from jax.sharding import PartitionSpec as P

BS = 128
W = 512
NB = 12
ROWS = NB * BS
SIDE = 4
PART = 64
COLS = 8
STEPS = (0, 1, -1, 2)
PAIR = 2 * PART
BOTH = ("row", "col")
MIB = 1024 * 1024
BF = jnp.bfloat16
F32 = jnp.float32


def device(z, y, x, core):
    return ((z % SIDE) * SIDE + y % SIDE) * 8 + (x % SIDE) * 2 + core % 2


def all_places():
    return [
        (z, y, x, core)
        for z in range(SIDE)
        for y in range(SIDE)
        for x in range(SIDE)
        for core in range(2)
    ]


def shifted(dz=0, dy=0, dx=0, dc=0):
    return [
        (device(z, y, x, c), device(z + dz, y + dy, x + dx, c + dc))
        for z, y, x, c in all_places()
    ]


def spread_pairs():
    pairs = []
    for z, y, x, core in all_places():
        plane = (z * SIDE + y) % 8
        to = device(z + core, y + x, plane // 2, plane % 2)
        pairs.append((device(z, y, x, core), to))
    return pairs


def params(mib=24, **more):
    return pltpu.CompilerParams(vmem_limit_bytes=mib * MIB, **more)


def cost(flops, moved):
    return pl.CostEstimate(flops=flops, bytes_accessed=moved, transcendentals=0)


def whole(shape):
    return pl.BlockSpec(shape, lambda *_: (0,) * len(shape))


def find_slot(rows, counts, owner, block):
    slot = jnp.int32(0)
    live = jnp.int32(0)
    for k in range(NB):
        hit = (rows[owner, k] == block) & (k < counts[owner])
        slot = jnp.where(hit, k, slot)
        live = jnp.where(hit, 1, live)
    return slot, live


def half_of(value, upper):
    return jnp.where(upper > 0, value[PART:], value[:PART])


def prep_a_body(place, rows_a, counts_a, part_a, out_a):
    for block in range(NB):
        slot, live = find_slot(rows_a, counts_a, place[0], block)
        at = pl.ds(pl.multiple_of(slot * BS, BS), BS)
        piece = half_of(part_a[at, :].T, place[1] % 2)
        out_a[block] = jnp.where(live > 0, piece, jnp.zeros_like(piece))


def width_slice(rows):
    return pl.BlockSpec((rows, BS), lambda i, place, *_: (0, place[1] // 2))


def prep_a(place, lists, factor_a):
    return pl.pallas_call(
        prep_a_body,
        name="prep_a",
        grid_spec=pltpu.PrefetchScalarGridSpec(
            num_scalar_prefetch=3,
            grid=(1,),
            in_specs=[width_slice(ROWS)],
            out_specs=whole((NB, PART, BS)),
        ),
        out_shape=jax.ShapeDtypeStruct((NB, PART, BS), BF),
        compiler_params=params(56),
        cost_estimate=cost(0, 4 * ROWS * BS),
    )(place, *lists[:2], factor_a)


def prep_b_body(place, rows_a, counts_a, rows_b, counts_b, fa, part_b, top, out_b, fix):
    owner = place[0]
    upper = place[1] % 2
    fix[...] = lax.dot_general(
        top[...], fa[...], (((0,), (1,)), ((), ())), preferred_element_type=F32
    )
    for block in range(NB):
        slot_a, live_a = find_slot(rows_a, counts_a, owner, block)
        slot_b, live_b = find_slot(rows_b, counts_b, owner, block)
        at_a = pl.ds(pl.multiple_of(slot_a * BS, BS), BS)
        at_b = pl.ds(pl.multiple_of(slot_b * BS, BS), BS)
        moved = half_of(fix[:, at_a], upper)
        piece = half_of(part_b[at_b, :].T, upper).astype(F32)
        piece = jnp.where(live_b > 0, piece, jnp.zeros_like(piece))
        out_b[block] = (piece - jnp.where(live_a > 0, moved, jnp.zeros_like(moved))).astype(BF)


def prep_b(place, lists, factor_a, factor_b, factor_top):
    return pl.pallas_call(
        prep_b_body,
        name="prep_b",
        grid_spec=pltpu.PrefetchScalarGridSpec(
            num_scalar_prefetch=5,
            grid=(1,),
            in_specs=[whole((ROWS, W)), width_slice(ROWS), width_slice(W)],
            out_specs=whole((NB, PART, BS)),
            scratch_shapes=[pltpu.VMEM((BS, ROWS), F32)],
        ),
        out_shape=jax.ShapeDtypeStruct((NB, PART, BS), BF),
        compiler_params=params(56),
        cost_estimate=cost(2 * BS * ROWS * W, 2 * ROWS * (W + 4 * BS)),
    )(place, *lists, factor_a, factor_b, factor_top)


def where(place):
    z, y, plane = place[0] // SIDE, place[0] % SIDE, place[1]
    u = (z - plane // SIDE + SIDE) % SIDE
    v = (y - plane % SIDE + SIDE) % SIDE
    return u, v


def turn(value, by):
    return (value + by + SIDE) % SIDE


def load_b(copies, buf, u, first, spread, start=0, many=SIDE):
    for i in range(start, start + many):
        ui = turn(u, -STEPS[i])
        at = pl.ds(pl.multiple_of(first + (ui % 2) * PART, PART), PART)
        copies.append((buf.at[i - start], spread.at[:, ui // 2, at, :]))


def copies_of(copies, sems):
    return [pltpu.make_async_copy(a, b, sems.at[i]) for i, (a, b) in enumerate(copies)]


def multiply(spread, tile):
    left = jnp.concatenate([spread[n, h] for n in range(NB) for h in range(2)], axis=1)
    return lax.dot_general(
        left, tile, (((1,), (1,)), ((), ())), preferred_element_type=F32
    ).astype(BF)


def hold_body(source, _, target, sem):
    copy = pltpu.make_async_copy(source, target, sem)
    copy.start()
    copy.wait()


def hold(trailing, after):
    return pl.pallas_call(
        hold_body,
        name="hold",
        in_specs=[pl.BlockSpec(memory_space=pltpu.HBM), pl.BlockSpec(memory_space=pl.ANY)],
        out_specs=pl.BlockSpec(memory_space=pltpu.VMEM),
        out_shape=pltpu.VMEM(trailing.shape, BF),
        scratch_shapes=[pltpu.SemaphoreType.DMA],
        compiler_params=params(8),
        cost_estimate=cost(0, 2 * trailing.size),
    )(trailing, after)


def multiply_half(members, tile, strip, step, h):
    rows = pl.ds(pl.multiple_of(step * strip, strip), strip)
    left = jnp.concatenate(
        [jnp.concatenate([member[n] for member in members], axis=0) for n in range(NB)], axis=1
    )
    right = jnp.concatenate(
        [tile[rows, pl.ds(pl.multiple_of((2 * n + h) * BS, BS), BS)] for n in range(NB)], axis=1
    )
    return lax.dot_general(left, right, (((1,), (1,)), ((), ())), preferred_element_type=F32)


def members_of(*lists):
    return [part.at[i] for part in lists for i in range(part.shape[0])]


def on_first(action):
    pl.when(pl.program_id(0) == 0)(action)


def start_all(copies):
    for copy in copies:
        copy.start()


def wait_all(copies):
    for copy in copies:
        copy.wait()


def rows_of(tile, strip, step):
    return tile[pl.ds(pl.multiple_of(step * strip, strip), strip), :]


IN_VMEM = pl.BlockSpec(memory_space=pltpu.VMEM)
ANYWHERE = pl.BlockSpec(memory_space=pl.ANY)
WIDE = 4 * BS
NARROW = 3 * BS
HALF_STEPS = ROWS // NARROW // 2


def own_body(place, a_own, b_own, tile, half_a, whole_b, spread, sems):
    u, _ = where(place)
    step = pl.program_id(0)
    pairs = []
    load_b(pairs, b_own, u, 0, spread)
    copies = copies_of(pairs, sems)
    on_first(lambda: start_all(copies))
    half_a[...] = multiply_half(members_of(a_own), tile, WIDE, step, u // 2)
    on_first(lambda: wait_all(copies))
    whole_b[...] = multiply(spread, rows_of(tile, WIDE, step))


def own_product(place, a_own, b_own, trailing):
    deep = trailing.shape[1]
    return pl.pallas_call(
        own_body,
        name="own_product",
        grid_spec=pltpu.PrefetchScalarGridSpec(
            num_scalar_prefetch=1,
            grid=(ROWS // WIDE,),
            in_specs=[IN_VMEM, ANYWHERE, IN_VMEM],
            out_specs=[
                pl.BlockSpec((W // 2, WIDE), lambda i, *_: (0, i)),
                pl.BlockSpec((2 * PART, WIDE), lambda i, *_: (0, i)),
            ],
            scratch_shapes=[
                pltpu.VMEM((NB, 2, 2 * PART, BS), BF),
                pltpu.SemaphoreType.DMA((4,)),
            ],
        ),
        out_shape=[
            jax.ShapeDtypeStruct((W // 2, ROWS), F32),
            jax.ShapeDtypeStruct((2 * PART, ROWS), BF),
        ],
        compiler_params=params(20, dimension_semantics=("arbitrary",)),
        cost_estimate=cost(4 * PART * ROWS * deep + W // 2 * ROWS * deep, 8 * W * ROWS),
    )(place, a_own, b_own, trailing)


def early_body(place, a_down, a_up, b_down, b_up, tile, whole_b, out, spread, sems):
    u, v = where(place)
    step = pl.program_id(0)
    pairs = []
    load_b(pairs, b_down, u, 0, spread)
    load_b(pairs, b_up, u, 2 * PART, spread)
    copies = copies_of(pairs, sems)
    on_first(lambda: start_all(copies))
    value = multiply_half(members_of(a_down), tile, WIDE, step, turn(u, -1) // 2)
    value = value + multiply_half(members_of(a_up), tile, WIDE, step, turn(u, 1) // 2)
    value = value.astype(BF)
    for i, far in enumerate(STEPS):
        out[2 * turn(v, -far) + (u + 1) % 2, :PART, :] = value[i * PART : (i + 1) * PART]
    on_first(lambda: wait_all(copies))
    value = multiply(spread, rows_of(tile, WIDE, step))
    for j in range(4):
        to = 2 * turn(v, -STEPS[1 + j // 2]) + j % 2
        out[to, PART:, :] = value[j * PART : (j + 1) * PART]
    for j in range(2):
        out[2 * v + j, PART:, :] = whole_b[j * PART : (j + 1) * PART, :]


def early_product(place, bufs, trailing, whole_b):
    deep = trailing.shape[1]
    rows = W // 2 + 4 * PART
    return pl.pallas_call(
        early_body,
        name="early_product",
        grid_spec=pltpu.PrefetchScalarGridSpec(
            num_scalar_prefetch=1,
            grid=(ROWS // WIDE,),
            in_specs=[IN_VMEM] * 2
            + [ANYWHERE] * 2
            + [IN_VMEM, pl.BlockSpec((2 * PART, WIDE), lambda i, *_: (0, i))],
            out_specs=pl.BlockSpec((COLS, PAIR, WIDE), lambda i, *_: (0, 0, i)),
            scratch_shapes=[
                pltpu.VMEM((NB, 2, 4 * PART, BS), BF),
                pltpu.SemaphoreType.DMA((8,)),
            ],
        ),
        out_shape=jax.ShapeDtypeStruct((COLS, PAIR, ROWS), BF),
        compiler_params=params(20, dimension_semantics=("arbitrary",)),
        cost_estimate=cost(2 * rows * ROWS * deep, 2 * rows * deep + 4 * W * ROWS),
    )(place, *bufs, trailing, whole_b)


def late_body(
    half, place, a_far, a_more, b_far, b_more, tile, before, half_a, keep, give, spread, ready, sems
):
    u, v = where(place)
    core = place[1] % 2
    step = half * HALF_STEPS + pl.program_id(0)
    pairs = []
    load_b(pairs, b_far, u, 0, spread, 0, 2)
    load_b(pairs, b_more, u, 0, spread, 2, 2)
    copies = copies_of(pairs, sems)
    on_first(lambda: start_all(copies))
    ready[...] = before[...]
    value = multiply_half(members_of(a_far, a_more), tile, NARROW, step, turn(u, 2) // 2)
    value = (value + half_a[...]).astype(BF)
    for i, far in enumerate(STEPS):
        ready[2 * turn(v, -far) + u % 2, :PART, :] = value[i * PART : (i + 1) * PART]
    on_first(lambda: wait_all(copies))
    value = multiply(spread, rows_of(tile, NARROW, step))
    for j in range(2):
        ready[2 * turn(v, 2) + j, PART:, :] = value[j * PART : (j + 1) * PART]
    for x in range(SIDE):
        keep[x] = ready[2 * x + core]
        give[x] = ready[2 * x + 1 - core]


def late_product(half, place, bufs, trailing, before, half_a):
    deep = trailing.shape[1]
    rows = W // 4 + 2 * PART
    out = jax.ShapeDtypeStruct((SIDE, PAIR, ROWS // 2), BF)
    spec = pl.BlockSpec((SIDE, PAIR, NARROW), lambda i, *_: (0, 0, i))
    return pl.pallas_call(
        functools.partial(late_body, half),
        name="late_product",
        grid_spec=pltpu.PrefetchScalarGridSpec(
            num_scalar_prefetch=1,
            grid=(HALF_STEPS,),
            in_specs=[IN_VMEM] * 2
            + [ANYWHERE] * 2
            + [
                IN_VMEM,
                pl.BlockSpec((COLS, PAIR, NARROW), lambda i, *_: (0, 0, half * HALF_STEPS + i)),
                pl.BlockSpec((W // 2, NARROW), lambda i, *_: (0, half * HALF_STEPS + i)),
            ],
            out_specs=[spec, spec],
            scratch_shapes=[
                pltpu.VMEM((NB, 2, 2 * PART, BS), BF),
                pltpu.VMEM((COLS, PAIR, NARROW), BF),
                pltpu.SemaphoreType.DMA((4,)),
            ],
        ),
        out_shape=[out, out],
        compiler_params=params(20, dimension_semantics=("arbitrary",)),
        cost_estimate=cost(rows * ROWS * deep, 2 * rows * deep + 4 * W * ROWS),
    )(place, *bufs, trailing, before, half_a)


def pair_body(place, mine, taken, *outs):
    x = place[1] // 2
    for i in range(SIDE):
        at = (x + i) % SIDE
        outs[i][...] = (mine[at].astype(F32) + taken[at].astype(F32)).astype(BF)


def pair_sum(place, mine, taken):
    lanes = 3 * BS
    width = mine.shape[2]
    spec = pl.BlockSpec((SIDE, PAIR, lanes), lambda i, *_: (0, 0, i))
    return pl.pallas_call(
        pair_body,
        name="pair_sum",
        grid_spec=pltpu.PrefetchScalarGridSpec(
            num_scalar_prefetch=1,
            grid=(width // lanes,),
            in_specs=[spec, spec],
            out_specs=[pl.BlockSpec((PAIR, lanes), lambda i, *_: (0, i))] * SIDE,
        ),
        out_shape=[jax.ShapeDtypeStruct((PAIR, width), BF)] * SIDE,
        compiler_params=params(dimension_semantics=("arbitrary",)),
        cost_estimate=cost(W * width, 6 * W * width),
    )(place, mine, taken)


def slots_body(
    place, rows_a, counts_a, rows_b, counts_b, *refs
):
    slabs, (fa, fb, columns, pieces, natural, left) = refs[:8], refs[8:]
    owner = place[0]
    width = ROWS // 2
    for half in range(2):
        total = total_of(slabs[half * SIDE : (half + 1) * SIDE], slice(None))
        natural[:, half * width : (half + 1) * width] = (-total).astype(BF)
    for k in range(NB):
        at = slice(k * BS, (k + 1) * BS)
        block = natural[:PART, pl.ds(pl.multiple_of(rows_a[owner, k] * BS, BS), BS)]
        columns[:PART, at] = jnp.where(k < counts_a[owner], block, jnp.zeros_like(block))
        block = natural[:, pl.ds(pl.multiple_of(rows_b[owner, k] * BS, BS), BS)]
        block = jnp.where(k < counts_b[owner], block, jnp.zeros_like(block))
        left[:, at] = block
        columns[PART:, at] = block[PART:]
    one = jnp.dot(columns[:PART, :], fa[...], preferred_element_type=F32)
    two = jnp.dot(left[...], fb[...], preferred_element_type=F32)
    pieces[:PART, :] = one.astype(BF)
    pieces[PART:, :] = two.astype(BF)


def slots(place, lists, slabs, factors):
    return pl.pallas_call(
        slots_body,
        name="slots",
        grid_spec=pltpu.PrefetchScalarGridSpec(
            num_scalar_prefetch=5,
            grid=(1,),
            in_specs=[whole((PAIR, ROWS // 2))] * 8 + [whole((ROWS, W))] * 2,
            out_specs=[whole((PAIR, ROWS)), whole((3 * PART, W))],
            scratch_shapes=[pltpu.VMEM((PAIR, ROWS), BF)] * 2,
        ),
        out_shape=[
            jax.ShapeDtypeStruct((PAIR, ROWS), BF),
            jax.ShapeDtypeStruct((3 * PART, W), BF),
        ],
        compiler_params=params(),
        cost_estimate=cost(6 * PART * ROWS * W, 4 * ROWS * W + 10 * PAIR * ROWS),
    )(place, *lists, *slabs, *factors)


def column_body(place, *refs):
    slabs, column_a, column_b, wide = refs[:8], refs[8], refs[9], refs[10]
    core, x = place[1] % 2, place[1] // 2
    for i in range(8):
        at = 2 * turn(x, -STEPS[i % SIDE]) + (core if i < SIDE else 1 - core)
        wide[at] = slabs[i][...]
    for first, out in ((0, column_a), (PART, column_b)):
        out[...] = wide[:, first : first + PART, :].reshape(W, wide.shape[2]).T


def whole_columns(place, slabs):
    lanes = 4 * BS
    out = jax.ShapeDtypeStruct((ROWS, W), BF)
    return pl.pallas_call(
        column_body,
        name="whole_columns",
        grid_spec=pltpu.PrefetchScalarGridSpec(
            num_scalar_prefetch=1,
            grid=(ROWS // lanes,),
            in_specs=[pl.BlockSpec((PAIR, lanes), lambda i, *_: (0, i))] * 8,
            out_specs=[pl.BlockSpec((lanes, W), lambda i, *_: (i, 0))] * 2,
            scratch_shapes=[pltpu.VMEM((COLS, PAIR, lanes), BF)],
        ),
        out_shape=[out, out],
        compiler_params=params(dimension_semantics=("arbitrary",)),
        cost_estimate=cost(0, 8 * ROWS * W),
    )(place, *slabs)


def total_of(refs, rows):
    parts = [ref[rows, :].astype(F32) for ref in refs]
    return (parts[0] + parts[1]) + (parts[2] + parts[3])


def fold_body(one, two, three, four, out):
    out[...] = total_of((one, two, three, four), slice(None)).astype(BF)


def fold(parts):
    return pl.pallas_call(
        fold_body,
        name="fold",
        out_shape=jax.ShapeDtypeStruct(parts[0].shape, BF),
        compiler_params=params(8),
        cost_estimate=cost(4 * parts[0].size, 10 * parts[0].size),
    )(*parts)


def top_body(one, two, three, four, base, top, diag_a, top_b, sent):
    got = (one, two, three, four)
    value = base[...] - total_of(got, slice(0, PART))
    diag_a[...] = value
    total = total_of(got, slice(PART, 2 * PART))
    for _ in range(3):
        part = value.astype(BF)
        value = value - part.astype(F32)
        total = total + jnp.dot(part, top[...], preferred_element_type=F32)
    total = (-total).astype(BF)
    top_b[...] = total
    for c in range(COLS):
        sent[c] = jnp.concatenate([total[:, c * PART : (c + 1) * PART]] * 2, axis=1)


def top_part(got, base_a, factor_top):
    return pl.pallas_call(
        top_body,
        name="top_part",
        out_shape=[
            jax.ShapeDtypeStruct((PART, W), F32),
            jax.ShapeDtypeStruct((PART, W), BF),
            jax.ShapeDtypeStruct((COLS, PART, 2 * PART), BF),
        ],
        compiler_params=params(8),
        cost_estimate=cost(6 * PART * W * W, 2 * W * W),
    )(*got, base_a, factor_top)


def last_body(one, two, three, four, base, taken, top, diag_b):
    across = taken[...].reshape(W, 2 * PART)
    cross = lax.dot_general(
        across, top[...], (((0,), (0,)), ((), ())), preferred_element_type=F32
    )
    total = total_of((one, two, three, four), slice(2 * PART, 3 * PART))
    diag_b[...] = base[...] - total - cross[:PART]


def last_part(got, base_b, taken, factor_top):
    return pl.pallas_call(
        last_body,
        name="last_part",
        out_shape=jax.ShapeDtypeStruct((PART, W), F32),
        compiler_params=params(8),
        cost_estimate=cost(4 * PART * W * W, 2 * W * W),
    )(*got, base_b, taken, factor_top)


def send(value, **by):
    return lax.ppermute(value, BOTH, shifted(**by))


def around(value, axis):
    return [value] + [send(value, **{axis: step}) for step in STEPS[1:]]


def on_device(
    trailing, rows_a, counts_a, factor_a, rows_b, counts_b, factor_b, factor_top, base_a, base_b
):
    place = jnp.stack([lax.axis_index("row"), lax.axis_index("col")]).astype(jnp.int32)
    lists = (rows_a, counts_a, rows_b, counts_b)
    part_a = lax.ppermute(prep_a(place, lists, factor_a), BOTH, spread_pairs())
    part_b = prep_b(place, lists, factor_a, factor_b, factor_top)
    part_b = lax.ppermute(part_b, BOTH, spread_pairs())
    a_own = jnp.stack(around(part_a, "dy"))
    b_own = jnp.stack(around(part_b, "dz"))
    a_down, a_up = send(a_own, dz=1), send(a_own, dz=-1)
    b_down, b_up = send(b_own, dy=1), send(b_own, dy=-1)
    trailing = hold(trailing, a_own)
    half_a, whole_b = own_product(place, a_own, b_own, trailing)
    a_next, b_next, _ = lax.optimization_barrier((a_down, b_down, half_a))
    a_far, b_far = send(a_next[:2], dz=1), send(b_next[:2], dy=1)
    a_far_more, b_far_more = send(a_up[2:], dz=-1), send(b_up[2:], dy=-1)
    before = early_product(place, (a_down, a_up, b_down, b_up), trailing, whole_b)
    slabs = []
    for half in range(2):
        keep, give = late_product(
            half, place, (a_far, a_far_more, b_far, b_far_more), trailing, before, half_a
        )
        own, one, two, three = pair_sum(place, keep, send(give, dc=1))
        slabs += [own, send(one, dx=1), send(two, dx=2), send(three, dx=-1)]
    columns, pieces = slots(place, lists, slabs, (factor_a, factor_b))
    near, other = send(columns, dx=1), send(columns, dx=-1)
    first, near, other = lax.optimization_barrier((around(pieces, "dy"), near, other))
    folded = fold(first)
    got = around(folded, "dz")
    far = send(lax.optimization_barrier((columns, folded))[0], dx=2)
    _, (own, near, other) = lax.optimization_barrier((got, (columns, near, other)))
    mates = [send(slab, dc=1) for slab in (own, near, other)]
    diag_a, top_b, sent = top_part(got, base_a, factor_top)
    far, _ = lax.optimization_barrier((far, sent))
    taken = lax.all_to_all(sent, "col", 0, 0)
    column_a, column_b = whole_columns(place, [own, near, other, far, *mates, send(far, dc=1)])
    base_b, _ = lax.optimization_barrier((base_b, column_a))
    diag_b = last_part(got, base_b, taken, factor_top)
    return (column_a, diag_a, column_b, top_b, diag_b)


def solution(mesh):
    in_specs = (
        P("row", "col"),
        P(),
        P(),
        P("row", None),
        P(),
        P(),
        P("row", None),
        P(),
        P("col", None),
        P("col", None),
    )
    out_specs = (P("row", None), P("col", None), P("row", None), P("col", None), P("col", None))
    return jax.shard_map(
        on_device, mesh=mesh, in_specs=in_specs, out_specs=out_specs, check_vma=False
    )
```

```python
import functools

import jax
import jax.numpy as jnp
from jax import lax
from jax.experimental import pallas as pl
from jax.experimental.pallas import tpu as pltpu
from jax.sharding import PartitionSpec as P

BS = 128
W = 512
NB = 12
ROWS = NB * BS
SIDE = 4
PART = 64
COLS = 8
STEPS = (0, 2, 1, -1)
STRIP = 2 * BS
PAIR = 2 * PART
BOTH = ("row", "col")
MIB = 1024 * 1024
BF = jnp.bfloat16
F32 = jnp.float32


def device(z, y, x, core):
    return ((z % SIDE) * SIDE + y % SIDE) * 8 + (x % SIDE) * 2 + core % 2


def all_places():
    return [
        (z, y, x, core)
        for z in range(SIDE)
        for y in range(SIDE)
        for x in range(SIDE)
        for core in range(2)
    ]


def shifted(dz=0, dy=0, dx=0, dc=0):
    return [
        (device(z, y, x, c), device(z + dz, y + dy, x + dx, c + dc))
        for z, y, x, c in all_places()
    ]


def spread_pairs():
    pairs = []
    for z, y, x, core in all_places():
        plane = (z * SIDE + y) % 8
        to = device(z + core, y + x, plane // 2, plane % 2)
        pairs.append((device(z, y, x, core), to))
    return pairs


def params(mib=24, **more):
    return pltpu.CompilerParams(vmem_limit_bytes=mib * MIB, **more)


def cost(flops, moved):
    return pl.CostEstimate(flops=flops, bytes_accessed=moved, transcendentals=0)


def whole(shape):
    return pl.BlockSpec(shape, lambda *_: (0,) * len(shape))


def find_slot(rows, counts, owner, block):
    slot = jnp.int32(0)
    live = jnp.int32(0)
    for k in range(NB):
        hit = (rows[owner, k] == block) & (k < counts[owner])
        slot = jnp.where(hit, k, slot)
        live = jnp.where(hit, 1, live)
    return slot, live


def half_of(value, upper):
    return jnp.where(upper > 0, value[PART:], value[:PART])


def prep_a_body(place, rows_a, counts_a, part_a, out_a):
    for block in range(NB):
        slot, live = find_slot(rows_a, counts_a, place[0], block)
        at = pl.ds(pl.multiple_of(slot * BS, BS), BS)
        piece = half_of(part_a[at, :].T, place[1] % 2)
        out_a[block] = jnp.where(live > 0, piece, jnp.zeros_like(piece))


def width_slice(rows):
    return pl.BlockSpec((rows, BS), lambda i, place, *_: (0, place[1] // 2))


def prep_a(place, lists, factor_a):
    return pl.pallas_call(
        prep_a_body,
        name="prep_a",
        grid_spec=pltpu.PrefetchScalarGridSpec(
            num_scalar_prefetch=3,
            grid=(1,),
            in_specs=[width_slice(ROWS)],
            out_specs=whole((NB, PART, BS)),
        ),
        out_shape=jax.ShapeDtypeStruct((NB, PART, BS), BF),
        compiler_params=params(56),
        cost_estimate=cost(0, 4 * ROWS * BS),
    )(place, *lists[:2], factor_a)


def prep_b_body(place, rows_a, counts_a, rows_b, counts_b, fa, part_b, top, out_b, fix):
    owner = place[0]
    upper = place[1] % 2
    fix[...] = lax.dot_general(
        top[...], fa[...], (((0,), (1,)), ((), ())), preferred_element_type=F32
    )
    for block in range(NB):
        slot_a, live_a = find_slot(rows_a, counts_a, owner, block)
        slot_b, live_b = find_slot(rows_b, counts_b, owner, block)
        at_a = pl.ds(pl.multiple_of(slot_a * BS, BS), BS)
        at_b = pl.ds(pl.multiple_of(slot_b * BS, BS), BS)
        moved = half_of(fix[:, at_a], upper)
        piece = half_of(part_b[at_b, :].T, upper).astype(F32)
        piece = jnp.where(live_b > 0, piece, jnp.zeros_like(piece))
        out_b[block] = (piece - jnp.where(live_a > 0, moved, jnp.zeros_like(moved))).astype(BF)


def prep_b(place, lists, factor_a, factor_b, factor_top):
    return pl.pallas_call(
        prep_b_body,
        name="prep_b",
        grid_spec=pltpu.PrefetchScalarGridSpec(
            num_scalar_prefetch=5,
            grid=(1,),
            in_specs=[whole((ROWS, W)), width_slice(ROWS), width_slice(W)],
            out_specs=whole((NB, PART, BS)),
            scratch_shapes=[pltpu.VMEM((BS, ROWS), F32)],
        ),
        out_shape=jax.ShapeDtypeStruct((NB, PART, BS), BF),
        compiler_params=params(56),
        cost_estimate=cost(2 * BS * ROWS * W, 2 * ROWS * (W + 4 * BS)),
    )(place, *lists, factor_a, factor_b, factor_top)


def where(place):
    z, y, plane = place[0] // SIDE, place[0] % SIDE, place[1]
    u = (z - plane // SIDE + SIDE) % SIDE
    v = (y - plane % SIDE + SIDE) % SIDE
    return u, v


def turn(value, by):
    return (value + by + SIDE) % SIDE


def load_a(copies, buf, u, spread, start=0, many=SIDE):
    for i in range(start, start + many):
        copies.append((buf.at[i - start], spread.at[:, u // 2, i * PART : (i + 1) * PART, :]))


def load_b(copies, buf, u, first, spread, start=0, many=SIDE):
    for i in range(start, start + many):
        ui = turn(u, -STEPS[i])
        at = pl.ds(pl.multiple_of(first + (ui % 2) * PART, PART), PART)
        copies.append((buf.at[i - start], spread.at[:, ui // 2, at, :]))


def run_copies(copies, sems):
    started = [pltpu.make_async_copy(a, b, sems.at[i]) for i, (a, b) in enumerate(copies)]
    for copy in started:
        copy.start()
    for copy in started:
        copy.wait()


def multiply(spread, tile):
    left = jnp.concatenate([spread[n, h] for n in range(NB) for h in range(2)], axis=1)
    return lax.dot_general(
        left, tile, (((1,), (1,)), ((), ())), preferred_element_type=F32
    ).astype(BF)


def hold_body(source, _, target, sem):
    copy = pltpu.make_async_copy(source, target, sem)
    copy.start()
    copy.wait()


def hold(trailing, after):
    return pl.pallas_call(
        hold_body,
        name="hold",
        in_specs=[pl.BlockSpec(memory_space=pltpu.HBM), pl.BlockSpec(memory_space=pl.ANY)],
        out_specs=pl.BlockSpec(memory_space=pltpu.VMEM),
        out_shape=pltpu.VMEM(trailing.shape, BF),
        scratch_shapes=[pltpu.SemaphoreType.DMA],
        compiler_params=params(8),
        cost_estimate=cost(0, 2 * trailing.size),
    )(trailing, after)


def rows_of(tile, step):
    return tile[pl.ds(pl.multiple_of(step * STRIP, STRIP), STRIP), :]


def half_multiply(spread, tile, step, h):
    rows = pl.ds(pl.multiple_of(step * STRIP, STRIP), STRIP)
    left = jnp.concatenate([spread[n] for n in range(NB)], axis=1)
    right = jnp.concatenate(
        [tile[rows, pl.ds(pl.multiple_of((2 * n + h) * BS, BS), BS)] for n in range(NB)], axis=1
    )
    return lax.dot_general(left, right, (((1,), (1,)), ((), ())), preferred_element_type=F32)


def load_half(copies, buf, spread, start=0, many=SIDE):
    for i in range(start, start + many):
        copies.append((buf.at[i - start], spread.at[:, i * PART : (i + 1) * PART, :]))


def own_body(place, a_own, b_own, tile, half_a, whole_b, spread_a, spread_b, sems):
    u, _ = where(place)

    @pl.when(pl.program_id(0) == 0)
    def _():
        copies = []
        load_half(copies, a_own, spread_a)
        load_b(copies, b_own, u, 0, spread_b)
        run_copies(copies, sems)

    half_a[...] = half_multiply(spread_a, tile, pl.program_id(0), u // 2)
    whole_b[...] = multiply(spread_b, rows_of(tile, pl.program_id(0)))


def own_product(place, a_own, b_own, trailing):
    deep = trailing.shape[1]
    return pl.pallas_call(
        own_body,
        name="own_product",
        grid_spec=pltpu.PrefetchScalarGridSpec(
            num_scalar_prefetch=1,
            grid=(ROWS // STRIP,),
            in_specs=[pl.BlockSpec(memory_space=pl.ANY)] * 2
            + [pl.BlockSpec(memory_space=pltpu.VMEM)],
            out_specs=[
                pl.BlockSpec((W // 2, STRIP), lambda i, *_: (0, i)),
                pl.BlockSpec((2 * PART, STRIP), lambda i, *_: (0, i)),
            ],
            scratch_shapes=[
                pltpu.VMEM((NB, W // 2, BS), BF),
                pltpu.VMEM((NB, 2, 2 * PART, BS), BF),
                pltpu.SemaphoreType.DMA((8,)),
            ],
        ),
        out_shape=[
            jax.ShapeDtypeStruct((W // 2, ROWS), F32),
            jax.ShapeDtypeStruct((2 * PART, ROWS), BF),
        ],
        compiler_params=params(20, dimension_semantics=("arbitrary",)),
        cost_estimate=cost(4 * PART * ROWS * deep + W // 2 * ROWS * deep, 8 * W * ROWS),
    )(place, a_own, b_own, trailing)


def early_body(place, a_down, a_up, b_down, b_up, tile, whole_b, out, spread, sems):
    u, v = where(place)

    @pl.when(pl.program_id(0) == 0)
    def _():
        copies = []
        load_a(copies, a_down, turn(u, -1), spread)
        load_a(copies, a_up, turn(u, 1), spread)
        for t, buf in enumerate((b_down, b_up)):
            load_b(copies, buf, u, W // 2 + 2 * t * PART, spread)
        run_copies(copies, sems)

    value = multiply(spread, rows_of(tile, pl.program_id(0)))
    for i, step in enumerate(STEPS):
        out[2 * turn(v, -step) + (u + 1) % 2, :PART, :] = value[i * PART : (i + 1) * PART]
    for j in range(4):
        to = 2 * turn(v, (-1, 1)[j // 2]) + j % 2
        out[to, PART:, :] = value[W // 2 + j * PART : W // 2 + (j + 1) * PART]
    for j in range(2):
        out[2 * v + j, PART:, :] = whole_b[j * PART : (j + 1) * PART, :]


def early_product(place, bufs, trailing, whole_b):
    deep = trailing.shape[1]
    rows = W // 2 + 4 * PART
    return pl.pallas_call(
        early_body,
        name="early_product",
        grid_spec=pltpu.PrefetchScalarGridSpec(
            num_scalar_prefetch=1,
            grid=(ROWS // STRIP,),
            in_specs=[pl.BlockSpec(memory_space=pl.ANY)] * 4
            + [
                pl.BlockSpec(memory_space=pltpu.VMEM),
                pl.BlockSpec((2 * PART, STRIP), lambda i, *_: (0, i)),
            ],
            out_specs=pl.BlockSpec((COLS, PAIR, STRIP), lambda i, *_: (0, 0, i)),
            scratch_shapes=[
                pltpu.VMEM((NB, 2, rows, BS), BF),
                pltpu.SemaphoreType.DMA((16,)),
            ],
        ),
        out_shape=jax.ShapeDtypeStruct((COLS, PAIR, ROWS), BF),
        compiler_params=params(20, dimension_semantics=("arbitrary",)),
        cost_estimate=cost(2 * rows * ROWS * deep, 2 * rows * deep + 4 * W * ROWS),
    )(place, *bufs, trailing, whole_b)


def late_body(
    half, place, a_far, a_far_more, b_far, b_far_more, tile, before, half_a, keep, give, spread_a, spread_b, ready, sems
):
    u, v = where(place)
    core = place[1] % 2

    @pl.when(pl.program_id(0) == 0)
    def _():
        copies = []
        load_half(copies, a_far, spread_a, 0, 2)
        load_half(copies, a_far_more, spread_a, 2, 2)
        load_b(copies, b_far, u, 0, spread_b, 0, 2)
        load_b(copies, b_far_more, u, 0, spread_b, 2, 2)
        run_copies(copies, sems)

    ready[...] = before[...]
    step = half * HALF_STEPS + pl.program_id(0)
    value = half_multiply(spread_a, tile, step, turn(u, 2) // 2)
    value = (value + half_a[...]).astype(BF)
    for i, far in enumerate(STEPS):
        ready[2 * turn(v, -far) + u % 2, :PART, :] = value[i * PART : (i + 1) * PART]
    value = multiply(spread_b, rows_of(tile, step))
    for j in range(2):
        ready[2 * turn(v, 2) + j, PART:, :] = value[j * PART : (j + 1) * PART]
    for x in range(SIDE):
        keep[x] = ready[2 * x + core]
        give[x] = ready[2 * x + 1 - core]


HALF_STEPS = ROWS // STRIP // 2


def late_product(half, place, bufs, trailing, before, half_a):
    deep = trailing.shape[1]
    rows = W // 4 + 2 * PART
    out = jax.ShapeDtypeStruct((SIDE, PAIR, ROWS // 2), BF)
    spec = pl.BlockSpec((SIDE, PAIR, STRIP), lambda i, *_: (0, 0, i))
    return pl.pallas_call(
        functools.partial(late_body, half),
        name="late_product",
        grid_spec=pltpu.PrefetchScalarGridSpec(
            num_scalar_prefetch=1,
            grid=(HALF_STEPS,),
            in_specs=[pl.BlockSpec(memory_space=pl.ANY)] * 4
            + [
                pl.BlockSpec(memory_space=pltpu.VMEM),
                pl.BlockSpec((COLS, PAIR, STRIP), lambda i, *_: (0, 0, half * HALF_STEPS + i)),
                pl.BlockSpec((W // 2, STRIP), lambda i, *_: (0, half * HALF_STEPS + i)),
            ],
            out_specs=[spec, spec],
            scratch_shapes=[
                pltpu.VMEM((NB, W // 2, BS), BF),
                pltpu.VMEM((NB, 2, 2 * PART, BS), BF),
                pltpu.VMEM((COLS, PAIR, STRIP), BF),
                pltpu.SemaphoreType.DMA((8,)),
            ],
        ),
        out_shape=[out, out],
        compiler_params=params(20, dimension_semantics=("arbitrary",)),
        cost_estimate=cost(rows * ROWS * deep, 2 * rows * deep + 4 * W * ROWS),
    )(place, *bufs, trailing, before, half_a)


def pair_body(place, mine, taken, *outs):
    x = place[1] // 2
    for i in range(SIDE):
        at = (x + i) % SIDE
        outs[i][...] = (mine[at].astype(F32) + taken[at].astype(F32)).astype(BF)


def pair_sum(place, mine, taken):
    lanes = 3 * BS
    width = mine.shape[2]
    spec = pl.BlockSpec((SIDE, PAIR, lanes), lambda i, *_: (0, 0, i))
    return pl.pallas_call(
        pair_body,
        name="pair_sum",
        grid_spec=pltpu.PrefetchScalarGridSpec(
            num_scalar_prefetch=1,
            grid=(width // lanes,),
            in_specs=[spec, spec],
            out_specs=[pl.BlockSpec((PAIR, lanes), lambda i, *_: (0, i))] * SIDE,
        ),
        out_shape=[jax.ShapeDtypeStruct((PAIR, width), BF)] * SIDE,
        compiler_params=params(dimension_semantics=("arbitrary",)),
        cost_estimate=cost(W * width, 6 * W * width),
    )(place, mine, taken)


def slots_body(
    place, rows_a, counts_a, rows_b, counts_b, *refs
):
    slabs, (fa, fb, columns, pieces, natural, left) = refs[:8], refs[8:]
    owner = place[0]
    width = ROWS // 2
    for half in range(2):
        total = total_of(slabs[half * SIDE : (half + 1) * SIDE], slice(None))
        natural[:, half * width : (half + 1) * width] = (-total).astype(BF)
    for k in range(NB):
        at = slice(k * BS, (k + 1) * BS)
        block = natural[:PART, pl.ds(pl.multiple_of(rows_a[owner, k] * BS, BS), BS)]
        columns[:PART, at] = jnp.where(k < counts_a[owner], block, jnp.zeros_like(block))
        block = natural[:, pl.ds(pl.multiple_of(rows_b[owner, k] * BS, BS), BS)]
        block = jnp.where(k < counts_b[owner], block, jnp.zeros_like(block))
        left[:, at] = block
        columns[PART:, at] = block[PART:]
    one = jnp.dot(columns[:PART, :], fa[...], preferred_element_type=F32)
    two = jnp.dot(left[...], fb[...], preferred_element_type=F32)
    pieces[:PART, :] = one.astype(BF)
    pieces[PART:, :] = two.astype(BF)


def slots(place, lists, slabs, factors):
    return pl.pallas_call(
        slots_body,
        name="slots",
        grid_spec=pltpu.PrefetchScalarGridSpec(
            num_scalar_prefetch=5,
            grid=(1,),
            in_specs=[whole((PAIR, ROWS // 2))] * 8 + [whole((ROWS, W))] * 2,
            out_specs=[whole((PAIR, ROWS)), whole((3 * PART, W))],
            scratch_shapes=[pltpu.VMEM((PAIR, ROWS), BF)] * 2,
        ),
        out_shape=[
            jax.ShapeDtypeStruct((PAIR, ROWS), BF),
            jax.ShapeDtypeStruct((3 * PART, W), BF),
        ],
        compiler_params=params(),
        cost_estimate=cost(6 * PART * ROWS * W, 4 * ROWS * W + 10 * PAIR * ROWS),
    )(place, *lists, *slabs, *factors)


def column_body(place, *refs):
    slabs, column_a, column_b, wide = refs[:8], refs[8], refs[9], refs[10]
    core, x = place[1] % 2, place[1] // 2
    for i in range(8):
        at = 2 * turn(x, -STEPS[i % SIDE]) + (core if i < SIDE else 1 - core)
        wide[at] = slabs[i][...]
    for first, out in ((0, column_a), (PART, column_b)):
        out[...] = wide[:, first : first + PART, :].reshape(W, wide.shape[2]).T


def whole_columns(place, slabs):
    lanes = 4 * BS
    out = jax.ShapeDtypeStruct((ROWS, W), BF)
    return pl.pallas_call(
        column_body,
        name="whole_columns",
        grid_spec=pltpu.PrefetchScalarGridSpec(
            num_scalar_prefetch=1,
            grid=(ROWS // lanes,),
            in_specs=[pl.BlockSpec((PAIR, lanes), lambda i, *_: (0, i))] * 8,
            out_specs=[pl.BlockSpec((lanes, W), lambda i, *_: (i, 0))] * 2,
            scratch_shapes=[pltpu.VMEM((COLS, PAIR, lanes), BF)],
        ),
        out_shape=[out, out],
        compiler_params=params(dimension_semantics=("arbitrary",)),
        cost_estimate=cost(0, 8 * ROWS * W),
    )(place, *slabs)


def total_of(refs, rows):
    parts = [ref[rows, :].astype(F32) for ref in refs]
    return (parts[0] + parts[1]) + (parts[2] + parts[3])


def fold_body(one, two, three, four, out):
    out[...] = total_of((one, two, three, four), slice(None)).astype(BF)


def fold(parts):
    return pl.pallas_call(
        fold_body,
        name="fold",
        out_shape=jax.ShapeDtypeStruct(parts[0].shape, BF),
        compiler_params=params(8),
        cost_estimate=cost(4 * parts[0].size, 10 * parts[0].size),
    )(*parts)


def top_body(one, two, three, four, base, top, diag_a, top_b, sent):
    got = (one, two, three, four)
    value = base[...] - total_of(got, slice(0, PART))
    diag_a[...] = value
    total = total_of(got, slice(PART, 2 * PART))
    for _ in range(3):
        part = value.astype(BF)
        value = value - part.astype(F32)
        total = total + jnp.dot(part, top[...], preferred_element_type=F32)
    total = (-total).astype(BF)
    top_b[...] = total
    for c in range(COLS):
        sent[c] = jnp.concatenate([total[:, c * PART : (c + 1) * PART]] * 2, axis=1)


def top_part(got, base_a, factor_top):
    return pl.pallas_call(
        top_body,
        name="top_part",
        out_shape=[
            jax.ShapeDtypeStruct((PART, W), F32),
            jax.ShapeDtypeStruct((PART, W), BF),
            jax.ShapeDtypeStruct((COLS, PART, 2 * PART), BF),
        ],
        compiler_params=params(8),
        cost_estimate=cost(6 * PART * W * W, 2 * W * W),
    )(*got, base_a, factor_top)


def last_body(one, two, three, four, base, taken, top, diag_b):
    across = taken[...].reshape(W, 2 * PART)
    cross = lax.dot_general(
        across, top[...], (((0,), (0,)), ((), ())), preferred_element_type=F32
    )
    total = total_of((one, two, three, four), slice(2 * PART, 3 * PART))
    diag_b[...] = base[...] - total - cross[:PART]


def last_part(got, base_b, taken, factor_top):
    return pl.pallas_call(
        last_body,
        name="last_part",
        out_shape=jax.ShapeDtypeStruct((PART, W), F32),
        compiler_params=params(8),
        cost_estimate=cost(4 * PART * W * W, 2 * W * W),
    )(*got, base_b, taken, factor_top)


def send(value, **by):
    return lax.ppermute(value, BOTH, shifted(**by))


def around(value, axis):
    return [value] + [send(value, **{axis: step}) for step in STEPS[1:]]


def on_device(
    trailing, rows_a, counts_a, factor_a, rows_b, counts_b, factor_b, factor_top, base_a, base_b
):
    place = jnp.stack([lax.axis_index("row"), lax.axis_index("col")]).astype(jnp.int32)
    lists = (rows_a, counts_a, rows_b, counts_b)
    part_a = lax.ppermute(prep_a(place, lists, factor_a), BOTH, spread_pairs())
    part_b = prep_b(place, lists, factor_a, factor_b, factor_top)
    part_b = lax.ppermute(part_b, BOTH, spread_pairs())
    a_own = jnp.stack(around(part_a, "dy"))
    b_own = jnp.stack(around(part_b, "dz"))
    a_down, a_up = send(a_own, dz=1), send(a_own, dz=-1)
    b_down, b_up = send(b_own, dy=1), send(b_own, dy=-1)
    trailing = hold(trailing, a_own)
    half_a, whole_b = own_product(place, a_own, b_own, trailing)
    a_next, b_next, _ = lax.optimization_barrier((a_down, b_down, half_a))
    a_far, b_far = send(a_next[:2], dz=1), send(b_next[:2], dy=1)
    a_far_more, b_far_more = send(a_up[2:], dz=-1), send(b_up[2:], dy=-1)
    before = early_product(place, (a_down, a_up, b_down, b_up), trailing, whole_b)
    slabs = []
    for half in range(2):
        keep, give = late_product(
            half, place, (a_far, a_far_more, b_far, b_far_more), trailing, before, half_a
        )
        own, one, two, three = pair_sum(place, keep, send(give, dc=1))
        slabs += [own, send(two, dx=2), send(one, dx=1), send(three, dx=-1)]
    columns, pieces = slots(place, lists, slabs, (factor_a, factor_b))
    near, other = send(columns, dx=1), send(columns, dx=-1)
    first, near, other = lax.optimization_barrier((around(pieces, "dy"), near, other))
    folded = fold(first)
    got = around(folded, "dz")
    far = send(lax.optimization_barrier((columns, folded))[0], dx=2)
    _, (own, near, other) = lax.optimization_barrier((got, (columns, near, other)))
    mates = [send(slab, dc=1) for slab in (near, other)]
    mate = send(own, dc=1)
    diag_a, top_b, sent = top_part(got, base_a, factor_top)
    far, _ = lax.optimization_barrier((far, sent))
    taken = lax.all_to_all(sent, "col", 0, 0)
    column_a, column_b = whole_columns(
        place, [own, far, near, other, mate, send(far, dc=1), *mates]
    )
    base_b, _ = lax.optimization_barrier((base_b, column_a))
    diag_b = last_part(got, base_b, taken, factor_top)
    return (column_a, diag_a, column_b, top_b, diag_b)


def solution(mesh):
    in_specs = (
        P("row", "col"),
        P(),
        P(),
        P("row", None),
        P(),
        P(),
        P("row", None),
        P(),
        P("col", None),
        P("col", None),
    )
    out_specs = (P("row", None), P("col", None), P("row", None), P("col", None), P("col", None))
    return jax.shard_map(
        on_device, mesh=mesh, in_specs=in_specs, out_specs=out_specs, check_vma=False
    )
```

```python
import functools

import jax
import jax.numpy as jnp
from jax import lax
from jax.experimental import pallas as pl
from jax.experimental.pallas import tpu as pltpu
from jax.sharding import PartitionSpec as P

BS = 128
W = 512
NB = 12
ROWS = NB * BS
SIDE = 4
PART = 64
COLS = 8
STEPS = (0, 2, 1, -1)
STRIP = 2 * BS
PAIR = 2 * PART
BOTH = ("row", "col")
MIB = 1024 * 1024
BF = jnp.bfloat16
F32 = jnp.float32


def device(z, y, x, core):
    return ((z % SIDE) * SIDE + y % SIDE) * 8 + (x % SIDE) * 2 + core % 2


def all_places():
    return [
        (z, y, x, core)
        for z in range(SIDE)
        for y in range(SIDE)
        for x in range(SIDE)
        for core in range(2)
    ]


def shifted(dz=0, dy=0, dx=0, dc=0):
    return [
        (device(z, y, x, c), device(z + dz, y + dy, x + dx, c + dc))
        for z, y, x, c in all_places()
    ]


def spread_pairs():
    pairs = []
    for z, y, x, core in all_places():
        plane = (z * SIDE + y) % 8
        far = 2 - (x - plane // 2)
        to = device(z + core, y + far, plane // 2, plane % 2)
        pairs.append((device(z, y, x, core), to))
    return pairs


def params(mib=24, **more):
    return pltpu.CompilerParams(vmem_limit_bytes=mib * MIB, **more)


def cost(flops, moved):
    return pl.CostEstimate(flops=flops, bytes_accessed=moved, transcendentals=0)


def whole(shape):
    return pl.BlockSpec(shape, lambda *_: (0,) * len(shape))


def find_slot(rows, counts, owner, block):
    slot = jnp.int32(0)
    live = jnp.int32(0)
    for k in range(NB):
        hit = (rows[owner, k] == block) & (k < counts[owner])
        slot = jnp.where(hit, k, slot)
        live = jnp.where(hit, 1, live)
    return slot, live


def half_of(value, upper):
    return jnp.where(upper > 0, value[PART:], value[:PART])


def prep_a_body(place, rows_a, counts_a, part_a, out_a):
    for block in range(NB):
        slot, live = find_slot(rows_a, counts_a, place[0], block)
        at = pl.ds(pl.multiple_of(slot * BS, BS), BS)
        piece = half_of(part_a[at, :].T, place[1] % 2)
        out_a[block] = jnp.where(live > 0, piece, jnp.zeros_like(piece))


def width_slice(rows):
    return pl.BlockSpec((rows, BS), lambda i, place, *_: (0, place[1] // 2))


def prep_a(place, lists, factor_a):
    return pl.pallas_call(
        prep_a_body,
        name="prep_a",
        grid_spec=pltpu.PrefetchScalarGridSpec(
            num_scalar_prefetch=3,
            grid=(1,),
            in_specs=[width_slice(ROWS)],
            out_specs=whole((NB, PART, BS)),
        ),
        out_shape=jax.ShapeDtypeStruct((NB, PART, BS), BF),
        compiler_params=params(56),
        cost_estimate=cost(0, 4 * ROWS * BS),
    )(place, *lists[:2], factor_a)


def prep_b_body(place, rows_a, counts_a, rows_b, counts_b, fa, part_b, top, out_b, fix):
    owner = place[0]
    upper = place[1] % 2
    fix[...] = lax.dot_general(
        top[...], fa[...], (((0,), (1,)), ((), ())), preferred_element_type=F32
    )
    for block in range(NB):
        slot_a, live_a = find_slot(rows_a, counts_a, owner, block)
        slot_b, live_b = find_slot(rows_b, counts_b, owner, block)
        at_a = pl.ds(pl.multiple_of(slot_a * BS, BS), BS)
        at_b = pl.ds(pl.multiple_of(slot_b * BS, BS), BS)
        moved = half_of(fix[:, at_a], upper)
        piece = half_of(part_b[at_b, :].T, upper).astype(F32)
        piece = jnp.where(live_b > 0, piece, jnp.zeros_like(piece))
        out_b[block] = (piece - jnp.where(live_a > 0, moved, jnp.zeros_like(moved))).astype(BF)


def prep_b(place, lists, factor_a, factor_b, factor_top):
    return pl.pallas_call(
        prep_b_body,
        name="prep_b",
        grid_spec=pltpu.PrefetchScalarGridSpec(
            num_scalar_prefetch=5,
            grid=(1,),
            in_specs=[whole((ROWS, W)), width_slice(ROWS), width_slice(W)],
            out_specs=whole((NB, PART, BS)),
            scratch_shapes=[pltpu.VMEM((BS, ROWS), F32)],
        ),
        out_shape=jax.ShapeDtypeStruct((NB, PART, BS), BF),
        compiler_params=params(56),
        cost_estimate=cost(2 * BS * ROWS * W, 2 * ROWS * (W + 4 * BS)),
    )(place, *lists, factor_a, factor_b, factor_top)


def where(place):
    z, y, plane = place[0] // SIDE, place[0] % SIDE, place[1]
    u = (z - plane // SIDE + SIDE) % SIDE
    v = (y - plane % SIDE + SIDE) % SIDE
    return u, v


def slice_of(place, v):
    return (place[1] // 2 + 2 - v + SIDE) % SIDE


def turn(value, by):
    return (value + by + SIDE) % SIDE


def load_a(copies, buf, u, spread, start=0, many=SIDE):
    for i in range(start, start + many):
        copies.append((buf.at[i - start], spread.at[:, u // 2, i * PART : (i + 1) * PART, :]))


def load_b(copies, buf, u, first, spread, start=0, many=SIDE):
    for i in range(start, start + many):
        ui = turn(u, -STEPS[i])
        at = pl.ds(pl.multiple_of(first + (ui % 2) * PART, PART), PART)
        copies.append((buf.at[i - start], spread.at[:, ui // 2, at, :]))


def run_copies(copies, sems):
    started = [pltpu.make_async_copy(a, b, sems.at[i]) for i, (a, b) in enumerate(copies)]
    for copy in started:
        copy.start()
    for copy in started:
        copy.wait()


def multiply(spread, tile):
    left = jnp.concatenate([spread[n, h] for n in range(NB) for h in range(2)], axis=1)
    return lax.dot_general(
        left, tile, (((1,), (1,)), ((), ())), preferred_element_type=F32
    ).astype(BF)


def hold_body(source, _, target, sem):
    copy = pltpu.make_async_copy(source, target, sem)
    copy.start()
    copy.wait()


def hold(trailing, after):
    return pl.pallas_call(
        hold_body,
        name="hold",
        in_specs=[pl.BlockSpec(memory_space=pltpu.HBM), pl.BlockSpec(memory_space=pl.ANY)],
        out_specs=pl.BlockSpec(memory_space=pltpu.VMEM),
        out_shape=pltpu.VMEM(trailing.shape, BF),
        scratch_shapes=[pltpu.SemaphoreType.DMA],
        compiler_params=params(8),
        cost_estimate=cost(0, 2 * trailing.size),
    )(trailing, after)


def rows_of(tile, step):
    return tile[pl.ds(pl.multiple_of(step * STRIP, STRIP), STRIP), :]


def half_multiply(spread, tile, step, h):
    rows = pl.ds(pl.multiple_of(step * STRIP, STRIP), STRIP)
    left = jnp.concatenate([spread[n] for n in range(NB)], axis=1)
    right = jnp.concatenate(
        [tile[rows, pl.ds(pl.multiple_of((2 * n + h) * BS, BS), BS)] for n in range(NB)], axis=1
    )
    return lax.dot_general(left, right, (((1,), (1,)), ((), ())), preferred_element_type=F32)


def load_half(copies, buf, spread, start=0, many=SIDE):
    for i in range(start, start + many):
        copies.append((buf.at[i - start], spread.at[:, i * PART : (i + 1) * PART, :]))


def own_body(place, a_own, b_own, tile, half_a, whole_b, spread_a, spread_b, sems):
    u, _ = where(place)

    @pl.when(pl.program_id(0) == 0)
    def _():
        copies = []
        load_half(copies, a_own, spread_a)
        load_b(copies, b_own, u, 0, spread_b)
        run_copies(copies, sems)

    half_a[...] = half_multiply(spread_a, tile, pl.program_id(0), u // 2)
    whole_b[...] = multiply(spread_b, rows_of(tile, pl.program_id(0)))


def own_product(place, a_own, b_own, trailing):
    deep = trailing.shape[1]
    return pl.pallas_call(
        own_body,
        name="own_product",
        grid_spec=pltpu.PrefetchScalarGridSpec(
            num_scalar_prefetch=1,
            grid=(ROWS // STRIP,),
            in_specs=[pl.BlockSpec(memory_space=pl.ANY)] * 2
            + [pl.BlockSpec(memory_space=pltpu.VMEM)],
            out_specs=[
                pl.BlockSpec((W // 2, STRIP), lambda i, *_: (0, i)),
                pl.BlockSpec((2 * PART, STRIP), lambda i, *_: (0, i)),
            ],
            scratch_shapes=[
                pltpu.VMEM((NB, W // 2, BS), BF),
                pltpu.VMEM((NB, 2, 2 * PART, BS), BF),
                pltpu.SemaphoreType.DMA((8,)),
            ],
        ),
        out_shape=[
            jax.ShapeDtypeStruct((W // 2, ROWS), F32),
            jax.ShapeDtypeStruct((2 * PART, ROWS), BF),
        ],
        compiler_params=params(20, dimension_semantics=("arbitrary",)),
        cost_estimate=cost(4 * PART * ROWS * deep + W // 2 * ROWS * deep, 8 * W * ROWS),
    )(place, a_own, b_own, trailing)


def early_body(place, a_down, a_up, b_down, b_up, tile, whole_b, out, spread, sems):
    u, v = where(place)

    @pl.when(pl.program_id(0) == 0)
    def _():
        copies = []
        load_a(copies, a_down, turn(u, -1), spread)
        load_a(copies, a_up, turn(u, 1), spread)
        for t, buf in enumerate((b_down, b_up)):
            load_b(copies, buf, u, W // 2 + 2 * t * PART, spread)
        run_copies(copies, sems)

    value = multiply(spread, rows_of(tile, pl.program_id(0)))
    for i, step in enumerate(STEPS):
        out[2 * slice_of(place, turn(v, -step)) + (u + 1) % 2, :PART, :] = value[i * PART : (i + 1) * PART]
    for j in range(4):
        to = 2 * slice_of(place, turn(v, (-1, 1)[j // 2])) + j % 2
        out[to, PART:, :] = value[W // 2 + j * PART : W // 2 + (j + 1) * PART]
    for j in range(2):
        out[2 * slice_of(place, v) + j, PART:, :] = whole_b[j * PART : (j + 1) * PART, :]


def early_product(place, bufs, trailing, whole_b):
    deep = trailing.shape[1]
    rows = W // 2 + 4 * PART
    return pl.pallas_call(
        early_body,
        name="early_product",
        grid_spec=pltpu.PrefetchScalarGridSpec(
            num_scalar_prefetch=1,
            grid=(ROWS // STRIP,),
            in_specs=[pl.BlockSpec(memory_space=pl.ANY)] * 4
            + [
                pl.BlockSpec(memory_space=pltpu.VMEM),
                pl.BlockSpec((2 * PART, STRIP), lambda i, *_: (0, i)),
            ],
            out_specs=pl.BlockSpec((COLS, PAIR, STRIP), lambda i, *_: (0, 0, i)),
            scratch_shapes=[
                pltpu.VMEM((NB, 2, rows, BS), BF),
                pltpu.SemaphoreType.DMA((16,)),
            ],
        ),
        out_shape=jax.ShapeDtypeStruct((COLS, PAIR, ROWS), BF),
        compiler_params=params(20, dimension_semantics=("arbitrary",)),
        cost_estimate=cost(2 * rows * ROWS * deep, 2 * rows * deep + 4 * W * ROWS),
    )(place, *bufs, trailing, whole_b)


def late_body(
    half, place, a_far, a_far_more, b_far, b_far_more, tile, before, half_a, keep, give, spread_a, spread_b, ready, sems
):
    u, v = where(place)
    core = place[1] % 2

    @pl.when(pl.program_id(0) == 0)
    def _():
        copies = []
        load_half(copies, a_far, spread_a, 0, 2)
        load_half(copies, a_far_more, spread_a, 2, 2)
        load_b(copies, b_far, u, 0, spread_b, 0, 2)
        load_b(copies, b_far_more, u, 0, spread_b, 2, 2)
        run_copies(copies, sems)

    ready[...] = before[...]
    step = half * HALF_STEPS + pl.program_id(0)
    value = half_multiply(spread_a, tile, step, turn(u, 2) // 2)
    value = (value + half_a[...]).astype(BF)
    for i, far in enumerate(STEPS):
        ready[2 * slice_of(place, turn(v, -far)) + u % 2, :PART, :] = value[i * PART : (i + 1) * PART]
    value = multiply(spread_b, rows_of(tile, step))
    for j in range(2):
        ready[2 * slice_of(place, turn(v, 2)) + j, PART:, :] = value[j * PART : (j + 1) * PART]
    for x in range(SIDE):
        keep[x] = ready[2 * x + core]
        give[x] = ready[2 * x + 1 - core]


HALF_STEPS = ROWS // STRIP // 2


def late_product(half, place, bufs, trailing, before, half_a):
    deep = trailing.shape[1]
    rows = W // 4 + 2 * PART
    out = jax.ShapeDtypeStruct((SIDE, PAIR, ROWS // 2), BF)
    spec = pl.BlockSpec((SIDE, PAIR, STRIP), lambda i, *_: (0, 0, i))
    return pl.pallas_call(
        functools.partial(late_body, half),
        name="late_product",
        grid_spec=pltpu.PrefetchScalarGridSpec(
            num_scalar_prefetch=1,
            grid=(HALF_STEPS,),
            in_specs=[pl.BlockSpec(memory_space=pl.ANY)] * 4
            + [
                pl.BlockSpec(memory_space=pltpu.VMEM),
                pl.BlockSpec((COLS, PAIR, STRIP), lambda i, *_: (0, 0, half * HALF_STEPS + i)),
                pl.BlockSpec((W // 2, STRIP), lambda i, *_: (0, half * HALF_STEPS + i)),
            ],
            out_specs=[spec, spec],
            scratch_shapes=[
                pltpu.VMEM((NB, W // 2, BS), BF),
                pltpu.VMEM((NB, 2, 2 * PART, BS), BF),
                pltpu.VMEM((COLS, PAIR, STRIP), BF),
                pltpu.SemaphoreType.DMA((8,)),
            ],
        ),
        out_shape=[out, out],
        compiler_params=params(20, dimension_semantics=("arbitrary",)),
        cost_estimate=cost(rows * ROWS * deep, 2 * rows * deep + 4 * W * ROWS),
    )(place, *bufs, trailing, before, half_a)


def pair_body(place, mine, taken, *outs):
    x = place[1] // 2
    for i in range(SIDE):
        at = (x + i) % SIDE
        outs[i][...] = (mine[at].astype(F32) + taken[at].astype(F32)).astype(BF)


def pair_sum(place, mine, taken):
    lanes = 3 * BS
    width = mine.shape[2]
    spec = pl.BlockSpec((SIDE, PAIR, lanes), lambda i, *_: (0, 0, i))
    return pl.pallas_call(
        pair_body,
        name="pair_sum",
        grid_spec=pltpu.PrefetchScalarGridSpec(
            num_scalar_prefetch=1,
            grid=(width // lanes,),
            in_specs=[spec, spec],
            out_specs=[pl.BlockSpec((PAIR, lanes), lambda i, *_: (0, i))] * SIDE,
        ),
        out_shape=[jax.ShapeDtypeStruct((PAIR, width), BF)] * SIDE,
        compiler_params=params(dimension_semantics=("arbitrary",)),
        cost_estimate=cost(W * width, 6 * W * width),
    )(place, mine, taken)


def slots_body(
    place, rows_a, counts_a, rows_b, counts_b, *refs
):
    slabs, (fa, fb, columns, pieces, natural, left) = refs[:8], refs[8:]
    owner = place[0]
    width = ROWS // 2
    for half in range(2):
        total = total_of(slabs[half * SIDE : (half + 1) * SIDE], slice(None))
        natural[:, half * width : (half + 1) * width] = (-total).astype(BF)
    for k in range(NB):
        at = slice(k * BS, (k + 1) * BS)
        block = natural[:PART, pl.ds(pl.multiple_of(rows_a[owner, k] * BS, BS), BS)]
        columns[:PART, at] = jnp.where(k < counts_a[owner], block, jnp.zeros_like(block))
        block = natural[:, pl.ds(pl.multiple_of(rows_b[owner, k] * BS, BS), BS)]
        block = jnp.where(k < counts_b[owner], block, jnp.zeros_like(block))
        left[:, at] = block
        columns[PART:, at] = block[PART:]
    one = jnp.dot(columns[:PART, :], fa[...], preferred_element_type=F32)
    two = jnp.dot(left[...], fb[...], preferred_element_type=F32)
    pieces[:PART, :] = one.astype(BF)
    pieces[PART:, :] = two.astype(BF)


def slots(place, lists, slabs, factors):
    return pl.pallas_call(
        slots_body,
        name="slots",
        grid_spec=pltpu.PrefetchScalarGridSpec(
            num_scalar_prefetch=5,
            grid=(1,),
            in_specs=[whole((PAIR, ROWS // 2))] * 8 + [whole((ROWS, W))] * 2,
            out_specs=[whole((PAIR, ROWS)), whole((3 * PART, W))],
            scratch_shapes=[pltpu.VMEM((PAIR, ROWS), BF)] * 2,
        ),
        out_shape=[
            jax.ShapeDtypeStruct((PAIR, ROWS), BF),
            jax.ShapeDtypeStruct((3 * PART, W), BF),
        ],
        compiler_params=params(),
        cost_estimate=cost(6 * PART * ROWS * W, 4 * ROWS * W + 10 * PAIR * ROWS),
    )(place, *lists, *slabs, *factors)


def column_body(place, *refs):
    slabs, column_a, column_b, wide = refs[:8], refs[8], refs[9], refs[10]
    core, x = place[1] % 2, place[1] // 2
    for i in range(8):
        at = 2 * turn(x, -STEPS[i % SIDE]) + (core if i < SIDE else 1 - core)
        wide[at] = slabs[i][...]
    for first, out in ((0, column_a), (PART, column_b)):
        out[...] = wide[:, first : first + PART, :].reshape(W, wide.shape[2]).T


def whole_columns(place, slabs):
    lanes = 4 * BS
    out = jax.ShapeDtypeStruct((ROWS, W), BF)
    return pl.pallas_call(
        column_body,
        name="whole_columns",
        grid_spec=pltpu.PrefetchScalarGridSpec(
            num_scalar_prefetch=1,
            grid=(ROWS // lanes,),
            in_specs=[pl.BlockSpec((PAIR, lanes), lambda i, *_: (0, i))] * 8,
            out_specs=[pl.BlockSpec((lanes, W), lambda i, *_: (i, 0))] * 2,
            scratch_shapes=[pltpu.VMEM((COLS, PAIR, lanes), BF)],
        ),
        out_shape=[out, out],
        compiler_params=params(dimension_semantics=("arbitrary",)),
        cost_estimate=cost(0, 8 * ROWS * W),
    )(place, *slabs)


def total_of(refs, rows):
    parts = [ref[rows, :].astype(F32) for ref in refs]
    return (parts[0] + parts[1]) + (parts[2] + parts[3])


def fold_body(one, two, three, four, out):
    out[...] = total_of((one, two, three, four), slice(None)).astype(BF)


def fold(parts):
    return pl.pallas_call(
        fold_body,
        name="fold",
        out_shape=jax.ShapeDtypeStruct(parts[0].shape, BF),
        compiler_params=params(8),
        cost_estimate=cost(4 * parts[0].size, 10 * parts[0].size),
    )(*parts)


def top_body(one, two, three, four, base, top, diag_a, top_b, sent):
    got = (one, two, three, four)
    value = base[...] - total_of(got, slice(0, PART))
    diag_a[...] = value
    total = total_of(got, slice(PART, 2 * PART))
    for _ in range(3):
        part = value.astype(BF)
        value = value - part.astype(F32)
        total = total + jnp.dot(part, top[...], preferred_element_type=F32)
    total = (-total).astype(BF)
    top_b[...] = total
    for c in range(COLS):
        sent[c] = jnp.concatenate([total[:, c * PART : (c + 1) * PART]] * 2, axis=1)


def top_part(got, base_a, factor_top):
    return pl.pallas_call(
        top_body,
        name="top_part",
        out_shape=[
            jax.ShapeDtypeStruct((PART, W), F32),
            jax.ShapeDtypeStruct((PART, W), BF),
            jax.ShapeDtypeStruct((COLS, PART, 2 * PART), BF),
        ],
        compiler_params=params(8),
        cost_estimate=cost(6 * PART * W * W, 2 * W * W),
    )(*got, base_a, factor_top)


def last_body(one, two, three, four, base, taken, top, diag_b):
    across = taken[...].reshape(W, 2 * PART)
    cross = lax.dot_general(
        across, top[...], (((0,), (0,)), ((), ())), preferred_element_type=F32
    )
    total = total_of((one, two, three, four), slice(2 * PART, 3 * PART))
    diag_b[...] = base[...] - total - cross[:PART]


def last_part(got, base_b, taken, factor_top):
    return pl.pallas_call(
        last_body,
        name="last_part",
        out_shape=jax.ShapeDtypeStruct((PART, W), F32),
        compiler_params=params(8),
        cost_estimate=cost(4 * PART * W * W, 2 * W * W),
    )(*got, base_b, taken, factor_top)


def send(value, **by):
    return lax.ppermute(value, BOTH, shifted(**by))


def around(value, axis):
    return [value] + [send(value, **{axis: step}) for step in STEPS[1:]]


def on_device(
    trailing, rows_a, counts_a, factor_a, rows_b, counts_b, factor_b, factor_top, base_a, base_b
):
    place = jnp.stack([lax.axis_index("row"), lax.axis_index("col")]).astype(jnp.int32)
    lists = (rows_a, counts_a, rows_b, counts_b)
    part_a = lax.ppermute(prep_a(place, lists, factor_a), BOTH, spread_pairs())
    part_b = prep_b(place, lists, factor_a, factor_b, factor_top)
    part_b = lax.ppermute(part_b, BOTH, spread_pairs())
    a_own = jnp.stack(around(part_a, "dy"))
    b_own = jnp.stack(around(part_b, "dz"))
    a_down, a_up = send(a_own, dz=1), send(a_own, dz=-1)
    b_down, b_up = send(b_own, dy=1), send(b_own, dy=-1)
    trailing = hold(trailing, a_own)
    half_a, whole_b = own_product(place, a_own, b_own, trailing)
    a_next, b_next, _ = lax.optimization_barrier((a_down, b_down, half_a))
    a_far, b_far = send(a_next[:2], dz=1), send(b_next[:2], dy=1)
    a_far_more, b_far_more = send(a_up[2:], dz=-1), send(b_up[2:], dy=-1)
    before = early_product(place, (a_down, a_up, b_down, b_up), trailing, whole_b)
    slabs = []
    for half in range(2):
        keep, give = late_product(
            half, place, (a_far, a_far_more, b_far, b_far_more), trailing, before, half_a
        )
        own, one, two, three = pair_sum(place, keep, send(give, dc=1))
        slabs += [own, send(two, dx=2), send(one, dx=1), send(three, dx=-1)]
    columns, pieces = slots(place, lists, slabs, (factor_a, factor_b))
    near, other = send(columns, dx=1), send(columns, dx=-1)
    first, near, other = lax.optimization_barrier((around(pieces, "dy"), near, other))
    folded = fold(first)
    got = around(folded, "dz")
    far = send(lax.optimization_barrier((columns, folded))[0], dx=2)
    _, (own, near, other) = lax.optimization_barrier((got, (columns, near, other)))
    mates = [send(slab, dc=1) for slab in (near, other)]
    mate = send(own, dc=1)
    diag_a, top_b, sent = top_part(got, base_a, factor_top)
    far, _ = lax.optimization_barrier((far, sent))
    taken = lax.all_to_all(sent, "col", 0, 0)
    column_a, column_b = whole_columns(
        place, [own, far, near, other, mate, send(far, dc=1), *mates]
    )
    base_b, _ = lax.optimization_barrier((base_b, column_a))
    diag_b = last_part(got, base_b, taken, factor_top)
    return (column_a, diag_a, column_b, top_b, diag_b)


def solution(mesh):
    in_specs = (
        P("row", "col"),
        P(),
        P(),
        P("row", None),
        P(),
        P(),
        P("row", None),
        P(),
        P("col", None),
        P("col", None),
    )
    out_specs = (P("row", None), P("col", None), P("row", None), P("col", None), P("col", None))
    return jax.shard_map(
        on_device, mesh=mesh, in_specs=in_specs, out_specs=out_specs, check_vma=False
    )
```
